32 devices in a mesh: dp: 4 (over z), fsdp: 8 (over y, x, core).
Axes of the slice: x: 2, y: 2, z: 4, core: 2. Of those that a mesh axis runs over, the one named last changes fastest.
Arguments:
- x_in: bfloat16 [49152, 512], P(('dp', 'fsdp')), may hold values from -6 to 6
- cotangent: bfloat16 [49152, 512], P(('dp', 'fsdp')), may hold values from -6 to 6
- table_lengths: int32 [32, 4], P(('dp', 'fsdp')), may hold values from 64 to 1024, as said below
- support_counts: int32 [32, 4], P(('dp', 'fsdp')), may hold values from 16 to 768, as said below
- master: float32 [3147776], P(('dp', 'fsdp')), as said below
- first_moment: float32 [3147776], P(('dp', 'fsdp')), may hold values from -150 to 150
- second_moment: float32 [3147776], P(('dp', 'fsdp')), may hold values from 100 to 10000
- step_count: int32 [1], replicated, may hold values from 1 to 20
Outputs:
- output: bfloat16 [49152, 512], P(('dp', 'fsdp'))
- grad_input: bfloat16 [49152, 512], P(('dp', 'fsdp'))
- grads: float32 [3147776], P(('dp', 'fsdp'))
- new_first: float32 [3147776], P(('dp', 'fsdp'))
- new_second: float32 [3147776], P(('dp', 'fsdp'))
- adam_step: float32 [3147776], P(('dp', 'fsdp'))
- bias_two_grad: float32 [512], replicated
The draws below stay inside these ranges and needn't reach their ends.
Inputs may be any that keep to these rules, and one draw needn't show every extreme that they name: `table_lengths`: on every device the lengths sum to 1536, and one table has exactly 1024 rows. `support_counts`: each table's support count is between a quarter (at least one) and three quarters of its rows. `master`: gains lie near one.
All inputs are finite; a program needn't handle non-finite values.
Results may differ from the reference program's by a relative error of at most 0.012.
The reference program's roundings to bfloat16 on the way count: a program that leaves them out, or rounds other values in their place, can miss the bound.
Values may be sent and summed in bfloat16 or wider, within the bound.
A program may use at most 192 MiB of HBM per device.

```python
import math
import jax
import jax.numpy as jnp
from jax import lax

D = 512
FF = 2048
HEADS = 4
HEAD = 128
TOK_DEV = 1536
GROUPS = 32
TOKENS = 49152
NPARAM = 3147776


def table_draw(key):
    base_key = jax.random.fold_in(key, 11)
    shortest = TOK_DEV // 24
    longest = 2 * TOK_DEV // 3
    remainder = TOK_DEV - longest

    def one_row(row_index):
        row_key = jax.random.fold_in(base_key, row_index)
        key_cut, key_order, key_support = jax.random.split(row_key, 3)
        extra_rows = jax.random.randint(key_cut, (2,), 0, 2 * shortest + 1, dtype=jnp.int32)
        first_extra = jnp.where(row_index == 0, jnp.int32(0), extra_rows[0])
        first_len = shortest + first_extra
        second_len = shortest + extra_rows[1]
        sizes_row = jnp.stack([jnp.int32(longest), first_len, second_len, jnp.int32(remainder) - first_len - second_len]).astype(jnp.int32)
        low_bound = jnp.maximum(sizes_row // 4, 1)
        high_bound = 3 * sizes_row // 4 + 1
        support_row = jax.random.randint(key_support, (4,), low_bound, high_bound, dtype=jnp.int32)
        slot = jnp.arange(4, dtype=jnp.int32)
        support_row = jnp.where((row_index == 0) & (slot == 0), jnp.int32(3 * longest // 4), support_row)
        support_row = jnp.where((row_index == 0) & (slot == 1), jnp.int32(max(shortest // 4, 1)), support_row)
        table_order = jax.random.permutation(key_order, 4)
        return (sizes_row[table_order].astype(jnp.int32), support_row[table_order].astype(jnp.int32))
    return jax.vmap(one_row)(jnp.arange(GROUPS, dtype=jnp.int32))


def draw_table_lengths(key, part):
    return table_draw(key)[0]


def draw_support_counts(key, part):
    return table_draw(key)[1]


def draw_master(key, part):
    position = jnp.arange(NPARAM)
    random_normal = jnp.clip(jax.random.normal(jax.random.fold_in(key, 5), (NPARAM,), jnp.float32), -4.0, 4.0)
    start_out = 4 * D + 3 * D * D
    start_up = start_out + D * D
    start_down = start_up + D * FF
    spread = jnp.where(position < D, 0.15, jnp.where(position < 2 * D, 0.2, jnp.where(position < 3 * D, 0.15, jnp.where(position < 4 * D, 0.2, jnp.where(position < start_out, 1.3 / math.sqrt(D), jnp.where(position < start_up, 6.0 / math.sqrt(D), jnp.where(position < start_down, 1.0 / math.sqrt(D), 1.5 / math.sqrt(FF))))))))
    offset = jnp.where((position < D) | (position >= 2 * D) & (position < 3 * D), 1.0, 0.0)
    return (offset + spread * random_normal).astype(jnp.float32)


def level_of(own_key, dims, cuts, least, high):
    level = 1.0
    for dim, blocks in cuts:
        steps = jax.random.uniform(jax.random.fold_in(jax.random.fold_in(own_key, 6), dim), (blocks,), jnp.float32, least / len(cuts), high / len(cuts))
        level = level * jnp.repeat(jnp.exp(steps), dims[dim] // blocks).reshape((-1,) + (1,) * (len(dims) - 1 - dim))
    return level


def centred(rng, dims, deviation, most, cuts=(), kind=jnp.bfloat16):
    factor_of = level_of(rng, dims, cuts, -0.22, 0.18) if cuts else 1.0
    drawn = jax.random.normal(rng, dims, jnp.float32) * deviation * factor_of
    return jnp.minimum(jnp.maximum(drawn, -most), most).astype(kind)


def setup_inputs(seed: int = 0) -> dict:
    key_list = jax.random.split(jax.random.key(seed), 9)
    return {
        "x_in": centred(key_list[0], (TOKENS, D), 1.0, 6.0, ((0, 32),)),
        "cotangent": centred(key_list[1], (TOKENS, D), 1.0, 6.0, ((0, 32),)),
        "table_lengths": draw_table_lengths(jax.random.fold_in(key_list[8], 71), 0),
        "support_counts": draw_support_counts(jax.random.fold_in(key_list[8], 71), 0),
        "master": draw_master(jax.random.fold_in(key_list[8], 71), 0),
        "first_moment": centred(key_list[5], (NPARAM,), 30.0, 150.0, ((0, 32),), jnp.float32),
        "second_moment": jnp.clip(jnp.exp(math.log(10000.0) - 4.6051702 * jax.random.uniform(key_list[6], (NPARAM,), jnp.float32) ** level_of(key_list[6], (NPARAM,), ((0, 32),), -0.2, 0.2)), 100.0, 10000.0),
        "step_count": jax.random.randint(key_list[7], (1,), 1, 21).astype(jnp.int32),
    }


@jax.custom_vjp
def low(v):
    return lax.optimization_barrier(v.astype(jnp.bfloat16)).astype(jnp.float32)

@jax.custom_vjp
def low_back(v):
    return v

def low_keep(v):
    return (low(v), None)

def low_pass(kept, grad):
    return (grad,)

def back_keep(v):
    return (v, None)

def back_low(kept, grad):
    return (low(grad),)
low.defvjp(low_keep, low_pass)
low_back.defvjp(back_keep, back_low)
EPS_NORM = 1e-05
BETA_ONE = 0.9
BETA_TWO = 0.999
ADAM_EPS = 1e-08
DECAY_RATE = 0.01
MASKED = -1e+30
HIGHEST = lax.Precision.HIGHEST

def unpack(flat, model_width, ffn_width):
    square_size = model_width * model_width
    gain_one = flat[0:model_width]
    bias_one = flat[model_width:2 * model_width]
    gain_two = flat[2 * model_width:3 * model_width]
    bias_two = flat[3 * model_width:4 * model_width]
    start_qkv = 4 * model_width
    start_out = start_qkv + 3 * square_size
    start_up = start_out + square_size
    start_down = start_up + model_width * ffn_width
    w_qkv = flat[start_qkv:start_out].reshape(model_width, 3 * model_width)
    w_out = flat[start_out:start_up].reshape(model_width, model_width)
    w_up = flat[start_up:start_down].reshape(model_width, ffn_width)
    w_down = flat[start_down:start_down + ffn_width * model_width].reshape(ffn_width, model_width)
    return (gain_one, bias_one, gain_two, bias_two, w_qkv, w_out, w_up, w_down)

def token_tables(lengths, support, row_count):
    ends = jnp.cumsum(lengths).astype(jnp.int32)
    starts = (ends - lengths).astype(jnp.int32)
    position = jnp.arange(row_count, dtype=jnp.int32)
    table_id = lax.optimization_barrier(jnp.sum((position[:, None] >= ends[None, :]).astype(jnp.int32), axis=1)).astype(jnp.int32)
    one_hot = table_id[:, None] == jnp.arange(lengths.shape[0], dtype=jnp.int32)[None, :]
    token_start = lax.optimization_barrier(jnp.sum(jnp.where(one_hot, starts[None, :], 0), axis=1)).astype(jnp.int32)
    token_support = lax.optimization_barrier(jnp.sum(jnp.where(one_hot, support[None, :], 0), axis=1)).astype(jnp.int32)
    return (table_id, position - token_start < token_support)

def layer_norm(values, gain, bias):
    centre = values - lax.optimization_barrier(jnp.mean(values, axis=-1, keepdims=True))
    inverse = lax.rsqrt(lax.optimization_barrier(jnp.mean(centre * centre, axis=-1, keepdims=True)) + EPS_NORM)
    normed = centre * inverse
    return (normed, inverse, normed * gain + bias)

def gelu_tanh(values):
    inner = math.sqrt(2.0 / math.pi) * (values + 0.044715 * values * values * values)
    return 0.5 * values * (1.0 + jnp.tanh(inner))

def device_rows(params, rows_in, lengths, support):
    gain_one, bias_one, gain_two, bias_two, w_qkv, w_out, w_up, w_down = unpack(params, D, FF)
    row_count = rows_in.shape[0]
    table_id, support_flag = token_tables(lengths, support, row_count)
    _, _, hidden_one = layer_norm(rows_in, gain_one, bias_one)
    act_one = low(hidden_one)
    qkv = low_back(low(jnp.dot(act_one, w_qkv, precision=HIGHEST)))
    query = qkv[:, :D].reshape(row_count, HEADS, HEAD)
    keys = qkv[:, D:2 * D].reshape(row_count, HEADS, HEAD)
    values = qkv[:, 2 * D:].reshape(row_count, HEADS, HEAD)
    block_rows = min(512, row_count)
    block_count = row_count // block_rows
    score_scale = 1.0 / math.sqrt(HEAD)

    def attend(inputs):
        query_block, table_block = inputs
        scores = score_scale * jnp.einsum('qhd,khd->hqk', query_block, keys, precision=HIGHEST)
        allowed = (table_block[:, None] == table_id[None, :]) & support_flag[None, :]
        scores = low_back(jnp.where(allowed[None], scores, MASKED))
        row_max = lax.optimization_barrier(jnp.max(scores, axis=-1, keepdims=True))
        shifted = jnp.exp(scores - row_max)
        attn_probs = shifted / lax.optimization_barrier(jnp.sum(shifted, axis=-1, keepdims=True))
        return jnp.einsum('hqk,khd->qhd', low(attn_probs), values, precision=HIGHEST)
    context = lax.map(jax.checkpoint(attend), (query.reshape(block_count, block_rows, HEADS, HEAD), table_id.reshape(block_count, block_rows)))
    context = low_back(low(context.reshape(row_count, D)))
    resid = rows_in + low_back(jnp.dot(context, w_out, precision=HIGHEST))
    _, _, hidden_two = layer_norm(resid, gain_two, bias_two)
    act_two = low(hidden_two)
    pre = low_back(jnp.dot(act_two, w_up, precision=HIGHEST))
    hidden = low(gelu_tanh(pre))
    return resid + low_back(jnp.dot(hidden, w_down, precision=HIGHEST))

def reference(x_in, cotangent, table_lengths, support_counts, master, first_moment, second_moment, step_count):
    rows_all = x_in.astype(jnp.float32).reshape(GROUPS, TOK_DEV, D)

    def layer(master_copy, inputs_all):
        params = low(master_copy)

        def one_group(running, inputs):
            rows_in, lengths, support = inputs
            return (running, jax.checkpoint(device_rows)(params, rows_in, lengths, support))
        _, outputs = lax.scan(one_group, jnp.zeros((), jnp.float32), (inputs_all, table_lengths, support_counts))
        return outputs
    outputs, pullback = jax.vjp(layer, master, rows_all)
    grads, grad_rows = pullback(cotangent.astype(jnp.float32).reshape(GROUPS, TOK_DEV, D))
    step_float = step_count[0].astype(jnp.float32)
    new_first = BETA_ONE * first_moment + (1.0 - BETA_ONE) * grads
    new_second = BETA_TWO * second_moment + (1.0 - BETA_TWO) * grads * grads
    first_hat = new_first / (1.0 - jnp.power(jnp.float32(BETA_ONE), step_float))
    second_hat = new_second / (1.0 - jnp.power(jnp.float32(BETA_TWO), step_float))
    adam_step = first_hat / (jnp.sqrt(second_hat) + ADAM_EPS) + DECAY_RATE * master
    return (outputs.reshape(TOKENS, D).astype(jnp.bfloat16), grad_rows.reshape(TOKENS, D).astype(jnp.bfloat16), grads, new_first, new_second, adam_step, grads[3 * D:4 * D])
```

```python
import functools
import math

import jax
import jax.numpy as jnp
from jax import lax
from jax.experimental import pallas as pl
from jax.experimental.pallas import tpu as pltpu
from jax.sharding import PartitionSpec as P

HEAD = 128
EPS_NORM = 1e-05
BETA_ONE = 0.9
BETA_TWO = 0.999
ADAM_EPS = 1e-08
DECAY_RATE = 0.01
MASKED = -1e30
F32 = jnp.float32
BF16 = jnp.bfloat16
BLOCK = 256
CUT = 128
GELU_ONE = math.sqrt(2.0 / math.pi)
GELU_THREE = 0.044715


def mm(left, right):
    return jnp.dot(left, right, preferred_element_type=F32)


def mm_t(left, right):
    return lax.dot_general(left, right, (((1,), (1,)), ((), ())), preferred_element_type=F32)


def rows_at(index, size=BLOCK):
    return pl.ds(pl.multiple_of(index * size, size), size)


class Shapes:
    def __init__(self, rows, width, ffn):
        self.rows, self.width, self.ffn = rows, width, ffn
        self.heads = width // HEAD
        self.big = 2 * rows // 3
        self.big_keys = 3 * self.big // 4
        self.small = rows - self.big


def table_facts(sz, len_ref, sup_ref):
    lengths = [len_ref[0, t] for t in range(4)]
    support = [sup_ref[0, t] for t in range(4)]
    starts = [jnp.int32(0), lengths[0], lengths[0] + lengths[1], lengths[0] + lengths[1] + lengths[2]]
    is_big = [lengths[t] == sz.big for t in range(4)]

    def pick(values):
        total = jnp.int32(0)
        for t in range(4):
            total = total + jnp.where(is_big[t], values[t], 0)
        return total

    shift = pick(starts)
    lens = [pick([lengths[(t + j) % 4] for t in range(4)]) for j in range(4)]
    sups = [pick([support[(t + j) % 4] for t in range(4)]) for j in range(4)]
    begins = [jnp.int32(0), lens[0], lens[0] + lens[1], lens[0] + lens[1] + lens[2]]
    return shift, begins, sups


def mask_features(sz, begins, sups, qm_ref, km_ref):
    def step(i, carry):
        shape = (BLOCK, HEAD)
        row = lax.broadcasted_iota(jnp.int32, shape, 0) + i * BLOCK
        lane = lax.broadcasted_iota(jnp.int32, shape, 1)
        table = jnp.zeros(shape, jnp.int32)
        limit = jnp.full(shape, begins[0] + sups[0], jnp.int32)
        for t in range(1, 4):
            inside = row >= begins[t]
            table = jnp.where(inside, t, table)
            limit = jnp.where(inside, begins[t] + sups[t], limit)
        own = table == lane
        qm_ref[rows_at(i), :] = jnp.where(own, 1.0, 0.0).astype(BF16)
        bad = jnp.where(own, jnp.where(row < limit, 0.0, MASKED), jnp.where(lane < 4, MASKED, 0.0))
        km_ref[rows_at(i), :] = bad.astype(BF16)
        return carry

    lax.fori_loop(0, sz.rows // BLOCK, step, 0)


def roll_rows(sz, shift, read, write):
    blocks = sz.rows // CUT
    coarse, fine = shift // CUT, shift % CUT
    row = lax.broadcasted_iota(jnp.int32, (CUT, 2 * CUT), 0)
    column = lax.broadcasted_iota(jnp.int32, (CUT, 2 * CUT), 1)
    chosen = jnp.where(row + fine == column, 1.0, 0.0).astype(BF16)

    def step(i, carry):
        here = lax.rem(i + coarse, blocks)
        after = lax.rem(i + coarse + 1, blocks)
        pair = jnp.concatenate([read(rows_at(here, CUT)), read(rows_at(after, CUT))], axis=0)
        write(rows_at(i, CUT), mm(chosen, pair).astype(BF16))
        return carry

    lax.fori_loop(0, blocks, step, 0)


def normed(values):
    centre = values - jnp.mean(values, axis=-1, keepdims=True)
    inverse = lax.rsqrt(jnp.mean(centre * centre, axis=-1, keepdims=True) + EPS_NORM)
    return centre * inverse, inverse


def norm_back(grad_out, norm, inverse, gain):
    grad_normed = grad_out * gain
    return inverse * (
        grad_normed
        - jnp.mean(grad_normed, axis=-1, keepdims=True)
        - norm * jnp.mean(grad_normed * norm, axis=-1, keepdims=True)
    )


def eight_rows(values):
    rows, width = values.shape
    return jnp.sum(values.reshape(rows // 8, 8, width), axis=0)


def phase_qkv(sz, gb_ref, xr, act_t, w_qkv, qkv, kv_t):
    gain, bias = gb_ref[0:1, :], gb_ref[1:2, :]

    def step(i, carry):
        norm, _ = normed(xr[rows_at(i), :].astype(F32))
        act = (norm * gain + bias).astype(BF16)
        act_t[:, rows_at(i)] = act.T
        out = mm(act, w_qkv[...]).astype(BF16)
        qkv[rows_at(i), :] = out
        kv_t[:, rows_at(i)] = out[:, sz.width :].T
        return carry

    lax.fori_loop(0, sz.rows // BLOCK, step, 0)


def head_at(head, offset=0):
    return pl.ds(pl.multiple_of(offset + head * HEAD, HEAD), HEAD)


def attend_forward(sz, base, key_count, query_count, exps, qkv, kv_t, qm, km, ctx, ctx_t, inv_ref):
    keep = pl.ds(base, key_count)
    scale = math.log2(math.e) / math.sqrt(HEAD)

    def per_head(head, carry):
        keys = jnp.concatenate([qkv[keep, head_at(head, sz.width)], km[keep, :]], axis=1)
        values_t = kv_t[head_at(head, sz.width), keep]
        for j in range(query_count // BLOCK):
            here = pl.ds(base + j * BLOCK, BLOCK)
            queries = jnp.concatenate([qkv[here, head_at(head)], qm[here, :]], axis=1)
            scores = mm_t(keys, queries)
            top = jnp.max(scores, axis=0, keepdims=True)
            shifted = jnp.exp2((scores - top) * scale)
            total = jnp.sum(shifted, axis=0, keepdims=True)
            low = shifted.astype(BF16)
            exps[head, :, pl.ds(j * BLOCK, BLOCK)] = low
            inverse = 1.0 / total
            mixed = (mm(values_t, low) * inverse).astype(BF16)
            ctx_t[head_at(head), here] = mixed
            ctx[here, head_at(head)] = mixed.T
            inv_ref[head, :, here] = jnp.broadcast_to(inverse, (8, BLOCK))
        return carry

    lax.fori_loop(0, sz.heads, per_head, 0)


def phase_ffn(sz, gb_ref, xr, cr, ctx, inv_ref, w_out, w_up, w_down, act_t, cot_t, hid, gpre, out_r, gres, gres_low, dox, sums):
    gain, bias = gb_ref[2:3, :], gb_ref[3:4, :]
    cut = 512

    def step(i, carry):
        here = rows_at(i)
        resid = xr[here, :].astype(F32) + mm(ctx[here, :], w_out[...])
        norm, inverse = normed(resid)
        act = (norm * gain + bias).astype(BF16)
        act_t[:, here] = act.T
        cot = cr[here, :]
        cot_t[:, here] = cot.T
        total = resid
        grad_act = jnp.zeros_like(resid)
        for f in range(sz.ffn // cut):
            part = slice(f * cut, (f + 1) * cut)
            pre = mm(act, w_up[:, part])
            grad_hidden = mm_t(cot, w_down[part, :])
            square = pre * pre
            bent = jnp.tanh(pre * (GELU_ONE + GELU_ONE * GELU_THREE * square))
            half = 0.5 + 0.5 * bent
            hidden = (pre * half).astype(BF16)
            slope = half + pre * (half * (1.0 - bent)) * (GELU_ONE + 3.0 * GELU_ONE * GELU_THREE * square)
            grad_pre = (grad_hidden * slope).astype(BF16)
            hid[here, part] = hidden
            gpre[here, part] = grad_pre
            total = total + mm(hidden, w_down[part, :])
            grad_act = grad_act + mm_t(grad_pre, w_up[:, part])
        out_r[here, :] = total.astype(BF16)
        sums[2] += eight_rows(grad_act * norm)
        sums[3] += eight_rows(grad_act)
        grad = cot.astype(F32) + norm_back(grad_act, norm, inverse, gain)
        gres[here, :] = grad
        low = grad.astype(BF16)
        gres_low[here, :] = low
        grad_ctx = mm_t(low, w_out[...]).astype(BF16).astype(F32)
        lane = lax.broadcasted_iota(jnp.int32, (BLOCK, HEAD), 1)
        for head in range(sz.heads):
            part = slice(head * HEAD, (head + 1) * HEAD)
            column = inv_ref[head, :, here].T[:, 0:1]
            scaled = (grad_ctx[:, part] * column).astype(BF16)
            delta = jnp.sum(scaled.astype(F32) * ctx[here, part].astype(F32), axis=1, keepdims=True)
            high = delta.astype(BF16).astype(F32)
            rest = delta - high
            dox[head, here, 0:HEAD] = scaled
            dox[head, here, HEAD : 2 * HEAD] = jnp.where(lane == 0, -high, jnp.where(lane == 1, -rest, 0.0)).astype(BF16)
        return carry

    lax.fori_loop(0, sz.rows // BLOCK, step, 0)


def weight_grad(left_t, right, columns, store, turn=False):
    def step(i, carry):
        product = mm(left_t[...], right[:, rows_at(i)]).astype(BF16)
        if turn:
            store[rows_at(i), :] = product.T
        else:
            store[:, rows_at(i)] = product
        return carry

    lax.fori_loop(0, columns // BLOCK, step, 0)


def attend_backward(sz, base, key_count, query_count, exps, qkv, kv_t, dox, gqkv):
    keep = pl.ds(base, key_count)
    asked = pl.ds(base, query_count)
    scale = 1.0 / math.sqrt(HEAD)
    lane = lax.broadcasted_iota(jnp.int32, (key_count, HEAD), 1)
    ones = jnp.where(lane < 2, 1.0, 0.0).astype(BF16)

    def per_head(head, carry):
        values = jnp.concatenate([qkv[keep, head_at(head, 2 * sz.width)], ones], axis=1)
        keys_t = kv_t[head_at(head), keep]
        gqkv[keep, head_at(head, 2 * sz.width)] = mm(exps[head], dox[head, asked, 0:HEAD]).astype(BF16)
        for j in range(query_count // BLOCK):
            here = pl.ds(base + j * BLOCK, BLOCK)
            columns = pl.ds(j * BLOCK, BLOCK)
            grad_probs = mm_t(values, dox[head, here, :])
            grad_scores = (exps[head, :, columns].astype(F32) * grad_probs).astype(BF16)
            exps[head, :, columns] = grad_scores
            gqkv[here, head_at(head)] = (mm(keys_t, grad_scores) * scale).astype(BF16).T
        gqkv[keep, head_at(head, sz.width)] = (mm(exps[head], qkv[asked, head_at(head)]) * scale).astype(BF16)
        return carry

    lax.fori_loop(0, sz.heads, per_head, 0)


def phase_input(sz, gb_ref, xr, gqkv, w_qkv, gres, gin_r, sums):
    gain = gb_ref[0:1, :]

    def step(i, carry):
        here = rows_at(i)
        grad_act = mm_t(gqkv[here, 0 : 3 * sz.width], w_qkv[...])
        norm, inverse = normed(xr[here, :].astype(F32))
        sums[0] += eight_rows(grad_act * norm)
        sums[1] += eight_rows(grad_act)
        gin_r[here, :] = (gres[here, :] + norm_back(grad_act, norm, inverse, gain)).astype(BF16)
        return carry

    lax.fori_loop(0, sz.rows // BLOCK, step, 0)


def layer_kernel(
    sz,
    len_ref, sup_ref, x_hbm, cot_hbm, gb_ref, w_qkv_hbm, w_out_hbm, w_up_hbm, w_down_hbm,
    out_hbm, gin_hbm, g_qkv_hbm, g_out_hbm, g_up_hbm, g_down_hbm, small_ref,
    xr, cr, act1_t, act2_t, cot_t, qkv, kv_t, exps_big, exps_small, ctx, ctx_t, hid, gpre, gres, gres_low, dox, out_r,
    qm, km, inv_ref, sums, w_qkv, w_out, w_up, w_down, in_sem, out_sem,
):
    width = sz.width
    load_x = pltpu.make_async_copy(x_hbm, hid.at[:, 0:width], in_sem.at[0])
    load_c = pltpu.make_async_copy(cot_hbm, hid.at[:, width : 2 * width], in_sem.at[1])
    loads = [
        pltpu.make_async_copy(src, dst, in_sem.at[2 + i])
        for i, (src, dst) in enumerate(
            ((w_qkv_hbm, w_qkv), (w_out_hbm, w_out), (w_up_hbm, w_up), (w_down_hbm, w_down))
        )
    ]
    for copy in (load_x, load_c, *loads):
        copy.start()
    shift, begins, sups = table_facts(sz, len_ref, sup_ref)
    mask_features(sz, begins, sups, qm, km)
    sums[...] = jnp.zeros_like(sums)

    load_x.wait()
    roll_rows(sz, shift, lambda r: hid[r, 0:width], lambda r, v: xr.__setitem__((r, slice(None)), v))
    load_c.wait()
    roll_rows(sz, shift, lambda r: hid[r, width : 2 * width], lambda r, v: cr.__setitem__((r, slice(None)), v))

    loads[0].wait()
    phase_qkv(sz, gb_ref, xr, act1_t, w_qkv, qkv, kv_t)
    attend_forward(sz, 0, sz.big_keys, sz.big, exps_big, qkv, kv_t, qm, km, ctx, ctx_t, inv_ref)
    attend_forward(sz, sz.big, sz.small, sz.small, exps_small, qkv, kv_t, qm, km, ctx, ctx_t, inv_ref)
    for copy in loads[1:]:
        copy.wait()
    phase_ffn(sz, gb_ref, xr, cr, ctx, inv_ref, w_out, w_up, w_down, act2_t, cot_t, hid, gpre, out_r, gres, gres_low, dox, sums)
    gs_out, gs_up, gs_down = w_out, w_up, w_down
    gs_qkv = gpre.at[0:width, 0 : 3 * width]
    stores = []

    def put(src, dst):
        copy = pltpu.make_async_copy(src, dst, out_sem.at[len(stores)])
        copy.start()
        stores.append(copy)

    weight_grad(cot_t, hid, sz.ffn, gs_down, turn=True)
    put(gs_down, g_down_hbm)
    weight_grad(act2_t, gpre, sz.ffn, gs_up)
    put(gs_up, g_up_hbm)
    weight_grad(ctx_t, gres_low, width, gs_out)
    put(gs_out, g_out_hbm)

    back = lax.rem(sz.rows - shift, sz.rows)
    roll_rows(sz, back, lambda r: out_r[r, :], lambda r, v: ctx.__setitem__((r, slice(None)), v))
    put(ctx, out_hbm)

    gqkv = hid
    gqkv[sz.big_keys : sz.big, width : 3 * width] = jnp.zeros((sz.big - sz.big_keys, 2 * width), BF16)
    attend_backward(sz, 0, sz.big_keys, sz.big, exps_big, qkv, kv_t, dox, gqkv)
    attend_backward(sz, sz.big, sz.small, sz.small, exps_small, qkv, kv_t, dox, gqkv)
    weight_grad(act1_t, gqkv, 3 * width, gs_qkv)
    put(gs_qkv, g_qkv_hbm)
    gin_r = gres_low
    phase_input(sz, gb_ref, xr, gqkv, w_qkv, gres, gin_r, sums)
    roll_rows(sz, back, lambda r: gin_r[r, :], lambda r, v: cr.__setitem__((r, slice(None)), v))
    put(cr, gin_hbm)
    for t in range(4):
        small_ref[t : t + 1, :] = jnp.sum(sums[t], axis=0, keepdims=True)
    for copy in stores:
        copy.wait()


def layer(x_in, cotangent, lengths, support, gains, w_qkv, w_out, w_up, w_down):
    rows, width = x_in.shape
    ffn = w_up.shape[1]
    sz = Shapes(rows, width, ffn)
    anywhere = pl.BlockSpec(memory_space=pl.ANY)
    vmem = pl.BlockSpec(memory_space=pltpu.VMEM)
    smem = pl.BlockSpec(memory_space=pltpu.SMEM)

    def low(*shape):
        return pltpu.VMEM(shape, BF16)

    scratch = [
        low(rows, width), low(rows, width), low(width, rows), low(width, rows), low(width, rows),
        low(rows, 3 * width), low(2 * width, rows),
        low(sz.heads, sz.big_keys, sz.big), low(sz.heads, sz.small, sz.small),
        low(rows, width), low(width, rows), low(rows, ffn), low(rows, ffn),
        pltpu.VMEM((rows, width), F32), low(rows, width), low(sz.heads, rows, 2 * HEAD), low(rows, width),
        low(rows, HEAD), low(rows, HEAD), pltpu.VMEM((sz.heads, 8, rows), F32), pltpu.VMEM((4, 8, width), F32),
        low(width, 3 * width), low(width, width), low(width, ffn), low(ffn, width),
        pltpu.SemaphoreType.DMA((6,)), pltpu.SemaphoreType.DMA((6,)),
    ]
    return pl.pallas_call(
        functools.partial(layer_kernel, sz),
        out_shape=(
            jax.ShapeDtypeStruct((rows, width), BF16),
            jax.ShapeDtypeStruct((rows, width), BF16),
            jax.ShapeDtypeStruct((width, 3 * width), BF16),
            jax.ShapeDtypeStruct((width, width), BF16),
            jax.ShapeDtypeStruct((width, ffn), BF16),
            jax.ShapeDtypeStruct((ffn, width), BF16),
            jax.ShapeDtypeStruct((4, width), F32),
        ),
        in_specs=[smem, smem, anywhere, anywhere, vmem, anywhere, anywhere, anywhere, anywhere],
        out_specs=[anywhere] * 6 + [vmem],
        scratch_shapes=scratch,
        compiler_params=pltpu.CompilerParams(vmem_limit_bytes=61 * 2**20),
    )(lengths, support, x_in, cotangent, gains, w_qkv, w_out, w_up, w_down)


def adam(grads, first_moment, second_moment, master, step_count):
    step_float = step_count[0].astype(F32)
    new_first = BETA_ONE * first_moment + (1.0 - BETA_ONE) * grads
    new_second = BETA_TWO * second_moment + (1.0 - BETA_TWO) * grads * grads
    first_hat = new_first / (1.0 - jnp.power(F32(BETA_ONE), step_float))
    second_hat = new_second / (1.0 - jnp.power(F32(BETA_TWO), step_float))
    adam_step = first_hat / (jnp.sqrt(second_hat) + ADAM_EPS) + DECAY_RATE * master
    return new_first, new_second, adam_step


def per_device_plain(x_in, cotangent, table_lengths, support_counts, master, first_moment, second_moment, step_count):
    width = x_in.shape[1]
    square = width * width
    axes = ("dp", "fsdp")
    flat = lax.all_gather(master.astype(BF16), axes, axis=0, tiled=True)
    ffn = (flat.shape[0] - 4 * width - 4 * square) // (2 * width)
    cuts = [0, 4 * width, 4 * width + 3 * square, 4 * width + 4 * square]
    cuts += [cuts[-1] + width * ffn, cuts[-1] + 2 * width * ffn]
    shapes = [(4, width), (width, 3 * width), (width, width), (width, ffn), (ffn, width)]
    gains, w_qkv, w_out, w_up, w_down = (flat[a:b].reshape(s) for a, b, s in zip(cuts[:-1], cuts[1:], shapes))
    output, grad_input, g_qkv, g_out, g_up, g_down, small = layer(
        x_in, cotangent, table_lengths, support_counts, gains.astype(F32), w_qkv, w_out, w_up, w_down
    )
    local = jnp.concatenate([v.astype(F32).reshape(-1) for v in (small, g_qkv, g_out, g_up, g_down)])
    bias_two_grad = lax.psum(small[3], axes)
    grads = lax.psum_scatter(local, axes, scatter_dimension=0, tiled=True)
    new_first, new_second, adam_step = adam(grads, first_moment, second_moment, master, step_count)
    return output, grad_input, grads, new_first, new_second, adam_step, bias_two_grad


def solution(mesh):
    rows, flat = P(("dp", "fsdp"), None), P(("dp", "fsdp"))
    return jax.shard_map(
        per_device_plain,
        mesh=mesh,
        in_specs=(rows, rows, rows, rows, flat, flat, flat, P()),
        out_specs=(rows, rows, flat, flat, flat, flat, P()),
        check_vma=False,
    )
```

```python
import functools
import math

import jax
import jax.numpy as jnp
from jax import lax
from jax.experimental import pallas as pl
from jax.experimental.pallas import tpu as pltpu
from jax.sharding import PartitionSpec as P

HEAD = 128
EPS_NORM = 1e-05
BETA_ONE = 0.9
BETA_TWO = 0.999
ADAM_EPS = 1e-08
DECAY_RATE = 0.01
MASKED = -1e30
F32 = jnp.float32
BF16 = jnp.bfloat16
BLOCK = 256
CUT = 128
GELU_ONE = math.sqrt(2.0 / math.pi)
GELU_THREE = 0.044715


def mm(left, right):
    return jnp.dot(left, right, preferred_element_type=F32)


def mm_t(left, right):
    return lax.dot_general(left, right, (((1,), (1,)), ((), ())), preferred_element_type=F32)


def rows_at(index, size=BLOCK):
    return pl.ds(pl.multiple_of(index * size, size), size)


class Shapes:
    def __init__(self, rows, width, ffn):
        self.rows, self.width, self.ffn = rows, width, ffn
        self.heads = width // HEAD
        self.big = 2 * rows // 3
        self.big_keys = 3 * self.big // 4
        self.small = rows - self.big


MESH = pl.DeviceIdType.MESH
LINE = 4
PLANE = 8
DEVICES = LINE * PLANE
HALO = 16


class Layout:
    def __init__(self, width, ffn):
        self.width, self.ffn = width, ffn
        shapes = [(width, 3 * width), (width, width), (width, ffn), (ffn, width)]
        self.blocks = [s[1] // HEAD for s in shapes]
        self.flat_rows = sum(r * c for r, c in shapes) // (HEAD * DEVICES)
        ends, total = [], 0
        for r, c in shapes:
            total += r * c // HEAD
            ends.append(total)
        starts = [0] + ends[:-1]
        self.pieces = []
        for k in range(DEVICES):
            lo, hi, own = k * self.flat_rows, (k + 1) * self.flat_rows, []
            for m in range(4):
                a, b = max(lo, starts[m]), min(hi, ends[m])
                if a < b:
                    own.append((m, (a - starts[m]) // self.blocks[m], (b - a) // self.blocks[m], a - lo))
            self.pieces.append(own)
        self.unit = math.gcd(*(n for own in self.pieces for m, _, n, _ in own if m == 3))
        self.kinds = []
        for k, own in enumerate(self.pieces):
            last = self.kinds[-1] if self.kinds else None
            if last and len(own) == 1 and self.same(self.pieces[last[0]], own):
                last[1] = k + 1
            else:
                self.kinds.append([k, k + 1])

    @staticmethod
    def same(left, right):
        return len(left) == len(right) and all(a[0] == b[0] and a[2:] == b[2:] for a, b in zip(left, right))

    def fits(self, param_count, devices):
        whole = self.flat_rows * HEAD * DEVICES + 4 * self.width
        exact = all(
            sum(p[2] * self.blocks[p[0]] for p in own) == self.flat_rows and all(p[1] % 8 == 0 and p[2] % 8 == 0 for p in own)
            for own in self.pieces
        )
        return devices == (LINE, PLANE) and exact and whole == param_count and 4 * self.width == HALO * HEAD

    def each_kind(self, k, act):
        for lo, hi in self.kinds:
            def run(lo=lo, hi=hi):
                first = self.pieces[lo]
                if hi - lo == 1:
                    act(first)
                else:
                    m, r, n, f = first[0]
                    act([(m, pl.multiple_of(r + (k - lo) * n, 8), n, f)])

            pl.when((k >= lo) & (k < hi))(run)

    def halves(self, pieces):
        goal, done, parts = self.flat_rows // 2, 0, ([], [])
        for m, r, n, f in pieces:
            take = min(n, max(0, (goal - done)) // self.blocks[m])
            if take:
                parts[0].append((m, r, take, f))
            if n - take:
                parts[1].append((m, r + take, n - take, f + take * self.blocks[m]))
            done += take * self.blocks[m]
        return parts


def table_facts(sz, len_ref, sup_ref):
    lengths = [len_ref[0, t] for t in range(4)]
    support = [sup_ref[0, t] for t in range(4)]
    starts = [jnp.int32(0), lengths[0], lengths[0] + lengths[1], lengths[0] + lengths[1] + lengths[2]]
    is_big = [lengths[t] == sz.big for t in range(4)]

    def pick(values):
        total = jnp.int32(0)
        for t in range(4):
            total = total + jnp.where(is_big[t], values[t], 0)
        return total

    shift = pick(starts)
    lens = [pick([lengths[(t + j) % 4] for t in range(4)]) for j in range(4)]
    sups = [pick([support[(t + j) % 4] for t in range(4)]) for j in range(4)]
    begins = [jnp.int32(0), lens[0], lens[0] + lens[1], lens[0] + lens[1] + lens[2]]
    return shift, begins, sups


def mask_features(sz, begins, sups, qm_ref, km_ref):
    def step(i, carry):
        shape = (BLOCK, HEAD)
        row = lax.broadcasted_iota(jnp.int32, shape, 0) + i * BLOCK
        lane = lax.broadcasted_iota(jnp.int32, shape, 1)
        table = jnp.zeros(shape, jnp.int32)
        limit = jnp.full(shape, begins[0] + sups[0], jnp.int32)
        for t in range(1, 4):
            inside = row >= begins[t]
            table = jnp.where(inside, t, table)
            limit = jnp.where(inside, begins[t] + sups[t], limit)
        own = table == lane
        qm_ref[rows_at(i), :] = jnp.where(own, 1.0, 0.0).astype(BF16)
        bad = jnp.where(own, jnp.where(row < limit, 0.0, MASKED), jnp.where(lane < 4, MASKED, 0.0))
        km_ref[rows_at(i), :] = bad.astype(BF16)
        return carry

    lax.fori_loop(0, sz.rows // BLOCK, step, 0)


def roll_rows(sz, shift, read, write):
    blocks = sz.rows // CUT
    coarse, fine = shift // CUT, shift % CUT
    row = lax.broadcasted_iota(jnp.int32, (CUT, 2 * CUT), 0)
    column = lax.broadcasted_iota(jnp.int32, (CUT, 2 * CUT), 1)
    chosen = jnp.where(row + fine == column, 1.0, 0.0).astype(BF16)

    def step(i, carry):
        here = lax.rem(i + coarse, blocks)
        after = lax.rem(i + coarse + 1, blocks)
        pair = jnp.concatenate([read(rows_at(here, CUT)), read(rows_at(after, CUT))], axis=0)
        write(rows_at(i, CUT), mm(chosen, pair).astype(BF16))
        return carry

    lax.fori_loop(0, blocks, step, 0)


def normed(values):
    centre = values - jnp.mean(values, axis=-1, keepdims=True)
    inverse = lax.rsqrt(jnp.mean(centre * centre, axis=-1, keepdims=True) + EPS_NORM)
    return centre * inverse, inverse


def norm_back(grad_out, norm, inverse, gain):
    grad_normed = grad_out * gain
    return inverse * (
        grad_normed
        - jnp.mean(grad_normed, axis=-1, keepdims=True)
        - norm * jnp.mean(grad_normed * norm, axis=-1, keepdims=True)
    )


def eight_rows(values):
    rows, width = values.shape
    return jnp.sum(values.reshape(rows // 8, 8, width), axis=0)


def phase_qkv(sz, gb_ref, xr, act_t, w_qkv, qkv):
    gain, bias = gb_ref[0:1, :], gb_ref[1:2, :]

    def step(i, carry):
        norm, _ = normed(xr[rows_at(i), :].astype(F32))
        act = (norm * gain + bias).astype(BF16)
        act_t[:, rows_at(i)] = act.T
        qkv[rows_at(i), :] = mm(act, w_qkv[...]).astype(BF16)
        return carry

    lax.fori_loop(0, sz.rows // BLOCK, step, 0)


def head_at(head, offset=0):
    return pl.ds(pl.multiple_of(offset + head * HEAD, HEAD), HEAD)


def attend_forward(sz, base, key_count, query_count, exps, qkv, qm, km, ctx, ctx_t, inv_ref):
    keep = pl.ds(base, key_count)
    scale = math.log2(math.e) / math.sqrt(HEAD)

    def per_head(head, carry):
        keys = jnp.concatenate([qkv[keep, head_at(head, sz.width)], km[keep, :]], axis=1)
        values_t = qkv[keep, head_at(head, 2 * sz.width)].T
        for j in range(query_count // BLOCK):
            here = pl.ds(base + j * BLOCK, BLOCK)
            queries = jnp.concatenate([qkv[here, head_at(head)], qm[here, :]], axis=1)
            scores = mm_t(keys, queries)
            top = jnp.max(scores, axis=0, keepdims=True)
            shifted = jnp.exp2((scores - top) * scale)
            total = jnp.sum(shifted, axis=0, keepdims=True)
            low = shifted.astype(BF16)
            exps[head, :, pl.ds(j * BLOCK, BLOCK)] = low
            inverse = 1.0 / total
            mixed = (mm(values_t, low) * inverse).astype(BF16)
            ctx_t[head_at(head), here] = mixed
            ctx[here, head_at(head)] = mixed.T
            inv_ref[head, :, here] = jnp.broadcast_to(inverse, (8, BLOCK))
        return carry

    lax.fori_loop(0, sz.heads, per_head, 0)


def phase_ffn(sz, gb_ref, xr, cr, ctx, inv_ref, w_out, w_up, w_down, act_t, cot_t, hid, gpre, out_r, gres_low, dox, sums):
    gain, bias = gb_ref[2:3, :], gb_ref[3:4, :]
    cut = 512

    def step(i, carry):
        here = rows_at(i)
        resid = xr[here, :].astype(F32) + mm(ctx[here, :], w_out[...])
        norm, inverse = normed(resid)
        act = (norm * gain + bias).astype(BF16)
        act_t[:, here] = act.T
        cot = cr[here, :]
        cot_t[:, here] = cot.T
        total = resid
        grad_act = jnp.zeros_like(resid)
        for f in range(sz.ffn // cut):
            part = slice(f * cut, (f + 1) * cut)
            pre = mm(act, w_up[:, part])
            grad_hidden = mm_t(cot, w_down[part, :])
            square = pre * pre
            bent = jnp.tanh(pre * (GELU_ONE + GELU_ONE * GELU_THREE * square))
            half = 0.5 + 0.5 * bent
            hidden = (pre * half).astype(BF16)
            slope = half + pre * (half * (1.0 - bent)) * (GELU_ONE + 3.0 * GELU_ONE * GELU_THREE * square)
            grad_pre = (grad_hidden * slope).astype(BF16)
            hid[here, part] = hidden
            gpre[here, part] = grad_pre
            total = total + mm(hidden, w_down[part, :])
            grad_act = grad_act + mm_t(grad_pre, w_up[:, part])
        out_r[here, :] = total.astype(BF16)
        sums[2] += eight_rows(grad_act * norm)
        sums[3] += eight_rows(grad_act)
        grad = cot.astype(F32) + norm_back(grad_act, norm, inverse, gain)
        low = grad.astype(BF16)
        gres_low[here, :] = low
        grad_ctx = mm_t(low, w_out[...]).astype(BF16).astype(F32)
        lane = lax.broadcasted_iota(jnp.int32, (BLOCK, HEAD), 1)
        for head in range(sz.heads):
            part = slice(head * HEAD, (head + 1) * HEAD)
            column = inv_ref[head, :, here].T[:, 0:1]
            scaled = (grad_ctx[:, part] * column).astype(BF16)
            delta = jnp.sum(scaled.astype(F32) * ctx[here, part].astype(F32), axis=1, keepdims=True)
            high = delta.astype(BF16).astype(F32)
            rest = delta - high
            dox[head, here, 0:HEAD] = scaled
            dox[head, here, HEAD : 2 * HEAD] = jnp.where(lane == 0, -high, jnp.where(lane == 1, -rest, 0.0)).astype(BF16)
        return carry

    lax.fori_loop(0, sz.rows // BLOCK, step, 0)


def weight_grad(layout, m, left_t, right, parts):
    rows, per = layout.flat_rows, BLOCK // HEAD

    def step(i, carry):
        product = mm(left_t[...], right[:, rows_at(i)]).astype(BF16)
        for k, own in enumerate(layout.pieces):
            for matrix, r, n, f in own:
                if matrix == m:
                    for c in range(per):
                        there = pl.multiple_of(k * rows + f + (i * per + c) * n, 16)
                        parts[pl.ds(there, n), :] = product[r : r + n, c * HEAD : (c + 1) * HEAD]
        return carry

    lax.fori_loop(0, layout.blocks[m] // per, step, 0)


def weight_grad_turned(layout, m, left_t, right, parts):
    rows, unit = layout.flat_rows, layout.unit
    first_k, first = next((k, p) for k, own in enumerate(layout.pieces) for p in own if p[0] == m)
    later = layout.pieces[first_k + 1][-1][2]

    def step(i, carry):
        product = mm(left_t[...], right[:, rows_at(i)]).astype(BF16).T
        for q in range(BLOCK // unit):
            r = i * BLOCK + q * unit
            head = r < first[2]
            n = jnp.where(head, first[2], later)
            k = jnp.where(head, first_k, first_k + 1 + (r - first[2]) // later)
            base = jnp.where(head, first[3] + r, (r - first[2]) % later)
            for c in range(layout.blocks[m]):
                there = pl.multiple_of(k * rows + base + c * n, 16)
                parts[pl.ds(there, unit), :] = product[q * unit : (q + 1) * unit, c * HEAD : (c + 1) * HEAD]
        return carry

    lax.fori_loop(0, layout.ffn // BLOCK, step, 0)


def attend_backward(sz, base, key_count, query_count, exps, qkv, dox, gqkv):
    keep = pl.ds(base, key_count)
    asked = pl.ds(base, query_count)
    scale = 1.0 / math.sqrt(HEAD)
    lane = lax.broadcasted_iota(jnp.int32, (key_count, HEAD), 1)
    ones = jnp.where(lane < 2, 1.0, 0.0).astype(BF16)

    def per_head(head, carry):
        values = jnp.concatenate([qkv[keep, head_at(head, 2 * sz.width)], ones], axis=1)
        keys_t = qkv[keep, head_at(head, sz.width)].T
        gqkv[keep, head_at(head, 2 * sz.width)] = mm(exps[head], dox[head, asked, 0:HEAD]).astype(BF16)
        for j in range(query_count // BLOCK):
            here = pl.ds(base + j * BLOCK, BLOCK)
            columns = pl.ds(j * BLOCK, BLOCK)
            grad_probs = mm_t(values, dox[head, here, :])
            grad_scores = (exps[head, :, columns].astype(F32) * grad_probs).astype(BF16)
            exps[head, :, columns] = grad_scores
            gqkv[here, head_at(head)] = (mm(keys_t, grad_scores) * scale).astype(BF16).T
        gqkv[keep, head_at(head, sz.width)] = (mm(exps[head], qkv[asked, head_at(head)]) * scale).astype(BF16)
        return carry

    lax.fori_loop(0, sz.heads, per_head, 0)


def phase_input(sz, gb_ref, xr, gqkv, w_qkv, gin_r, sums):
    gain = gb_ref[0:1, :]

    def step(i, carry):
        here = rows_at(i)
        grad_act = mm_t(gqkv[here, 0 : 3 * sz.width], w_qkv[...])
        norm, inverse = normed(xr[here, :].astype(F32))
        sums[0] += eight_rows(grad_act * norm)
        sums[1] += eight_rows(grad_act)
        gin_r[here, :] = (gin_r[here, :].astype(F32) + norm_back(grad_act, norm, inverse, gain)).astype(BF16)
        return carry

    lax.fori_loop(0, sz.rows // BLOCK, step, 0)


def layer_kernel(
    sz, layout,
    len_ref, sup_ref, x_hbm, cot_hbm, gb_ref, w_qkv_hbm, w_out_hbm, w_up_hbm, w_down_hbm,
    out_hbm, gin_hbm, parts_hbm, small_ref,
    xr, cr, act1_t, act2_t, cot_t, qkv, exps_big, exps_small, ctx, ctx_t, hid, gpre, gres_low, dox, parts,
    qm, km, inv_ref, sums, w_qkv, w_out, w_up, w_down, in_sem, out_sem,
):
    width = sz.width
    load_x = pltpu.make_async_copy(x_hbm, hid.at[:, 0:width], in_sem.at[0])
    load_c = pltpu.make_async_copy(cot_hbm, hid.at[:, width : 2 * width], in_sem.at[1])
    loads = [
        pltpu.make_async_copy(src, dst, in_sem.at[2 + i])
        for i, (src, dst) in enumerate(
            ((w_qkv_hbm, w_qkv), (w_out_hbm, w_out), (w_up_hbm, w_up), (w_down_hbm, w_down))
        )
    ]
    for copy in (load_x, load_c, *loads):
        copy.start()
    shift, begins, sups = table_facts(sz, len_ref, sup_ref)
    mask_features(sz, begins, sups, qm, km)
    sums[...] = jnp.zeros_like(sums)

    load_x.wait()
    roll_rows(sz, shift, lambda r: hid[r, 0:width], lambda r, v: xr.__setitem__((r, slice(None)), v))
    load_c.wait()
    roll_rows(sz, shift, lambda r: hid[r, width : 2 * width], lambda r, v: cr.__setitem__((r, slice(None)), v))

    loads[0].wait()
    phase_qkv(sz, gb_ref, xr, act1_t, w_qkv, qkv)
    attend_forward(sz, 0, sz.big_keys, sz.big, exps_big, qkv, qm, km, ctx, ctx_t, inv_ref)
    attend_forward(sz, sz.big, sz.small, sz.small, exps_small, qkv, qm, km, ctx, ctx_t, inv_ref)
    for copy in loads[1:]:
        copy.wait()
    out_r = cr
    phase_ffn(sz, gb_ref, xr, cr, ctx, inv_ref, w_out, w_up, w_down, act2_t, cot_t, hid, gpre, out_r, gres_low, dox, sums)
    stores = []

    def put(src, dst):
        copy = pltpu.make_async_copy(src, dst, out_sem.at[len(stores)])
        copy.start()
        stores.append(copy)

    weight_grad(layout, 2, act2_t, gpre, parts)
    weight_grad_turned(layout, 3, cot_t, hid, parts)
    weight_grad(layout, 1, ctx_t, gres_low, parts)

    back = lax.rem(sz.rows - shift, sz.rows)
    roll_rows(sz, back, lambda r: out_r[r, :], lambda r, v: ctx.__setitem__((r, slice(None)), v))
    put(ctx, out_hbm)

    gqkv = hid
    gqkv[sz.big_keys : sz.big, width : 3 * width] = jnp.zeros((sz.big - sz.big_keys, 2 * width), BF16)
    attend_backward(sz, 0, sz.big_keys, sz.big, exps_big, qkv, dox, gqkv)
    attend_backward(sz, sz.big, sz.small, sz.small, exps_small, qkv, dox, gqkv)
    weight_grad(layout, 0, act1_t, gqkv, parts)
    put(parts, parts_hbm)
    gin_r = gres_low
    phase_input(sz, gb_ref, xr, gqkv, w_qkv, gin_r, sums)
    roll_rows(sz, back, lambda r: gin_r[r, :], lambda r, v: cr.__setitem__((r, slice(None)), v))
    put(cr, gin_hbm)
    for t in range(4):
        small_ref[t : t + 1, :] = jnp.sum(sums[t], axis=0, keepdims=True)
    for copy in stores:
        copy.wait()


def layer(x_in, cotangent, lengths, support, gains, w_qkv, w_out, w_up, w_down):
    rows, width = x_in.shape
    ffn = w_up.shape[1]
    sz, layout = Shapes(rows, width, ffn), Layout(width, ffn)
    part_rows = layout.flat_rows * DEVICES
    anywhere = pl.BlockSpec(memory_space=pl.ANY)
    vmem = pl.BlockSpec(memory_space=pltpu.VMEM)
    smem = pl.BlockSpec(memory_space=pltpu.SMEM)

    def low(*shape):
        return pltpu.VMEM(shape, BF16)

    scratch = [
        low(rows, width), low(rows, width), low(width, rows), low(width, rows), low(width, rows),
        low(rows, 3 * width),
        low(sz.heads, sz.big_keys, sz.big), low(sz.heads, sz.small, sz.small),
        low(rows, width), low(width, rows), low(rows, ffn), low(rows, ffn),
        low(rows, width), low(sz.heads, rows, 2 * HEAD), low(part_rows, HEAD),
        low(rows, HEAD), low(rows, HEAD), pltpu.VMEM((sz.heads, 8, rows), F32), pltpu.VMEM((4, 8, width), F32),
        low(width, 3 * width), low(width, width), low(width, ffn), low(ffn, width),
        pltpu.SemaphoreType.DMA((6,)), pltpu.SemaphoreType.DMA((6,)),
    ]
    return pl.pallas_call(
        functools.partial(layer_kernel, sz, layout),
        out_shape=(
            jax.ShapeDtypeStruct((rows, width), BF16),
            jax.ShapeDtypeStruct((rows, width), BF16),
            jax.ShapeDtypeStruct((part_rows, HEAD), BF16),
            jax.ShapeDtypeStruct((4, width), F32),
        ),
        in_specs=[smem, smem, anywhere, anywhere, vmem, anywhere, anywhere, anywhere, anywhere],
        out_specs=[anywhere] * 3 + [vmem],
        scratch_shapes=scratch,
        compiler_params=pltpu.CompilerParams(vmem_limit_bytes=63 * 2**20),
    )(lengths, support, x_in, cotangent, gains, w_qkv, w_out, w_up, w_down)


def place():
    z, f = lax.axis_index("dp"), lax.axis_index("fsdp")
    core, across, up = f % 2, (f // 2) % 2, f // 4
    return z, f, f + 1 - 2 * core, f + 2 - 4 * across, f + 4 - 8 * up


def meet(partners, edge, has_edge):
    barrier = pltpu.get_barrier_semaphore()
    for who in partners:
        pl.semaphore_signal(barrier, inc=1, device_id=who, device_id_type=MESH)

    @pl.when(has_edge)
    def _():
        pl.semaphore_signal(barrier, inc=1, device_id=edge, device_id_type=MESH)

    pl.semaphore_wait(barrier, len(partners) + has_edge.astype(jnp.int32))


def shifted_rows(source, off, odd, count, first):
    low = source[pl.ds(off + first, count), :]
    high = source[pl.ds(off + first + 1, count), :]
    lane = lax.broadcasted_iota(jnp.int32, (count, HEAD), 1)
    turned = jnp.where(lane < HEAD // 2, pltpu.roll(low, HEAD // 2, 1), pltpu.roll(high, HEAD // 2, 1))
    return jnp.where(odd, turned, low)


class Gather:
    def __init__(self, layout, mats, gains, send_sem, recv_sem, gain_send, gain_recv):
        self.layout, self.mats, self.gains = layout, mats, gains
        self.send_sem, self.recv_sem, self.gain_send, self.gain_recv = send_sem, recv_sem, gain_send, gain_recv
        self.z, self.f, self.mate, self.fx, self.fy = place()
        self.fd = self.fx + self.fy - self.f
        self.sent = []

    def refs(self, pieces):
        return [self.mats[m].at[pl.ds(r, n), :] for m, r, n, _ in pieces]

    def send(self, z, f, target, slot, half=None):
        k = z * PLANE + f
        index = len(self.sent)
        self.sent.append((k, half))

        def go(pieces):
            for ref in self.refs(pieces if half is None else self.layout.halves(pieces)[half]):
                pltpu.make_async_remote_copy(
                    src_ref=ref, dst_ref=ref, send_sem=self.send_sem.at[index], recv_sem=self.recv_sem.at[slot],
                    device_id=target, device_id_type=MESH,
                ).start()

        self.layout.each_kind(k, go)
        if half != 1:

            @pl.when(k == 0)
            def _():
                pltpu.make_async_remote_copy(
                    src_ref=self.gains, dst_ref=self.gains, send_sem=self.gain_send.at[index], recv_sem=self.gain_recv,
                    device_id=target, device_id_type=MESH,
                ).start()

    def dummy(self, half):
        rows = self.layout.flat_rows // self.layout.blocks[0]
        return self.mats[0].at[pl.ds(0, rows if half is None else rows // 2), :]

    def wait(self, slot, half=None):
        ref = self.dummy(half)
        pltpu.make_async_copy(ref, ref, self.recv_sem.at[slot]).wait()

    def wait_gains(self, z, f):
        @pl.when(z * PLANE + f == 0)
        def _():
            pltpu.make_async_copy(self.gains, self.gains, self.gain_recv).wait()

    def slot(self, way, z):
        return way * LINE + z

    def start(self):
        z, f = self.z, self.f
        for t in (1, 2, 3):
            self.send(z, f, ((z + t) % LINE, f), self.slot(0, z))
        self.send(z, f, (z, self.fx), self.slot(1, z))
        self.send(z, f, (z, self.fy), self.slot(2, z))
        self.send(z, f, (z, self.mate), self.slot(5, z))

    def line(self, t):
        z, f = (self.z + t) % LINE, self.f
        self.wait(self.slot(0, z))
        self.wait_gains(z, f)
        self.send(z, f, (self.z, self.fx), self.slot(1, z))
        self.send(z, f, (self.z, self.fy), self.slot(2, z))
        self.send(z, f, (self.z, self.mate), self.slot(5, z))

    def corner(self, t):
        z = (self.z + t) % LINE
        self.wait(self.slot(1, z))
        self.wait_gains(z, self.fx)
        self.send(z, self.fx, (self.z, self.fy), self.slot(3, z), 0)
        self.send(z, self.fx, (self.z, self.mate), self.slot(6, z))
        self.wait(self.slot(2, z))
        self.wait_gains(z, self.fy)
        self.send(z, self.fy, (self.z, self.fx), self.slot(4, z), 1)
        self.send(z, self.fy, (self.z, self.mate), self.slot(7, z))

    def far(self, t):
        z = (self.z + t) % LINE
        self.wait(self.slot(3, z), 0)
        self.wait_gains(z, self.fd)
        self.send(z, self.fd, (self.z, self.mate), self.slot(8, z), 0)
        self.wait(self.slot(4, z), 1)
        self.send(z, self.fd, (self.z, self.mate), self.slot(9, z), 1)

    def mates(self):
        for t in range(LINE):
            z = (self.z + t) % LINE
            for w in (5, 6, 7):
                self.wait(self.slot(w, z))
            self.wait(self.slot(8, z), 0)
            self.wait(self.slot(9, z), 1)

        @pl.when(self.f % 2 == 1)
        def _():
            pltpu.make_async_copy(self.gains, self.gains, self.gain_recv).wait()

    def finish(self):
        for index, (k, half) in enumerate(self.sent):
            ref = self.dummy(half)
            pltpu.make_async_copy(ref, ref, self.send_sem.at[index]).wait()
            if half != 1:

                @pl.when(k == 0)
                def _():
                    pltpu.make_async_copy(self.gains, self.gains, self.gain_send.at[index]).wait()


GATHER_SENDS = 6 + 3 * 3 + 4 * 4 + 4 * 2
GATHER_SLOTS = 10 * LINE


def own_part(layout, k, chunk, edge, flat, gains, mats, edge_sems):
    rows, half = layout.flat_rows, HEAD // 2
    before = jnp.maximum(k - 1, 0)
    send = pltpu.make_async_remote_copy(
        src_ref=chunk.at[pl.ds(0, HALO), :], dst_ref=edge, send_sem=edge_sems.at[0], recv_sem=edge_sems.at[1],
        device_id=(before // PLANE, before % PLANE), device_id_type=MESH,
    )

    @pl.when(k > 0)
    def _():
        send.start()

    @pl.when(k == 0)
    def _():
        gains[...] = chunk[pl.ds(0, HALO), :].astype(BF16).astype(F32)

    @pl.when(k < DEVICES - 1)
    def _():
        send.wait_recv()

    lane = lax.broadcasted_iota(jnp.int32, (HALO, HEAD), 1)
    row = lax.broadcasted_iota(jnp.int32, (HALO, HEAD), 0)
    turned = pltpu.roll(edge[...], half, 1)
    last = jnp.broadcast_to(chunk[pl.ds(rows, 1), :], (HALO, HEAD))
    down = jnp.where(row == 0, last, pltpu.roll(turned, 1, 0))
    chunk[pl.ds(rows, HALO), :] = jnp.where(lane < half, down, turned)
    off, odd = (DEVICES - k) // 2, (DEVICES - k) % 2 == 1
    step = 96
    for i in range(0, rows, step):
        flat[pl.ds(i, step), :] = shifted_rows(chunk, off, odd, step, i)

    def put(pieces):
        for m, r, n, f in pieces:
            blocks = layout.blocks[m]
            for c in range(blocks):
                mats[m][pl.ds(r, n), c * HEAD : (c + 1) * HEAD] = flat[pl.ds(f + c, n, stride=blocks), :].astype(BF16)

    layout.each_kind(k, put)

    @pl.when(k > 0)
    def _():
        send.wait_send()


def gather_kernel(layout, shard, w_qkv, w_out, w_up, w_down, gains_out, chunk, edge, flat, gains, send_sem, recv_sem, gain_send, gain_recv, edge_sems, load_sem):
    load = pltpu.make_async_copy(shard, chunk.at[pl.ds(0, shard.shape[0]), :], load_sem)
    load.start()
    mats = (w_qkv, w_out, w_up, w_down)
    g = Gather(layout, mats, gains, send_sem, recv_sem, gain_send, gain_recv)
    z, f = g.z, g.f
    k = z * PLANE + f
    step = 1 - 2 * ((k + 1) % 2)
    edge_with = jnp.clip(k + step, 0, DEVICES - 1)
    meet(
        [((z + t) % LINE, f) for t in (1, 2, 3)] + [(z, g.mate), (z, g.fx), (z, g.fy)],
        (edge_with // PLANE, edge_with % PLANE), (k > 0) & (k < DEVICES - 1),
    )
    load.wait()
    own_part(layout, k, chunk, edge, flat, gains, mats, edge_sems)
    g.start()
    g.line(1)
    g.corner(0)
    g.line(2)
    g.corner(1)
    g.line(3)
    g.corner(2)
    g.corner(3)
    for t in range(LINE):
        g.far(t)
    g.mates()
    g.finish()
    for t in range(4):
        for c in range(layout.width // HEAD):
            gains_out[t : t + 1, c * HEAD : (c + 1) * HEAD] = gains[pl.ds(t * (layout.width // HEAD) + c, 1), :]


def padded_rows(values):
    rows = -(-values.shape[0] // 1024) * 8
    return jnp.pad(values, (0, rows * HEAD - values.shape[0])).reshape(rows, HEAD)


def gather(layout, master):
    width, ffn = layout.width, layout.ffn
    vmem = pl.BlockSpec(memory_space=pltpu.VMEM)
    rows = layout.flat_rows
    dma = pltpu.SemaphoreType.DMA
    return pl.pallas_call(
        functools.partial(gather_kernel, layout),
        out_shape=(
            jax.ShapeDtypeStruct((width, 3 * width), BF16),
            jax.ShapeDtypeStruct((width, width), BF16),
            jax.ShapeDtypeStruct((width, ffn), BF16),
            jax.ShapeDtypeStruct((ffn, width), BF16),
            jax.ShapeDtypeStruct((4, width), F32),
        ),
        in_specs=[pl.BlockSpec(memory_space=pl.ANY)],
        out_specs=[vmem] * 5,
        scratch_shapes=[
            pltpu.VMEM((rows + 3 * HALO, HEAD), F32), pltpu.VMEM((HALO, HEAD), F32), pltpu.VMEM((rows, HEAD), F32),
            pltpu.VMEM((HALO, HEAD), F32), dma((GATHER_SENDS,)), dma((GATHER_SLOTS,)), dma((GATHER_SENDS,)), dma,
            dma((2,)), dma,
        ],
        compiler_params=pltpu.CompilerParams(collective_id=0, has_side_effects=True, vmem_limit_bytes=40 * 2**20),
    )(padded_rows(master))


class Scatter:
    def __init__(self, layout, parts, held, mate_in, corner_in, side_in, line_in, small, small_in, send_sem, recv_sem, load_sem):
        self.layout, self.parts, self.held, self.mate_in, self.corner_in = layout, parts, held, mate_in, corner_in
        self.side_in, self.line_in, self.small, self.small_in = side_in, line_in, small, small_in
        self.send_sem, self.recv_sem, self.load_sem = send_sem, recv_sem, load_sem
        self.z, self.f, self.mate, self.fx, self.fy = place()
        self.fd = self.fx + self.fy - self.f
        self.ways = [self.f, self.fx, self.fy, self.fd]
        self.flip = self.mate - self.f
        self.sent = []

    def copy(self, src, dst, slot, target):
        index = len(self.sent)
        self.sent.append(src)
        pltpu.make_async_remote_copy(
            src_ref=src, dst_ref=dst, send_sem=self.send_sem.at[index], recv_sem=self.recv_sem.at[slot],
            device_id=target, device_id_type=MESH,
        ).start()

    def wait(self, ref, slot):
        pltpu.make_async_copy(ref, ref, self.recv_sem.at[slot]).wait()

    def part(self, k):
        rows = self.layout.flat_rows
        return self.parts.at[pl.ds(pl.multiple_of(k * rows, rows), rows), :]

    def line_at(self, t):
        return (self.z + t) % LINE

    def slot(self, way, z):
        return way * LINE + z

    def share(self, way, t):
        z = self.line_at(t)
        s = self.slot(way, z)
        self.copy(self.part(z * PLANE + self.ways[way] + self.flip), self.mate_in.at[s], s, (self.z, self.mate))
        pltpu.make_async_copy(self.part(z * PLANE + self.ways[way]), self.held.at[s], self.load_sem.at[s]).start()

    def add(self, into, *terms, lo=0, hi=None):
        rows = self.layout.flat_rows if hi is None else hi
        step = 128

        def body(i, carry):
            here = pl.ds(pl.multiple_of(lo + i * step, step), step)
            total = into[here, :].astype(F32)
            for ref, base in terms:
                total = total + ref[pl.ds(pl.multiple_of(lo - base + i * step, step), step), :].astype(F32)
            into[here, :] = total.astype(BF16)
            return carry

        lax.fori_loop(0, (rows - lo) // step, body, 0)

    def mated(self, way, t):
        s = self.slot(way, self.line_at(t))
        self.wait(self.mate_in.at[s], s)
        pltpu.make_async_copy(self.held.at[s], self.held.at[s], self.load_sem.at[s]).wait()
        return s

    def corner(self, t):
        z, half = self.line_at(t), self.layout.flat_rows // 2
        s = self.mated(3, t)
        self.add(self.held.at[s], (self.mate_in.at[s], 0))
        held = self.held.at[s]
        self.copy(held.at[pl.ds(0, half), :], self.corner_in.at[z, 0], 16 + z, (self.z, self.fx))
        self.copy(held.at[pl.ds(half, half), :], self.corner_in.at[z, 1], 20 + z, (self.z, self.fy))

    def side(self, t):
        z, half = self.line_at(t), self.layout.flat_rows // 2
        for way, cut, slot, target in ((2, 0, 16, self.fy), (1, 1, 20, self.fx)):
            s = self.mated(way, t)
            held, mate_in = self.held.at[s], self.mate_in.at[s]
            other = half * (1 - cut)
            self.add(held, (mate_in, 0), lo=other, hi=other + half)
            self.wait(self.corner_in.at[z, cut], slot + z)
            self.add(held, (mate_in, 0), (self.corner_in.at[z, cut], half * cut), lo=half * cut, hi=half * cut + half)
            self.copy(held, self.side_in.at[z, way - 1], 24 + 4 * (way - 1) + z, (self.z, target))

    def line(self, t):
        z = self.line_at(t)
        s = self.mated(0, t)
        for way in (1, 2):
            self.wait(self.side_in.at[z, way - 1], 24 + 4 * (way - 1) + z)
        if t:
            self.add(self.held.at[s], (self.mate_in.at[s], 0), (self.side_in.at[z, 0], 0), (self.side_in.at[z, 1], 0))
            self.copy(self.held.at[s], self.line_in.at[self.z], 32 + self.z, (z, self.f))

    def total(self, out):
        z, s, step = self.z, self.slot(0, self.z), 128
        for t in (1, 2, 3):
            self.wait(self.line_in.at[self.line_at(t)], 32 + self.line_at(t))
        refs = [self.held.at[s], self.mate_in.at[s], self.side_in.at[z, 0], self.side_in.at[z, 1]]
        refs += [self.line_in.at[self.line_at(t)] for t in (1, 2, 3)]

        def body(i, carry):
            here = pl.ds(pl.multiple_of(i * step, step), step)
            total = refs[0][here, :].astype(F32)
            for ref in refs[1:]:
                total = total + ref[here, :].astype(F32)
            out[here, :] = total
            return carry

        lax.fori_loop(0, self.layout.flat_rows // step, body, 0)

    def small_send(self, stage):
        if stage < 3:
            target = (self.z, (self.mate, self.fx, self.fy)[stage])
            self.copy(self.small.at[stage], self.small_in.at[stage], 36 + stage, target)
        else:
            for t in (1, 2, 3):
                self.copy(self.small.at[3], self.small_in.at[3 + self.z], 39 + self.z, (self.line_at(t), self.f))

    def small_add(self, stage):
        if stage < 3:
            self.wait(self.small_in.at[stage], 36 + stage)
            self.small[stage + 1] = self.small[stage] + self.small_in[stage]
        else:
            for t in (1, 2, 3):
                self.wait(self.small_in.at[3 + self.line_at(t)], 39 + self.line_at(t))
            self.small_in[pl.ds(3 + self.z, 1)] = self.small[pl.ds(3, 1)]
            self.small[4] = (self.small_in[3] + self.small_in[4]) + (self.small_in[5] + self.small_in[6])

    def finish(self):
        for index, src in enumerate(self.sent):
            pltpu.make_async_copy(src, src, self.send_sem.at[index]).wait()


SCATTER_SENDS = 16 + 8 + 8 + 3 + 6
SCATTER_SLOTS = 39 + LINE


def own_rows(layout, k, total, small, flat, edge, out, edge_sems):
    rows = layout.flat_rows

    def put(pieces):
        for m, _, n, f in pieces:
            blocks = layout.blocks[m]
            for c in range(blocks):
                flat[pl.ds(HALO + f + c, n, stride=blocks), :] = total[pl.ds(f + c * n, n), :]

    layout.each_kind(k, put)
    after = jnp.minimum(k + 1, DEVICES - 1)
    send = pltpu.make_async_remote_copy(
        src_ref=flat.at[pl.ds(rows, HALO), :], dst_ref=edge, send_sem=edge_sems.at[0], recv_sem=edge_sems.at[1],
        device_id=(after // PLANE, after % PLANE), device_id_type=MESH,
    )

    @pl.when(k < DEVICES - 1)
    def _():
        send.start()

    @pl.when(k == 0)
    def _():
        across = layout.width // HEAD
        for t in range(4):
            for c in range(across):
                flat[t * across + c : t * across + c + 1, :] = small[t : t + 1, c * HEAD : (c + 1) * HEAD]

    @pl.when(k > 0)
    def _():
        send.wait_recv()
        flat[pl.ds(0, HALO), :] = edge[...]

    step = 8 * 97
    for i in range(0, out.shape[0], step):
        out[pl.ds(i, step), :] = shifted_rows(flat, k // 2, k % 2 == 1, step, i)

    @pl.when(k < DEVICES - 1)
    def _():
        send.wait_send()


def scatter_kernel(layout, parts, small_term, own_out, small_out, held, mate_in, corner_in, side_in, line_in, small, small_in, total, flat, edge, send_sem, recv_sem, load_sem, edge_sems):
    s = Scatter(layout, parts, held, mate_in, corner_in, side_in, line_in, small, small_in, send_sem, recv_sem, load_sem)
    z, f = s.z, s.f
    k = z * PLANE + f
    step = 1 - 2 * ((k + 1) % 2)
    edge_with = jnp.clip(k + step, 0, DEVICES - 1)
    meet(
        [(s.line_at(t), f) for t in (1, 2, 3)] + [(z, s.mate), (z, s.fx), (z, s.fy)],
        (edge_with // PLANE, edge_with % PLANE), (k > 0) & (k < DEVICES - 1),
    )
    small[0] = small_term[...]
    s.small_send(0)
    order = (1, 2, 3, 0)
    for way in (3, 2, 1, 0):
        for t in order:
            s.share(way, t)
    for t in order:
        s.corner(t)
    s.small_add(0)
    s.small_send(1)
    for t in order:
        s.side(t)
    s.small_add(1)
    s.small_send(2)
    s.small_add(2)
    s.small_send(3)
    for t in order:
        s.line(t)
    s.small_add(3)
    s.total(total)
    small_out[...] = small[4]
    own_rows(layout, k, total, small.at[4], flat, edge, own_out, edge_sems)
    s.finish()


def scatter(layout, parts, small):
    rows = layout.flat_rows
    vmem = pl.BlockSpec(memory_space=pltpu.VMEM)
    dma = pltpu.SemaphoreType.DMA
    width = layout.width
    return pl.pallas_call(
        functools.partial(scatter_kernel, layout),
        out_shape=(jax.ShapeDtypeStruct((rows + 8, HEAD), F32), jax.ShapeDtypeStruct((4, width), F32)),
        in_specs=[pl.BlockSpec(memory_space=pl.ANY), vmem],
        out_specs=[vmem] * 2,
        scratch_shapes=[
            pltpu.VMEM((16, rows, HEAD), BF16), pltpu.VMEM((16, rows, HEAD), BF16),
            pltpu.VMEM((LINE, 2, rows // 2, HEAD), BF16), pltpu.VMEM((LINE, 2, rows, HEAD), BF16),
            pltpu.VMEM((LINE, rows, HEAD), BF16), pltpu.VMEM((5, 4, width), F32), pltpu.VMEM((7, 4, width), F32),
            pltpu.VMEM((rows, HEAD), F32), pltpu.VMEM((rows + 2 * HALO, HEAD), F32), pltpu.VMEM((HALO, HEAD), F32),
            dma((SCATTER_SENDS,)), dma((SCATTER_SLOTS,)), dma((16,)), dma((2,)),
        ],
        compiler_params=pltpu.CompilerParams(collective_id=1, has_side_effects=True, vmem_limit_bytes=40 * 2**20),
    )(parts, small)


def adam(grads, first_moment, second_moment, master, step_count):
    step_float = step_count[0].astype(F32)
    new_first = BETA_ONE * first_moment + (1.0 - BETA_ONE) * grads
    new_second = BETA_TWO * second_moment + (1.0 - BETA_TWO) * grads * grads
    first_hat = new_first / (1.0 - jnp.power(F32(BETA_ONE), step_float))
    second_hat = new_second / (1.0 - jnp.power(F32(BETA_TWO), step_float))
    adam_step = first_hat / (jnp.sqrt(second_hat) + ADAM_EPS) + DECAY_RATE * master
    return new_first, new_second, adam_step


def flat_of_parts(layout, parts):
    by_part, flat = parts.reshape(DEVICES, layout.flat_rows, HEAD), []
    for k, own in enumerate(layout.pieces):
        for m, _, n, f in own:
            blocks = layout.blocks[m]
            piece = by_part[k, f : f + n * blocks].reshape(blocks, n, HEAD)
            flat.append(piece.transpose(1, 0, 2).reshape(-1))
    return jnp.concatenate(flat)


def plain_gather(layout, master):
    width, ffn = layout.width, layout.ffn
    flat = lax.all_gather(master.astype(BF16), ("dp", "fsdp"), axis=0, tiled=True)
    shapes = [(4, width), (width, 3 * width), (width, width), (width, ffn), (ffn, width)]
    arrays, start = [], 0
    for shape in shapes:
        arrays.append(flat[start : start + math.prod(shape)].reshape(shape))
        start += math.prod(shape)
    return (*arrays[1:], arrays[0].astype(F32))


def plain_scatter(layout, parts, small):
    axes = ("dp", "fsdp")
    local = jnp.concatenate([small.reshape(-1), flat_of_parts(layout, parts).astype(F32)])
    return lax.psum_scatter(local, axes, scatter_dimension=0, tiled=True), lax.psum(small[3], axes)


def per_device(sizes, x_in, cotangent, table_lengths, support_counts, master, first_moment, second_moment, step_count):
    width, shard = x_in.shape[1], master.shape[0]
    param_count = shard * sizes[0] * sizes[1]
    ffn = (param_count - 4 * width - 4 * width * width) // (2 * width)
    layout = Layout(width, ffn)
    own_kernels = layout.fits(param_count, sizes)
    *weights, gains = (gather if own_kernels else plain_gather)(layout, master)
    output, grad_input, parts, small = layer(x_in, cotangent, table_lengths, support_counts, gains, *weights)
    if own_kernels:
        rows, total = scatter(layout, parts, small)
        grads, bias_two_grad = rows.reshape(-1)[:shard], total[3]
    else:
        grads, bias_two_grad = plain_scatter(layout, parts, small)
    new_first, new_second, adam_step = adam(grads, first_moment, second_moment, master, step_count)
    return output, grad_input, grads, new_first, new_second, adam_step, bias_two_grad


def solution(mesh):
    rows, flat = P(("dp", "fsdp"), None), P(("dp", "fsdp"))
    return jax.shard_map(
        functools.partial(per_device, (mesh.shape["dp"], mesh.shape["fsdp"])),
        mesh=mesh,
        in_specs=(rows, rows, rows, rows, flat, flat, flat, P()),
        out_specs=(rows, rows, flat, flat, flat, flat, P()),
        check_vma=False,
    )
```

```python
import functools
import math

import jax
import jax.numpy as jnp
from jax import lax
from jax.experimental import pallas as pl
from jax.experimental.pallas import tpu as pltpu
from jax.sharding import PartitionSpec as P

HEAD = 128
EPS_NORM = 1e-05
BETA_ONE = 0.9
BETA_TWO = 0.999
ADAM_EPS = 1e-08
DECAY_RATE = 0.01
MASKED = -1e30
F32 = jnp.float32
BF16 = jnp.bfloat16
BLOCK = 256
TALL = 512
CUT = 128
GELU_ONE = math.sqrt(2.0 / math.pi)
GELU_THREE = 0.044715


def mm(left, right):
    return jnp.dot(left, right, preferred_element_type=F32)


def mm_t(left, right):
    return lax.dot_general(left, right, (((1,), (1,)), ((), ())), preferred_element_type=F32)


def rows_at(index, size=BLOCK):
    return pl.ds(pl.multiple_of(index * size, size), size)


class Shapes:
    def __init__(self, rows, width, ffn):
        self.rows, self.width, self.ffn = rows, width, ffn
        self.heads = width // HEAD
        self.big = 2 * rows // 3
        self.big_keys = 3 * self.big // 4
        self.small = rows - self.big


MESH = pl.DeviceIdType.MESH
LINE = 4
PLANE = 8
DEVICES = LINE * PLANE
HALO = 16
PIECES = 4


class Layout:
    def __init__(self, width, ffn):
        self.width, self.ffn = width, ffn
        shapes = [(width, 3 * width), (width, width), (width, ffn), (ffn, width)]
        self.blocks = [s[1] // HEAD for s in shapes]
        self.flat_rows = sum(r * c for r, c in shapes) // (HEAD * DEVICES)
        ends, total = [], 0
        for r, c in shapes:
            total += r * c // HEAD
            ends.append(total)
        starts = [0] + ends[:-1]
        self.pieces = []
        for k in range(DEVICES):
            lo, hi, own = k * self.flat_rows, (k + 1) * self.flat_rows, []
            for m in range(4):
                a, b = max(lo, starts[m]), min(hi, ends[m])
                if a < b:
                    own.append((m, (a - starts[m]) // self.blocks[m], (b - a) // self.blocks[m], a - lo))
            self.pieces.append(own)
        self.unit = math.gcd(*(n for own in self.pieces for m, _, n, _ in own if m == 3))
        self.kinds = []
        for k, own in enumerate(self.pieces):
            last = self.kinds[-1] if self.kinds else None
            if last and len(own) == 1 and self.same(self.pieces[last[0]], own):
                last[1] = k + 1
            else:
                self.kinds.append([k, k + 1])

    @staticmethod
    def same(left, right):
        return len(left) == len(right) and all(a[0] == b[0] and a[2:] == b[2:] for a, b in zip(left, right))

    def fits(self, param_count, devices):
        whole = self.flat_rows * HEAD * DEVICES + 4 * self.width
        first = all(len(own) == 1 and own[0][0] == 0 and own[0][2] % (8 * PIECES) == 0 for own in self.pieces[:PLANE])
        exact = all(
            sum(p[2] * self.blocks[p[0]] for p in own) == self.flat_rows and all(p[1] % 8 == 0 and p[2] % 8 == 0 for p in own)
            for own in self.pieces
        )
        return devices == (LINE, PLANE) and exact and first and whole == param_count and 4 * self.width == HALO * HEAD

    def each_kind(self, k, act):
        for lo, hi in self.kinds:
            def run(lo=lo, hi=hi):
                first = self.pieces[lo]
                if hi - lo == 1:
                    act(first)
                else:
                    m, r, n, f = first[0]
                    act([(m, pl.multiple_of(r + (k - lo) * n, 8), n, f)])

            pl.when((k >= lo) & (k < hi))(run)

    def halves(self, pieces):
        goal, done, parts = self.flat_rows // 2, 0, ([], [])
        for m, r, n, f in pieces:
            take = min(n, max(0, (goal - done)) // self.blocks[m])
            if take:
                parts[0].append((m, r, take, f))
            if n - take:
                parts[1].append((m, r + take, n - take, f + take * self.blocks[m]))
            done += take * self.blocks[m]
        return parts


def table_facts(sz, len_ref, sup_ref):
    lengths = [len_ref[0, t] for t in range(4)]
    support = [sup_ref[0, t] for t in range(4)]
    starts = [jnp.int32(0), lengths[0], lengths[0] + lengths[1], lengths[0] + lengths[1] + lengths[2]]
    is_big = [lengths[t] == sz.big for t in range(4)]

    def pick(values):
        total = jnp.int32(0)
        for t in range(4):
            total = total + jnp.where(is_big[t], values[t], 0)
        return total

    shift = pick(starts)
    lens = [pick([lengths[(t + j) % 4] for t in range(4)]) for j in range(4)]
    sups = [pick([support[(t + j) % 4] for t in range(4)]) for j in range(4)]
    begins = [jnp.int32(0), lens[0], lens[0] + lens[1], lens[0] + lens[1] + lens[2]]
    return shift, begins, sups


def mask_features(sz, begins, sups, qm_ref, km_ref):
    def step(i, carry):
        shape = (BLOCK, HEAD)
        row = lax.broadcasted_iota(jnp.int32, shape, 0) + i * BLOCK
        lane = lax.broadcasted_iota(jnp.int32, shape, 1)
        table = jnp.zeros(shape, jnp.int32)
        limit = jnp.full(shape, begins[0] + sups[0], jnp.int32)
        for t in range(1, 4):
            inside = row >= begins[t]
            table = jnp.where(inside, t, table)
            limit = jnp.where(inside, begins[t] + sups[t], limit)
        own = table == lane
        qm_ref[rows_at(i), :] = jnp.where(own, 1.0, 0.0).astype(BF16)
        bad = jnp.where(own, jnp.where(row < limit, 0.0, MASKED), jnp.where(lane < 4, MASKED, 0.0))
        km_ref[rows_at(i), :] = bad.astype(BF16)
        return carry

    lax.fori_loop(0, sz.rows // BLOCK, step, 0, unroll=2)


def roll_rows(sz, shift, source, write):
    blocks = sz.rows // CUT
    coarse, fine = shift // CUT, shift % CUT
    row = lax.broadcasted_iota(jnp.int32, (CUT, 2 * CUT), 0)
    column = lax.broadcasted_iota(jnp.int32, (CUT, 2 * CUT), 1)
    chosen = jnp.where(row + fine == column, 1.0, 0.0).astype(BF16)

    def step(i, carry):
        here = lax.rem(i + coarse, blocks)
        after = lax.rem(i + coarse + 1, blocks)
        pair = jnp.concatenate([source[here], source[after]], axis=0)
        write(rows_at(i, CUT), mm(chosen, pair).astype(BF16))
        return carry

    lax.fori_loop(0, blocks, step, 0, unroll=4)


def normed(values):
    centre = values - jnp.mean(values, axis=-1, keepdims=True)
    inverse = lax.rsqrt(jnp.mean(centre * centre, axis=-1, keepdims=True) + EPS_NORM)
    return centre * inverse, inverse


def norm_back(grad_out, norm, inverse, gain):
    grad_normed = grad_out * gain
    return inverse * (
        grad_normed
        - jnp.mean(grad_normed, axis=-1, keepdims=True)
        - norm * jnp.mean(grad_normed * norm, axis=-1, keepdims=True)
    )


def eight_rows(values):
    rows, width = values.shape
    return jnp.sum(values.reshape(rows // 8, 8, width), axis=0)


def phase_qkv(sz, gb_ref, xr, act_cuts, w_qkv, qkv):
    gain, bias = gb_ref[0:1, :], gb_ref[1:2, :]

    def step(i, carry):
        norm, _ = normed(xr[rows_at(i), :].astype(F32))
        act = (norm * gain + bias).astype(BF16)
        cuts = BLOCK // CUT
        act_cuts[pl.ds(i * cuts, cuts)] = act.reshape(cuts, CUT, sz.width)
        qkv[rows_at(i), :] = mm(act, w_qkv[...]).astype(BF16)
        return carry

    lax.fori_loop(0, sz.rows // BLOCK, step, 0, unroll=2)


def head_at(head, offset=0):
    return pl.ds(pl.multiple_of(offset + head * HEAD, HEAD), HEAD)


def attend_forward(sz, base, key_count, query_count, exps, qkv, qm, km, ctx, ctx_t, inv_ref, hook=None):
    keep = pl.ds(base, key_count)
    here = pl.ds(base, query_count)
    scale = math.log2(math.e) / math.sqrt(HEAD)

    def per_head(head, carry):
        keys = jnp.concatenate([qkv[keep, head_at(head, sz.width)], km[keep, :]], axis=1)
        values_t = qkv[keep, head_at(head, 2 * sz.width)].T
        queries = jnp.concatenate([qkv[here, head_at(head)], qm[here, :]], axis=1)
        scores = mm_t(keys, queries)
        top = jnp.max(scores, axis=0, keepdims=True)
        shifted = jnp.exp2((scores - top) * scale)
        total = jnp.sum(shifted, axis=0, keepdims=True)
        low = shifted.astype(BF16)
        exps[head] = low
        inverse = 1.0 / total
        mixed = (mm(values_t, low) * inverse).astype(BF16)
        ctx_t[head_at(head), here] = mixed
        ctx[here, head_at(head)] = mixed.T
        inv_ref[head, :, here] = jnp.broadcast_to(inverse, (8, query_count))
        if hook:
            hook(head)
        return carry

    lax.fori_loop(0, sz.heads, per_head, 0)


def pool_at(sz, column, start, size):
    return pl.ds(pl.multiple_of(column * sz.rows + start, 256), size)


def phase_up(sz, gb_ref, xr, ctx, w_out, w_up, act_t, hid, pool, resid_ref):
    gain, bias = gb_ref[2:3, :], gb_ref[3:4, :]

    def step(i, carry):
        here = rows_at(i, TALL)
        resid = xr[here, :].astype(F32) + mm(ctx[here, :], w_out[...])
        resid_ref[here, :] = resid
        norm, _ = normed(resid)
        act = (norm * gain + bias).astype(BF16)
        act_t[:, here] = act.T
        for f in range(sz.ffn // BLOCK):
            part = slice(f * BLOCK, (f + 1) * BLOCK)
            pre = mm(act, w_up[:, part])
            square = pre * pre
            bent = jnp.tanh(pre * (GELU_ONE + GELU_ONE * GELU_THREE * square))
            half = 0.5 + 0.5 * bent
            value = pre * half
            hid[here, part] = value.astype(BF16)
            slope = half + value * (1.0 - half) * (2.0 * GELU_ONE + 6.0 * GELU_ONE * GELU_THREE * square)
            slope = slope.astype(BF16)
            for c in range(BLOCK // HEAD):
                pool[pool_at(sz, f * (BLOCK // HEAD) + c, i * TALL, TALL), :] = slope[:, c * HEAD : (c + 1) * HEAD]
        return carry

    lax.fori_loop(0, sz.rows // TALL, step, 0)


def phase_down(sz, gb_ref, cr, w_up, w_down, hid, pool, resid_ref, out_r, gres_low, sums, hook=None):
    gain = gb_ref[2:3, :]

    def step(i, carry):
        here = rows_at(i, TALL)
        cot = cr[here, :]
        resid = resid_ref[here, :]
        norm, inverse = normed(resid)
        grad_pre = []
        for f in range(sz.ffn // BLOCK):
            part = slice(f * BLOCK, (f + 1) * BLOCK)
            grad_hidden = mm_t(cot, w_down[part, :])
            for c in range(BLOCK // HEAD):
                at = pool_at(sz, f * (BLOCK // HEAD) + c, i * TALL, TALL)
                low = (grad_hidden[:, c * HEAD : (c + 1) * HEAD] * pool[at, :].astype(F32)).astype(BF16)
                pool[at, :] = low
                grad_pre.append(low)
        grad_act = mm_t(jnp.concatenate(grad_pre, axis=1), w_up[...])
        total = resid + mm(hid[here, :], w_down[...])
        cuts = TALL // CUT
        out_r[pl.ds(i * cuts, cuts)] = total.astype(BF16).reshape(cuts, CUT, sz.width)
        sums[2] += eight_rows(grad_act * norm)
        sums[3] += eight_rows(grad_act)
        low = (cot.astype(F32) + norm_back(grad_act, norm, inverse, gain)).astype(BF16)
        gres_low[here, :] = low
        if hook:
            hook(i)
        return carry

    lax.fori_loop(0, sz.rows // TALL, step, 0)


def phase_heads(sz, ctx, inv_ref, w_out, gres_low, dox, hook=None):
    def step(i, carry):
        here = rows_at(i, TALL)
        grad_ctx = mm_t(gres_low[here, :], w_out[...]).astype(BF16).astype(F32)
        lane = lax.broadcasted_iota(jnp.int32, (TALL, HEAD), 1)
        for head in range(sz.heads):
            part = slice(head * HEAD, (head + 1) * HEAD)
            column = inv_ref[head, :, here].T[:, 0:1]
            scaled = (grad_ctx[:, part] * column).astype(BF16)
            delta = jnp.sum(scaled.astype(F32) * ctx[here, part].astype(F32), axis=1, keepdims=True)
            high = delta.astype(BF16).astype(F32)
            rest = delta - high
            dox[head, here, 0:HEAD] = scaled
            dox[head, here, HEAD : 2 * HEAD] = jnp.where(lane == 0, -high, jnp.where(lane == 1, -rest, 0.0)).astype(BF16)
        if hook:
            hook(i)
        return carry

    lax.fori_loop(0, sz.rows // TALL, step, 0, unroll=3)


def weight_grad(layout, m, left_t, right, parts):
    rows, per = layout.flat_rows, BLOCK // HEAD

    def step(i, carry):
        product = mm(left_t[...], right(i)).astype(BF16)
        for k, own in enumerate(layout.pieces):
            for matrix, r, n, f in own:
                if matrix == m:
                    for c in range(per):
                        there = pl.multiple_of(k * rows + f + (i * per + c) * n, 16)
                        parts[pl.ds(there, n), :] = product[r : r + n, c * HEAD : (c + 1) * HEAD]
        return carry

    lax.fori_loop(0, layout.blocks[m] // per, step, 0, unroll=2)


def weight_grad_turned(layout, m, left_t, right, parts):
    rows, unit = layout.flat_rows, layout.unit
    first_k, first = next((k, p) for k, own in enumerate(layout.pieces) for p in own if p[0] == m)
    later = layout.pieces[first_k + 1][-1][2]

    def step(i, carry):
        product = mm(left_t[...], right(i)).astype(BF16).T
        for q in range(BLOCK // unit):
            r = i * BLOCK + q * unit
            head = r < first[2]
            n = jnp.where(head, first[2], later)
            k = jnp.where(head, first_k, first_k + 1 + (r - first[2]) // later)
            base = jnp.where(head, first[3] + r, (r - first[2]) % later)
            for c in range(layout.blocks[m]):
                there = pl.multiple_of(k * rows + base + c * n, 16)
                parts[pl.ds(there, unit), :] = product[q * unit : (q + 1) * unit, c * HEAD : (c + 1) * HEAD]
        return carry

    lax.fori_loop(0, layout.ffn // BLOCK, step, 0, unroll=2)


def attend_backward(sz, base, key_count, query_count, exps, qkv, dox, gqkv, hook=None):
    keep = pl.ds(base, key_count)
    asked = pl.ds(base, query_count)
    scale = 1.0 / math.sqrt(HEAD)
    lane = lax.broadcasted_iota(jnp.int32, (key_count, HEAD), 1)
    ones = jnp.where(lane < 2, 1.0, 0.0).astype(BF16)

    def per_head(head, carry):
        values = jnp.concatenate([qkv[keep, head_at(head, 2 * sz.width)], ones], axis=1)
        keys_t = qkv[keep, head_at(head, sz.width)].T
        gqkv[keep, head_at(head, 2 * sz.width)] = mm(exps[head], dox[head, asked, 0:HEAD]).astype(BF16)
        for j in range(query_count // TALL):
            here = pl.ds(base + j * TALL, TALL)
            columns = pl.ds(j * TALL, TALL)
            grad_probs = mm_t(values, dox[head, here, :])
            grad_scores = (exps[head, :, columns].astype(F32) * grad_probs).astype(BF16)
            exps[head, :, columns] = grad_scores
            gqkv[here, head_at(head)] = (mm(keys_t, grad_scores) * scale).astype(BF16).T
        gqkv[keep, head_at(head, sz.width)] = (mm(exps[head], qkv[asked, head_at(head)]) * scale).astype(BF16)
        if hook:
            hook(head)
        return carry

    lax.fori_loop(0, sz.heads, per_head, 0)


def phase_input(sz, gb_ref, xr, gqkv, w_qkv, gres_low, gin_r, sums, hook=None):
    gain = gb_ref[0:1, :]

    def step(i, carry):
        for j in range(2):
            here = rows_at(2 * i + j)
            grad_act = mm_t(gqkv[here, 0 : 3 * sz.width], w_qkv[...])
            norm, inverse = normed(xr[here, :].astype(F32))
            sums[0] += eight_rows(grad_act * norm)
            sums[1] += eight_rows(grad_act)
            grad = (gres_low[here, :].astype(F32) + norm_back(grad_act, norm, inverse, gain)).astype(BF16)
            cuts = BLOCK // CUT
            gin_r[pl.ds((2 * i + j) * cuts, cuts)] = grad.reshape(cuts, CUT, sz.width)
        if hook:
            hook(i)
        return carry

    lax.fori_loop(0, sz.rows // (2 * BLOCK), step, 0)


def place():
    z, f = lax.axis_index("dp"), lax.axis_index("fsdp")
    core, across, up = f % 2, (f // 2) % 2, f // 4
    return z, f, f + 1 - 2 * core, f + 2 - 4 * across, f + 4 - 8 * up


def shifted_rows(source, off, odd, count, first):
    low = source[pl.ds(off + first, count), :]
    high = source[pl.ds(off + first + 1, count), :]
    lane = lax.broadcasted_iota(jnp.int32, (count, HEAD), 1)
    turned = jnp.where(lane < HEAD // 2, pltpu.roll(low, HEAD // 2, 1), pltpu.roll(high, HEAD // 2, 1))
    return jnp.where(odd, turned, low)


class Link:
    def __init__(self, layout, send_sem, recv_sem):
        self.layout, self.send_sem, self.recv_sem = layout, send_sem, recv_sem
        self.z, self.f, self.mate, self.fx, self.fy = place()
        self.fd = self.fx + self.fy - self.f
        self.ways = [self.f, self.fx, self.fy, self.fd]
        self.k = self.z * PLANE + self.f
        self.sent, self.finished, self.slots = [], 0, 0

    def new_slots(self, count):
        self.slots += count
        return self.slots - count

    def new_send(self, ref, condition=None):
        self.sent.append((ref, condition))
        return len(self.sent) - 1

    def start(self, src, dst, index, slot, target):
        pltpu.make_async_remote_copy(
            src_ref=src, dst_ref=dst, send_sem=self.send_sem.at[index], recv_sem=self.recv_sem.at[slot],
            device_id=target, device_id_type=MESH,
        ).start()

    def copy(self, src, dst, slot, target, like, condition=None):
        index = self.new_send(like, condition)
        self.when(condition, lambda: self.start(src, dst, index, slot, target))

    def wait(self, ref, slot, condition=None):
        self.when(condition, lambda: pltpu.make_async_copy(ref, ref, self.recv_sem.at[slot]).wait())

    @staticmethod
    def when(condition, act):
        if condition is None:
            act()
        else:
            pl.when(condition())(act)

    def finish(self):
        for index in range(self.finished, len(self.sent)):
            ref, condition = self.sent[index]
            self.when(condition, lambda: pltpu.make_async_copy(ref, ref, self.send_sem.at[index]).wait())
        self.finished = len(self.sent)

    def meet(self):
        step = 1 - 2 * ((self.k + 1) % 2)
        edge = jnp.clip(self.k + step, 0, DEVICES - 1)
        has_edge = (self.k > 0) & (self.k < DEVICES - 1)
        barrier = pltpu.get_barrier_semaphore()
        partners = [((self.z + t) % LINE, self.f) for t in (1, 2, 3)]
        partners += [(self.z, self.mate), (self.z, self.fx), (self.z, self.fy)]
        for who in partners:
            pl.semaphore_signal(barrier, inc=1, device_id=who, device_id_type=MESH)

        @pl.when(has_edge)
        def _():
            pl.semaphore_signal(barrier, inc=1, device_id=(edge // PLANE, edge % PLANE), device_id_type=MESH)

        pl.semaphore_wait(barrier, len(partners) + has_edge.astype(jnp.int32))

    def tell(self, sem):
        for who in (self.mate, self.fx, self.fy):
            pl.semaphore_signal(sem, inc=1, device_id=(self.z, who), device_id_type=MESH)

        @pl.when(self.z % 2 == 0)
        def _():
            sender = jnp.where(self.z == 0, 2, 3)
            pl.semaphore_signal(sem, inc=1, device_id=(sender, self.f), device_id_type=MESH)

        @pl.when(self.z == 2)
        def _():
            pl.semaphore_signal(sem, inc=1, device_id=(1, self.f), device_id_type=MESH)

    def told(self, sem):
        pl.semaphore_wait(sem, 3 + (self.z > 0).astype(jnp.int32))


class Gather:
    def __init__(self, link, mats, gains, gain_send, gain_recv):
        self.link, self.layout, self.mats, self.gains = link, link.layout, mats, gains
        self.gain_send, self.gain_recv, self.gain_sent = gain_send, gain_recv, []
        self.first = link.new_slots(5 * PIECES)
        self.later = {s: link.new_slots(9) for s in range(1, LINE)}

    def is_first(self, way, condition):
        first = self.link.ways[way] == 0
        return first if condition is None else first & condition()

    def send_gains(self, way, target, condition=None):
        index = len(self.gain_sent)
        self.gain_sent.append((way, condition))

        @pl.when(self.is_first(way, condition))
        def _():
            pltpu.make_async_remote_copy(
                src_ref=self.gains, dst_ref=self.gains, send_sem=self.gain_send.at[index], recv_sem=self.gain_recv,
                device_id=target, device_id_type=MESH,
            ).start()

    def wait_gains(self, way, condition=None):
        pl.when(self.is_first(way, condition))(lambda: pltpu.make_async_copy(self.gains, self.gains, self.gain_recv).wait())

    def piece(self, f, p):
        n = self.layout.pieces[0][0][2] // PIECES
        return self.mats[0].at[pl.ds(pl.multiple_of(f * (n * PIECES) + p * n, 8), n), :]

    def send_piece(self, of, p, way, target, condition=None):
        ref = self.piece(self.link.ways[of], p)
        self.link.copy(ref, ref, self.first + way * PIECES + p, target, self.piece(0, 0), condition)
        if p == 0:
            self.send_gains(of, target, condition)

    def wait_piece(self, of, p, way, condition=None):
        self.link.wait(self.piece(0, 0), self.first + way * PIECES + p, condition)
        if p == 0:
            self.wait_gains(of, condition)

    def along(self, p):
        link = self.link
        self.wait_piece(0, p, 0, lambda: link.z > 0)
        self.send_piece(0, p, 0, (jnp.minimum(link.z + 1, LINE - 1), link.f), lambda: link.z < LINE - 1)
        self.send_piece(0, p, 1, (link.z, link.fx))
        self.send_piece(0, p, 2, (link.z, link.fy))

    def across(self, p):
        link = self.link
        self.wait_piece(1, p, 1)
        if p < PIECES // 2:
            self.send_piece(1, p, 3, (link.z, link.fy))
        self.wait_piece(2, p, 2)
        if p >= PIECES // 2:
            self.send_piece(2, p, 3, (link.z, link.fx))

    def whole(self, f):
        n = self.layout.pieces[0][0][2]
        return self.mats[0].at[pl.ds(pl.multiple_of(f * n, 16), n), :]

    def first_to_mate(self, way):
        link = self.link
        if way == 3:
            for p in range(PIECES):
                self.wait_piece(3, p, 3)
        ref = self.whole(link.ways[way])
        link.copy(ref, ref, self.first + 4 * PIECES + way, (link.z, link.mate), self.whole(0))
        self.send_gains(way, (link.z, link.mate))

    def first_from_mate(self):
        for way in range(4):
            self.link.wait(self.whole(0), self.first + 4 * PIECES + way)
        pl.when(self.link.f % 2 == 1)(lambda: pltpu.make_async_copy(self.gains, self.gains, self.gain_recv).wait())

    def some(self, s, f, half):
        rows = self.layout.flat_rows // self.layout.blocks[0]
        return self.mats[0].at[pl.ds(0, rows if half is None else rows // 2), :]

    def send_part(self, s, f, slot, target, half=None, condition=None):
        link = self.link
        index = link.new_send(self.some(s, f, half), condition)

        def go(pieces):
            for m, r, n, _ in pieces if half is None else self.layout.halves(pieces)[half]:
                ref = self.mats[m].at[pl.ds(r, n), :]
                link.start(ref, ref, index, self.slot_of(s, slot), target)

        link.when(condition, lambda: self.layout.each_kind(s * PLANE + f, go))

    def slot_of(self, s, slot):
        return self.later[1] + (s - 1) * 9 + slot

    def wait_part(self, s, slot, half=None, condition=None):
        self.link.wait(self.some(s, 0, half), self.slot_of(s, slot), condition)

    def over_links(self, s, condition=None):
        link = self.link
        self.send_part(s, link.f, 1, (link.z, link.fx), None, condition)
        self.send_part(s, link.f, 2, (link.z, link.fy), None, condition)
        self.send_part(s, link.f, 5, (link.z, link.mate), None, condition)

    def start_later(self):
        link = self.link
        self.over_links(link.z, lambda: link.z > 0)
        for t in (1, 2, 3):
            target = jnp.maximum(link.z - t, 0)
            self.send_part(link.z, link.f, 0, (target, link.f), None, lambda t=t: link.z >= jnp.maximum(t, 1))

    def start_upward(self):
        link = self.link
        for t in (1, 2):
            target = jnp.minimum(link.z + t, LINE - 1)
            self.send_part(link.z, link.f, 0, (target, link.f), None, lambda t=t: (link.z > 0) & (link.z + t < LINE))

    def line(self, s):

        def elsewhere():
            return self.link.z != s

        self.wait_part(s, 0, None, elsewhere)
        self.over_links(s, elsewhere)

    def corner(self, s):
        link = self.link
        self.wait_part(s, 1)
        self.send_part(s, link.fx, 3, (link.z, link.fy), 0)
        self.send_part(s, link.fx, 6, (link.z, link.mate))
        self.wait_part(s, 2)
        self.send_part(s, link.fy, 4, (link.z, link.fx), 1)
        self.send_part(s, link.fy, 7, (link.z, link.mate))

    def far(self, s):
        link = self.link
        self.wait_part(s, 3, 0)
        self.wait_part(s, 4, 1)
        self.send_part(s, link.fd, 8, (link.z, link.mate))

    def mates(self, s):
        for slot in (5, 6, 7, 8):
            self.wait_part(s, slot)

    def finish(self):
        for index, (way, condition) in enumerate(self.gain_sent):
            pl.when(self.is_first(way, condition))(lambda: pltpu.make_async_copy(self.gains, self.gains, self.gain_send.at[index]).wait())


class Scatter:
    def __init__(self, link, parts, room, line_in, chain_in, small, small_in):
        self.link, self.layout, self.parts, self.room, self.line_in = link, link.layout, parts, room, line_in
        self.chain_in, self.small, self.small_in = chain_in, small, small_in
        self.flip = link.mate - link.f
        self.slot = {s: link.new_slots(8) for s in range(LINE)}
        self.line_slot, self.tail_slot, self.small_slot = link.new_slots(LINE), link.new_slots(6 * PIECES), link.new_slots(3 + LINE)
        self.piece_rows = self.layout.flat_rows // PIECES

    def part(self, s, f):
        rows = self.layout.flat_rows
        return self.parts.at[pl.ds(pl.multiple_of((s * PLANE + f) * rows, rows), rows), :]

    def like(self, size=None):
        return self.parts.at[pl.ds(0, self.layout.flat_rows if size is None else size), :]

    def buffer(self, s, index, lo=0, size=None):
        rows = self.layout.flat_rows
        ref, base = self.room(s)
        return ref.at[pl.ds(base + index * rows + lo, rows if size is None else size), :]

    def line_buffer(self, z, lo=0, size=None):
        rows = self.layout.flat_rows
        ref, base = self.line_in
        return ref.at[pl.ds(pl.multiple_of(base + z * rows + lo, 16), rows if size is None else size), :]

    def chain_buffer(self, index):
        ref, base = self.chain_in
        rows = self.layout.flat_rows
        return ref.at[pl.ds(base + index * rows, rows), :]

    def share(self, s):
        link = self.link
        for way in (3, 2, 1, 0):
            link.copy(self.part(s, link.ways[way] + self.flip), self.buffer(s, way), self.slot[s] + way, (link.z, link.mate), self.like())

    def add(self, into, terms):
        step = 96

        def body(i, carry):
            here = pl.ds(pl.multiple_of(i * step, step), step)
            total = into[here, :].astype(F32)
            for ref in terms:
                total = total + ref[here, :].astype(F32)
            into[here, :] = total.astype(BF16)
            return carry

        lax.fori_loop(0, into.shape[0] // step, body, 0, unroll=2)

    def mated(self, s, way):
        self.link.wait(self.buffer(s, way), self.slot[s] + way)

    def corner(self, s):
        link, half = self.link, self.layout.flat_rows // 2
        self.mated(s, 3)
        own = self.part(s, link.fd)
        for cut, target in ((0, link.fx), (1, link.fy)):
            some = own.at[pl.ds(cut * half, half), :]
            self.add(some, [self.buffer(s, 3, cut * half, half)])
            link.copy(some, self.buffer(s, 4, cut * half, half), self.slot[s] + 4 + cut, (link.z, target), self.like(half))

    def side(self, s):
        link, half = self.link, self.layout.flat_rows // 2
        for way, cut, f, target in ((2, 0, link.fy, link.fy), (1, 1, link.fx, link.fx)):
            self.mated(s, way)
            own = self.part(s, f)
            for now in (1 - cut, cut):
                some = own.at[pl.ds(now * half, half), :]
                terms = [self.buffer(s, way, now * half, half)]
                if now == cut:
                    corner = self.buffer(s, 4, cut * half, half)
                    link.wait(corner, self.slot[s] + 4 + cut)
                    terms.append(corner)
                self.add(some, terms)
            link.copy(own, self.buffer(s, 4 + way), self.slot[s] + 5 + way, (link.z, target), self.like())

    def sided(self, s):
        link = self.link
        self.mated(s, 0)
        for way in (1, 2):
            link.wait(self.buffer(s, 4 + way), self.slot[s] + 5 + way)

    def line(self, s):
        link = self.link
        self.sided(s)
        own = self.part(s, link.f)

        @pl.when(link.z != s)
        def _():
            self.add(own, [self.buffer(s, 0), self.buffer(s, 5), self.buffer(s, 6)])

        link.copy(own, self.line_buffer(link.z), self.line_slot + link.z, (s, link.f), self.like(), lambda: link.z != s)

    def piece_of(self, ref, p):
        return ref.at[pl.ds(p * self.piece_rows, self.piece_rows), :]

    def pass_on(self, own, way, p, into, target, condition=None):
        like, slot = self.like(self.piece_rows), self.tail_slot + way * PIECES + p
        self.link.copy(self.piece_of(own, p), self.piece_of(into, p), slot, target, like, condition)

    def passed(self, way, p):
        self.link.wait(self.like(self.piece_rows), self.tail_slot + way * PIECES + p)

    def add_piece(self, own, p, others):
        self.add(self.piece_of(own, p), [self.piece_of(ref, p) for ref in others])

    def tail_corner(self):
        link, half = self.link, PIECES // 2
        self.mated(0, 3)
        own = self.part(0, link.fd)
        for p in range(PIECES):
            self.add_piece(own, p, [self.buffer(0, 3)])
            self.pass_on(own, 0, p, self.buffer(0, 4), (link.z, link.fx if p < half else link.fy))
        for way, pieces, f in ((2, range(half, PIECES), link.fy), (1, range(half), link.fx)):
            self.mated(0, way)
            own = self.part(0, f)
            for p in pieces:
                self.add_piece(own, p, [self.buffer(0, way)])
                self.pass_on(own, way, p, self.buffer(0, 4 + way), (link.z, f))

    def tail_side(self):
        link, half = self.link, PIECES // 2
        for j in range(half):
            for way, p, f in ((2, j, link.fy), (1, half + j, link.fx)):
                own = self.part(0, f)
                self.passed(0, p)
                self.add_piece(own, p, [self.buffer(0, way), self.buffer(0, 4)])
                self.pass_on(own, way, p, self.buffer(0, 4 + way), (link.z, f))

    def tail_sum(self, p, others=()):
        self.passed(1, p)
        self.passed(2, p)
        own = self.part(0, self.link.f)
        self.add_piece(own, p, [self.buffer(0, 0), self.buffer(0, 5), self.buffer(0, 6), *others])


    ORDER = tuple(p for j in range(PIECES // 2) for p in (j, j + PIECES // 2))

    def leaf(self):
        link = self.link
        self.mated(0, 0)
        for p in self.ORDER:
            pl.when(link.z % 2 == 1)(lambda: self.tail_sum(p))
            own, target = self.part(0, link.f), (2, link.f)
            self.pass_on(own, 3, p, self.chain_buffer(0), target, lambda: link.z == 1)
            self.pass_on(own, 4, p, self.chain_buffer(1), target, lambda: link.z == 3)

    def middle(self):
        link = self.link
        for p in self.ORDER:

            @pl.when(link.z == 2)
            def _():
                self.passed(3, p)
                self.passed(4, p)
                self.tail_sum(p, (self.chain_buffer(0), self.chain_buffer(1)))

            self.pass_on(self.part(0, link.f), 5, p, self.chain_buffer(0), (0, link.f), lambda: link.z == 2)

    def total(self, out):
        link, rows, step = self.link, self.layout.flat_rows, 96

        def sum_of(refs):
            def body(i, carry):
                here = pl.ds(pl.multiple_of(i * step, step), step)
                total = refs[0][here, :].astype(F32)
                for ref in refs[1:]:
                    total = total + ref[here, :].astype(F32)
                out[here, :] = total
                return carry

            lax.fori_loop(0, rows // step, body, 0, unroll=2)

        for s in range(LINE):
            refs = [self.part(s, link.f), self.buffer(s, 0), self.buffer(s, 5), self.buffer(s, 6)]
            if s == 0:
                refs.append(self.chain_buffer(0))
            else:
                refs += [self.line_buffer(z) for z in range(LINE) if z != s]

            @pl.when(link.z == s)
            def _():
                for z in range(LINE):
                    if s and z != s:
                        link.wait(self.line_buffer(z), self.line_slot + z)
                if s == 0:
                    for p in self.ORDER:
                        for way in (1, 2, 5):
                            self.passed(way, p)
                sum_of(refs)

    def small_send(self, stage):
        link = self.link
        if stage < 3:
            target = (link.z, (link.mate, link.fx, link.fy)[stage])
            link.copy(self.small.at[stage], self.small_in.at[stage], self.small_slot + stage, target, self.small.at[0])
        else:
            for t in (1, 2, 3):
                target = ((link.z + t) % LINE, link.f)
                link.copy(self.small.at[3], self.small_in.at[3 + link.z], self.small_slot + 3 + link.z, target, self.small.at[0])

    def small_add(self, stage):
        link = self.link
        if stage < 3:
            link.wait(self.small_in.at[stage], self.small_slot + stage)
            self.small[stage + 1] = self.small[stage] + self.small_in[stage]
        else:
            for t in (1, 2, 3):
                z = (link.z + t) % LINE
                link.wait(self.small_in.at[3 + z], self.small_slot + 3 + z)
            self.small_in[pl.ds(3 + link.z, 1)] = self.small[pl.ds(3, 1)]
            self.small[4] = (self.small_in[3] + self.small_in[4]) + (self.small_in[5] + self.small_in[6])


def edge_copy(layout, k, shard, edge, edge_sems):
    before = jnp.maximum(k - 1, 0)
    return pltpu.make_async_remote_copy(
        src_ref=shard.at[pl.ds(0, HALO), :], dst_ref=edge, send_sem=edge_sems.at[0], recv_sem=edge_sems.at[1],
        device_id=(before // PLANE, before % PLANE), device_id_type=MESH,
    )


def own_part(layout, k, chunk, edge, flat, mats, send):
    rows, half = layout.flat_rows, HEAD // 2
    pl.when(k < DEVICES - 1)(lambda: send.wait_recv())
    lane = lax.broadcasted_iota(jnp.int32, (HALO, HEAD), 1)
    row = lax.broadcasted_iota(jnp.int32, (HALO, HEAD), 0)
    turned = pltpu.roll(edge[...], half, 1)
    last = jnp.broadcast_to(chunk[pl.ds(rows, 1), :], (HALO, HEAD))
    down = jnp.where(row == 0, last, pltpu.roll(turned, 1, 0))
    chunk[pl.ds(rows, HALO), :] = jnp.where(lane < half, down, turned)
    off, odd = (DEVICES - k) // 2, (DEVICES - k) % 2 == 1
    step = 96
    for i in range(0, rows, step):
        flat[pl.ds(i, step), :] = shifted_rows(chunk, off, odd, step, i)

    def put(pieces):
        for m, r, n, f in pieces:
            blocks = layout.blocks[m]
            for c in range(blocks):
                mats[m][pl.ds(r, n), c * HEAD : (c + 1) * HEAD] = flat[pl.ds(f + c, n, stride=blocks), :].astype(BF16)

    layout.each_kind(k, put)
    pl.when(k > 0)(lambda: send.wait_send())


def own_rows(layout, k, total, small, flat, edge, edge_sems):
    rows, out = layout.flat_rows, total

    def put(pieces):
        for m, _, n, f in pieces:
            blocks = layout.blocks[m]
            for c in range(blocks):
                flat[pl.ds(HALO + f + c, n, stride=blocks), :] = total[pl.ds(f + c * n, n), :]

    layout.each_kind(k, put)
    after = jnp.minimum(k + 1, DEVICES - 1)
    send = pltpu.make_async_remote_copy(
        src_ref=flat.at[pl.ds(rows, HALO), :], dst_ref=edge, send_sem=edge_sems.at[0], recv_sem=edge_sems.at[1],
        device_id=(after // PLANE, after % PLANE), device_id_type=MESH,
    )
    pl.when(k < DEVICES - 1)(lambda: send.start())

    @pl.when(k == 0)
    def _():
        across = layout.width // HEAD
        for t in range(4):
            for c in range(across):
                flat[t * across + c : t * across + c + 1, :] = small[t : t + 1, c * HEAD : (c + 1) * HEAD]

    @pl.when(k > 0)
    def _():
        send.wait_recv()
        flat[pl.ds(0, HALO), :] = edge[...]

    step = 8 * 97
    for i in range(0, rows + 8, step):
        out[pl.ds(i, step), :] = shifted_rows(flat, k // 2, k % 2 == 1, step, i)
    pl.when(k < DEVICES - 1)(lambda: send.wait_send())


class Steps:
    heads_hook = down_hook = forward_hook = small_forward_hook = backward_hook = small_backward_hook = input_hook = None

    def nothing(self, *args):
        pass

    enter = first_weights = up_weights = down_weights = pool_free = nothing
    up_done = qkv_done = before_output = between_outputs = close = nothing


def layer_body(sz, layout, steps, len_ref, sup_ref, x_hbm, cot_hbm, out_hbm, gin_hbm, gb_ref, work, io_sem):
    (xr, cr, act2_t, cot_t, qkv, exps_big, exps_small, ctx, ctx_t, hid, pool, gres_low, dox, parts,
     resid, qm, km, inv_ref, sums, w_qkv, w_out, w_up, w_down, x_cuts, c_cuts) = work
    width = sz.width
    load_x = pltpu.make_async_copy(x_hbm, x_cuts, io_sem.at[0])
    load_c = pltpu.make_async_copy(cot_hbm, c_cuts, io_sem.at[1])
    load_x.start()
    load_c.start()
    shift, begins, sups = table_facts(sz, len_ref, sup_ref)

    def masks():
        mask_features(sz, begins, sups, qm, km)
        sums[...] = jnp.zeros_like(sums)

    def set_rows(ref):
        def write(rows, values):
            ref[rows, :] = values

        return write

    def before_weights():
        masks()
        load_x.wait()
        roll_rows(sz, shift, x_cuts, set_rows(xr))

    steps.enter(before_weights)

    def take_cotangent():
        load_c.wait()
        roll_rows(sz, shift, c_cuts, set_rows(cr))
        for i in range(sz.rows // TALL):
            cot_t[:, i * TALL : (i + 1) * TALL] = cr[i * TALL : (i + 1) * TALL, :].T

    steps.first_weights(take_cotangent)
    phase_qkv(sz, gb_ref, xr, x_cuts, w_qkv, qkv)
    attend_forward(sz, 0, sz.big_keys, sz.big, exps_big, qkv, qm, km, ctx, ctx_t, inv_ref, steps.forward_hook)
    attend_forward(sz, sz.big, sz.small, sz.small, exps_small, qkv, qm, km, ctx, ctx_t, inv_ref, steps.small_forward_hook)
    steps.up_weights()
    phase_up(sz, gb_ref, xr, ctx, w_out, w_up, act2_t, hid, pool, resid)
    weight_grad_turned(layout, 3, cot_t, lambda i: hid[:, rows_at(i)], parts)
    steps.down_weights()
    out_r, gin_r, gqkv, act1_t = c_cuts, x_cuts, hid, cot_t
    phase_down(sz, gb_ref, cr, w_up, w_down, hid, pool, resid, out_r, gres_low, sums, steps.down_hook)
    per = BLOCK // HEAD
    weight_grad(
        layout, 2, act2_t,
        lambda i: jnp.concatenate([pool[pool_at(sz, i * per + c, 0, sz.rows), :] for c in range(per)], axis=1), parts,
    )
    steps.pool_free()
    weight_grad(layout, 1, ctx_t, lambda i: gres_low[:, rows_at(i)], parts)
    for i in range(sz.rows // CUT):
        act1_t[:, i * CUT : (i + 1) * CUT] = x_cuts[i].T
    steps.up_done()
    phase_heads(sz, ctx, inv_ref, w_out, gres_low, dox, steps.heads_hook)
    gqkv[sz.big_keys : sz.big, width : 3 * width] = jnp.zeros((sz.big - sz.big_keys, 2 * width), BF16)
    attend_backward(sz, 0, sz.big_keys, sz.big, exps_big, qkv, dox, gqkv, steps.backward_hook)
    attend_backward(sz, sz.big, sz.small, sz.small, exps_small, qkv, dox, gqkv, steps.small_backward_hook)
    weight_grad(layout, 0, act1_t, lambda i: gqkv[:, rows_at(i)], parts)
    steps.qkv_done()
    phase_input(sz, gb_ref, xr, gqkv, w_qkv, gres_low, gin_r, sums, steps.input_hook)
    steps.before_output()
    back = lax.rem(sz.rows - shift, sz.rows)
    roll_rows(sz, back, out_r, set_rows(ctx))
    store_out = pltpu.make_async_copy(ctx, out_hbm, io_sem.at[0])
    store_out.start()
    steps.between_outputs()
    roll_rows(sz, back, gin_r, set_rows(xr))
    store_gin = pltpu.make_async_copy(xr, gin_hbm, io_sem.at[1])
    store_gin.start()
    steps.close()
    store_out.wait()
    store_gin.wait()


def small_terms(sums, out):
    for t in range(4):
        out[t : t + 1, :] = jnp.sum(sums[t], axis=0, keepdims=True)


def work_shapes(sz, layout):
    rows, width, ffn = sz.rows, sz.width, sz.ffn

    def low(*shape):
        return pltpu.VMEM(shape, BF16)

    return [
        low(rows, width), low(rows, width), low(width, rows), low(width, rows), low(rows, 3 * width),
        low(sz.heads, sz.big_keys, sz.big), low(sz.heads, sz.small, sz.small), low(rows, width), low(width, rows),
        low(rows, ffn), low(rows * ffn // HEAD, HEAD), low(rows, width), low(sz.heads, rows, 2 * HEAD),
        low(layout.flat_rows * DEVICES, HEAD), pltpu.VMEM((rows, width), F32), low(rows, HEAD), low(rows, HEAD),
        pltpu.VMEM((sz.heads, 8, rows), F32), pltpu.VMEM((4, 8, width), F32),
        low(width, 3 * width), low(width, width), low(width, ffn), low(ffn, width),
        low(rows // CUT, CUT, width), low(rows // CUT, CUT, width),
    ]


WORK = 25
VMEM_LIMIT = 63 * 2**20 + 3 * 2**18


def plain_kernel(sz, layout, len_ref, sup_ref, x_hbm, cot_hbm, gb_ref, *rest):
    weights, (out_hbm, gin_hbm, parts_hbm, small_ref), rest = rest[:4], rest[4:8], rest[8:]
    work, (load_sem, io_sem) = rest[:WORK], rest[WORK:]
    parts, sums, mats = work[13], work[18], work[19:23]
    steps = Steps()
    loads = [pltpu.make_async_copy(src, dst, load_sem.at[i]) for i, (src, dst) in enumerate(zip(weights, mats))]
    store = pltpu.make_async_copy(parts, parts_hbm, load_sem.at[4])

    def enter(fill):
        for copy in loads:
            copy.start()
        fill()

    def first_weights(fill):
        fill()
        loads[0].wait()

    def up_weights():
        for copy in loads[1:]:
            copy.wait()

    def close():
        small_terms(sums, small_ref)
        store.wait()

    steps.enter, steps.first_weights, steps.up_weights = enter, first_weights, up_weights
    steps.qkv_done, steps.close = store.start, close
    layer_body(sz, layout, steps, len_ref, sup_ref, x_hbm, cot_hbm, out_hbm, gin_hbm, gb_ref, work, io_sem)


def cuts_of(values):
    return values.reshape(values.shape[0] // CUT, CUT, values.shape[1])


def layer(x_in, cotangent, lengths, support, gains, w_qkv, w_out, w_up, w_down):
    rows, width = x_in.shape
    ffn = w_up.shape[1]
    sz, layout = Shapes(rows, width, ffn), Layout(width, ffn)
    anywhere = pl.BlockSpec(memory_space=pl.ANY)
    vmem = pl.BlockSpec(memory_space=pltpu.VMEM)
    smem = pl.BlockSpec(memory_space=pltpu.SMEM)
    return pl.pallas_call(
        functools.partial(plain_kernel, sz, layout),
        out_shape=(
            jax.ShapeDtypeStruct((rows, width), BF16),
            jax.ShapeDtypeStruct((rows, width), BF16),
            jax.ShapeDtypeStruct((layout.flat_rows * DEVICES, HEAD), BF16),
            jax.ShapeDtypeStruct((4, width), F32),
        ),
        in_specs=[smem, smem, anywhere, anywhere, vmem, anywhere, anywhere, anywhere, anywhere],
        out_specs=[anywhere] * 3 + [vmem],
        scratch_shapes=work_shapes(sz, layout) + [pltpu.SemaphoreType.DMA((5,)), pltpu.SemaphoreType.DMA((2,))],
        compiler_params=pltpu.CompilerParams(vmem_limit_bytes=VMEM_LIMIT),
    )(lengths, support, cuts_of(x_in), cuts_of(cotangent), gains, w_qkv, w_out, w_up, w_down)


SENDS = 288
SLOTS = 208
ROOM = 7


HEADS_PLAN = {1: [("corner", 2)], 2: [("corner", 1)]}
BACKWARD_PLAN = {1: [("side", 2)], 2: [("side", 1)]}
SMALL_PLAN = {3: [("line", 2)]}


def planned(scatter, plan):
    return {step: [(getattr(scatter, way), s) for way, s in acts] for step, acts in plan.items()}


def whole_kernel(sz, layout, len_ref, sup_ref, x_hbm, cot_hbm, shard, out_hbm, gin_hbm, own_out, small_out, *rest):
    work, rest = rest[:WORK], rest[WORK:]
    (gb_ref, chunk, flat, edge, gains, extra, small, small_in,
     send_sem, recv_sem, gain_send, gain_recv, edge_sems, out_edge_sems, load_sem, io_sem, ready_sem) = rest
    pool, parts, sums, mats = work[10], work[13], work[18], work[19:23]
    rows = layout.flat_rows
    link = Link(layout, send_sem, recv_sem)
    gather = Gather(link, mats, gains, gain_send, gain_recv)
    scatter = Scatter(
        link, parts, lambda s: (extra, 0) if s == LINE - 1 else (pool, s * ROOM * rows), (extra, ROOM * rows),
        (pool, (LINE - 1) * ROOM * rows), small, small_in,
    )
    load = pltpu.make_async_copy(shard, chunk.at[pl.ds(0, shard.shape[0]), :], load_sem)
    steps = Steps()

    def at(index, table):
        for number, acts in table.items():

            @pl.when(index == number)
            def _():
                for act, s in acts:
                    act(s)

    def enter(fill):
        load.start()
        link.meet()
        load.wait()
        send = edge_copy(layout, link.k, chunk, edge, edge_sems)
        pl.when(link.k > 0)(lambda: send.start())

        @pl.when(link.k == 0)
        def _():
            gains[...] = chunk[pl.ds(0, HALO), :].astype(BF16).astype(F32)

        fill()
        own_part(layout, link.k, chunk, edge, flat, mats, send)
        gather.start_later()

    def first_weights(fill):
        pl.when(link.z >= LINE // 2)(fill)
        for p in range(PIECES):
            gather.along(p)
        gather.first_to_mate(0)
        gather.start_upward()
        for p in range(PIECES):
            gather.across(p)
        gather.first_to_mate(1)
        gather.first_to_mate(2)
        gather.first_to_mate(3)
        for s in range(1, LINE):
            gather.line(s)
        gather.first_from_mate()
        pl.when(link.z < LINE // 2)(fill)
        across = layout.width // HEAD
        for t in range(4):
            for c in range(across):
                gb_ref[t : t + 1, c * HEAD : (c + 1) * HEAD] = gains[pl.ds(t * across + c, 1), :]

    def forward_hook(head):
        at(head, {1: [(gather.corner, 1)], 3: [(gather.corner, 2)]})

    def small_forward_hook(head):
        at(head, {1: [(gather.far, 1)], 2: [(gather.corner, 3)], 3: [(gather.far, 2)]})

    def up_weights():
        gather.mates(1)
        gather.mates(2)

    def down_weights():
        scatter.share(3)
        gather.far(3)
        gather.mates(3)

    def down_hook(i):
        at(i, {0: [(scatter.corner, 3)], 1: [(scatter.side, 3)], 2: [(scatter.line, 3)]})

    def pool_free():
        link.tell(ready_sem)

    def up_done():
        link.told(ready_sem)
        scatter.share(2)
        scatter.share(1)

    def heads_hook(i):
        at(i, planned(scatter, HEADS_PLAN))

    def backward_hook(head):
        at(head, planned(scatter, BACKWARD_PLAN))

    def small_backward_hook(head):
        at(head, planned(scatter, SMALL_PLAN))

    def qkv_done():
        scatter.share(0)
        scatter.line(1)

    def input_hook(i):
        at(i, {0: [(lambda s: scatter.tail_corner(), 0)], 2: [(lambda s: scatter.tail_side(), 0)]})

    def before_output():
        small_terms(sums, small.at[0])
        scatter.small_send(0)
        scatter.leaf()
        scatter.small_add(0)
        scatter.small_send(1)

    def between_outputs():
        scatter.small_add(1)
        scatter.small_send(2)
        scatter.middle()
        scatter.small_add(2)
        scatter.small_send(3)

    def close():
        gather.finish()
        link.finish()
        scatter.total(chunk)
        scatter.small_add(3)
        small_out[...] = small[4, 3:4, :]
        own_rows(layout, link.k, chunk, small.at[4], flat, edge, out_edge_sems)
        store = pltpu.make_async_copy(chunk.at[pl.ds(0, rows + 8), :], own_out, load_sem)
        store.start()
        store.wait()

    steps.enter, steps.first_weights, steps.pool_free = enter, first_weights, pool_free
    steps.forward_hook, steps.small_forward_hook, steps.up_weights = forward_hook, small_forward_hook, up_weights
    steps.down_weights, steps.down_hook, steps.up_done = down_weights, down_hook, up_done
    steps.heads_hook = heads_hook
    steps.backward_hook, steps.small_backward_hook, steps.qkv_done = backward_hook, small_backward_hook, qkv_done
    steps.input_hook, steps.before_output, steps.between_outputs, steps.close = input_hook, before_output, between_outputs, close
    layer_body(sz, layout, steps, len_ref, sup_ref, x_hbm, cot_hbm, out_hbm, gin_hbm, gb_ref, work, io_sem)


def padded_rows(values):
    rows = -(-values.shape[0] // 1024) * 8
    return jnp.pad(values, (0, rows * HEAD - values.shape[0])).reshape(rows, HEAD)


def whole_layer(layout, x_in, cotangent, lengths, support, master):
    rows, width = x_in.shape
    sz = Shapes(rows, width, layout.ffn)
    anywhere = pl.BlockSpec(memory_space=pl.ANY)
    vmem = pl.BlockSpec(memory_space=pltpu.VMEM)
    smem = pl.BlockSpec(memory_space=pltpu.SMEM)
    dma = pltpu.SemaphoreType.DMA
    part = layout.flat_rows
    return pl.pallas_call(
        functools.partial(whole_kernel, sz, layout),
        out_shape=(
            jax.ShapeDtypeStruct((rows, width), BF16),
            jax.ShapeDtypeStruct((rows, width), BF16),
            jax.ShapeDtypeStruct((part + 8, HEAD), F32),
            jax.ShapeDtypeStruct((1, width), F32),
        ),
        in_specs=[smem, smem, anywhere, anywhere, anywhere],
        out_specs=[anywhere] * 3 + [vmem],
        scratch_shapes=work_shapes(sz, layout) + [
            pltpu.VMEM((4, width), F32), pltpu.VMEM((part + 3 * HALO, HEAD), F32), pltpu.VMEM((part + 2 * HALO, HEAD), F32),
            pltpu.VMEM((HALO, HEAD), F32), pltpu.VMEM((HALO, HEAD), F32), pltpu.VMEM(((ROOM + LINE) * part, HEAD), BF16),
            pltpu.VMEM((5, 4, width), F32), pltpu.VMEM((3 + LINE, 4, width), F32),
            dma((SENDS,)), dma((SLOTS,)), dma((64,)), dma, dma((2,)), dma((2,)), dma, dma((2,)),
            pltpu.SemaphoreType.REGULAR,
        ],
        compiler_params=pltpu.CompilerParams(collective_id=0, has_side_effects=True, vmem_limit_bytes=VMEM_LIMIT),
    )(lengths, support, cuts_of(x_in), cuts_of(cotangent), padded_rows(master))


CARRIERS = 4


def hand_over_kernel(count, *refs):
    sources, targets, (held, semaphores) = refs[:count], refs[count : 2 * count], (refs[2 * count : 3 * count], refs[3 * count :])
    pairs = []
    for src, dst, mid in zip(sources, targets, held):
        step = max(src.shape[0] // CARRIERS, 1)
        for i in range(0, src.shape[0], step):
            some, index = pl.ds(i, step), len(pairs)
            pairs.append((
                pltpu.make_async_copy(src.at[some, :], mid.at[some, :], semaphores[0].at[index]),
                pltpu.make_async_copy(mid.at[some, :], dst.at[some, :], semaphores[1].at[index]),
            ))
    for load, _ in pairs:
        load.start()
    for load, store in pairs:
        load.wait()
        store.start()
    for _, store in pairs:
        store.wait()


def hand_over(*arrays):
    anywhere = pl.BlockSpec(memory_space=pl.ANY)
    dma = pltpu.SemaphoreType.DMA((CARRIERS * len(arrays),))
    return pl.pallas_call(
        functools.partial(hand_over_kernel, len(arrays)),
        out_shape=tuple(jax.ShapeDtypeStruct(v.shape, v.dtype) for v in arrays),
        in_specs=[anywhere] * len(arrays),
        out_specs=[anywhere] * len(arrays),
        scratch_shapes=[pltpu.VMEM(v.shape, v.dtype) for v in arrays] + [dma, dma],
    )(*arrays)


def adam(grads, first_moment, second_moment, master, step_count):
    step_float = step_count[0].astype(F32)
    new_first = BETA_ONE * first_moment + (1.0 - BETA_ONE) * grads
    new_second = BETA_TWO * second_moment + (1.0 - BETA_TWO) * grads * grads
    first_hat = new_first / (1.0 - jnp.power(F32(BETA_ONE), step_float))
    second_hat = new_second / (1.0 - jnp.power(F32(BETA_TWO), step_float))
    adam_step = first_hat / (jnp.sqrt(second_hat) + ADAM_EPS) + DECAY_RATE * master
    return new_first, new_second, adam_step


def flat_of_parts(layout, parts):
    by_part, flat = parts.reshape(DEVICES, layout.flat_rows, HEAD), []
    for k, own in enumerate(layout.pieces):
        for m, _, n, f in own:
            blocks = layout.blocks[m]
            piece = by_part[k, f : f + n * blocks].reshape(blocks, n, HEAD)
            flat.append(piece.transpose(1, 0, 2).reshape(-1))
    return jnp.concatenate(flat)


def plain_gather(layout, master):
    width, ffn = layout.width, layout.ffn
    flat = lax.all_gather(master.astype(BF16), ("dp", "fsdp"), axis=0, tiled=True)
    shapes = [(4, width), (width, 3 * width), (width, width), (width, ffn), (ffn, width)]
    arrays, start = [], 0
    for shape in shapes:
        arrays.append(flat[start : start + math.prod(shape)].reshape(shape))
        start += math.prod(shape)
    return (*arrays[1:], arrays[0].astype(F32))


def plain_scatter(layout, parts, small):
    axes = ("dp", "fsdp")
    local = jnp.concatenate([small.reshape(-1), flat_of_parts(layout, parts).astype(F32)])
    return lax.psum_scatter(local, axes, scatter_dimension=0, tiled=True), lax.psum(small[3], axes)


def per_device(sizes, x_in, cotangent, table_lengths, support_counts, master, first_moment, second_moment, step_count):
    width, shard = x_in.shape[1], master.shape[0]
    param_count = shard * sizes[0] * sizes[1]
    ffn = (param_count - 4 * width - 4 * width * width) // (2 * width)
    layout = Layout(width, ffn)
    if layout.fits(param_count, sizes):
        output, grad_input, rows, total = whole_layer(layout, x_in, cotangent, table_lengths, support_counts, master)
        output, grad_input, total = hand_over(output, grad_input, total)
        grads, bias_two_grad = rows.reshape(-1)[:shard], total[0]
    else:
        *weights, gains = plain_gather(layout, master)
        output, grad_input, parts, small = layer(x_in, cotangent, table_lengths, support_counts, gains, *weights)
        grads, bias_two_grad = plain_scatter(layout, parts, small)
    new_first, new_second, adam_step = adam(grads, first_moment, second_moment, master, step_count)
    return output, grad_input, grads, new_first, new_second, adam_step, bias_two_grad


def solution(mesh):
    rows, flat = P(("dp", "fsdp"), None), P(("dp", "fsdp"))
    return jax.shard_map(
        functools.partial(per_device, (mesh.shape["dp"], mesh.shape["fsdp"])),
        mesh=mesh,
        in_specs=(rows, rows, rows, rows, flat, flat, flat, P()),
        out_specs=(rows, rows, flat, flat, flat, flat, P()),
        check_vma=False,
    )
```

```python
import functools
import math

import jax
import jax.numpy as jnp
from jax import lax
from jax.experimental import pallas as pl
from jax.experimental.pallas import tpu as pltpu
from jax.sharding import PartitionSpec as P

HEAD = 128
EPS_NORM = 1e-05
BETA_ONE = 0.9
BETA_TWO = 0.999
ADAM_EPS = 1e-08
DECAY_RATE = 0.01
MASKED = -1e30
F32 = jnp.float32
BF16 = jnp.bfloat16
BLOCK = 256
TALL = 512
CUT = 128
GELU_ONE = math.sqrt(2.0 / math.pi)
GELU_THREE = 0.044715


def mm(left, right):
    return jnp.dot(left, right, preferred_element_type=F32)


def mm_t(left, right):
    return lax.dot_general(left, right, (((1,), (1,)), ((), ())), preferred_element_type=F32)


def rows_at(index, size=BLOCK):
    return pl.ds(pl.multiple_of(index * size, size), size)


class Shapes:
    def __init__(self, rows, width, ffn):
        self.rows, self.width, self.ffn = rows, width, ffn
        self.heads = width // HEAD
        self.big = 2 * rows // 3
        self.big_keys = 3 * self.big // 4
        self.small = rows - self.big


MESH = pl.DeviceIdType.MESH
LINE = 4
PLANE = 8
DEVICES = LINE * PLANE
HALO = 16
PIECES = 4


class Layout:
    def __init__(self, width, ffn):
        self.width, self.ffn = width, ffn
        shapes = [(width, 3 * width), (width, width), (width, ffn), (ffn, width)]
        self.blocks = [s[1] // HEAD for s in shapes]
        self.flat_rows = sum(r * c for r, c in shapes) // (HEAD * DEVICES)
        ends, total = [], 0
        for r, c in shapes:
            total += r * c // HEAD
            ends.append(total)
        starts = [0] + ends[:-1]
        self.pieces = []
        for k in range(DEVICES):
            lo, hi, own = k * self.flat_rows, (k + 1) * self.flat_rows, []
            for m in range(4):
                a, b = max(lo, starts[m]), min(hi, ends[m])
                if a < b:
                    own.append((m, (a - starts[m]) // self.blocks[m], (b - a) // self.blocks[m], a - lo))
            self.pieces.append(own)
        self.unit = math.gcd(*(n for own in self.pieces for m, _, n, _ in own if m == 3))
        self.kinds = []
        for k, own in enumerate(self.pieces):
            last = self.kinds[-1] if self.kinds else None
            if last and len(own) == 1 and self.same(self.pieces[last[0]], own):
                last[1] = k + 1
            else:
                self.kinds.append([k, k + 1])

    @staticmethod
    def same(left, right):
        return len(left) == len(right) and all(a[0] == b[0] and a[2:] == b[2:] for a, b in zip(left, right))

    def fits(self, param_count, devices):
        whole = self.flat_rows * HEAD * DEVICES + 4 * self.width
        first = all(len(own) == 1 and own[0][0] == 0 and own[0][2] % (8 * PIECES) == 0 for own in self.pieces[:PLANE])
        exact = all(
            sum(p[2] * self.blocks[p[0]] for p in own) == self.flat_rows and all(p[1] % 8 == 0 and p[2] % 8 == 0 for p in own)
            for own in self.pieces
        )
        return devices == (LINE, PLANE) and exact and first and whole == param_count and 4 * self.width == HALO * HEAD

    def each_kind(self, k, act):
        for lo, hi in self.kinds:
            def run(lo=lo, hi=hi):
                first = self.pieces[lo]
                if hi - lo == 1:
                    act(first)
                else:
                    m, r, n, f = first[0]
                    act([(m, pl.multiple_of(r + (k - lo) * n, 8), n, f)])

            pl.when((k >= lo) & (k < hi))(run)

    def halves(self, pieces):
        goal, done, parts = self.flat_rows // 2, 0, ([], [])
        for m, r, n, f in pieces:
            take = min(n, max(0, (goal - done)) // self.blocks[m])
            if take:
                parts[0].append((m, r, take, f))
            if n - take:
                parts[1].append((m, r + take, n - take, f + take * self.blocks[m]))
            done += take * self.blocks[m]
        return parts


def table_facts(sz, len_ref, sup_ref):
    lengths = [len_ref[0, t] for t in range(4)]
    support = [sup_ref[0, t] for t in range(4)]
    starts = [jnp.int32(0), lengths[0], lengths[0] + lengths[1], lengths[0] + lengths[1] + lengths[2]]
    is_big = [lengths[t] == sz.big for t in range(4)]

    def pick(values):
        total = jnp.int32(0)
        for t in range(4):
            total = total + jnp.where(is_big[t], values[t], 0)
        return total

    shift = pick(starts)
    lens = [pick([lengths[(t + j) % 4] for t in range(4)]) for j in range(4)]
    sups = [pick([support[(t + j) % 4] for t in range(4)]) for j in range(4)]
    begins = [jnp.int32(0), lens[0], lens[0] + lens[1], lens[0] + lens[1] + lens[2]]
    return shift, begins, sups


def mask_features(sz, begins, sups, qm_ref, km_ref):
    def step(i, carry):
        shape = (BLOCK, HEAD)
        row = lax.broadcasted_iota(jnp.int32, shape, 0) + i * BLOCK
        lane = lax.broadcasted_iota(jnp.int32, shape, 1)
        table = jnp.zeros(shape, jnp.int32)
        limit = jnp.full(shape, begins[0] + sups[0], jnp.int32)
        for t in range(1, 4):
            inside = row >= begins[t]
            table = jnp.where(inside, t, table)
            limit = jnp.where(inside, begins[t] + sups[t], limit)
        own = table == lane
        qm_ref[rows_at(i), :] = jnp.where(own, 1.0, 0.0).astype(BF16)
        bad = jnp.where(own, jnp.where(row < limit, 0.0, MASKED), jnp.where(lane < 4, MASKED, 0.0))
        km_ref[rows_at(i), :] = bad.astype(BF16)
        return carry

    lax.fori_loop(0, sz.rows // BLOCK, step, 0, unroll=2)


def roll_rows(sz, shift, source, write):
    blocks = sz.rows // CUT
    coarse, fine = shift // CUT, shift % CUT
    row = lax.broadcasted_iota(jnp.int32, (CUT, 2 * CUT), 0)
    column = lax.broadcasted_iota(jnp.int32, (CUT, 2 * CUT), 1)
    chosen = jnp.where(row + fine == column, 1.0, 0.0).astype(BF16)

    def step(i, carry):
        here = lax.rem(i + coarse, blocks)
        after = lax.rem(i + coarse + 1, blocks)
        pair = jnp.concatenate([source[here], source[after]], axis=0)
        write(rows_at(i, CUT), mm(chosen, pair).astype(BF16))
        return carry

    lax.fori_loop(0, blocks, step, 0, unroll=4)


def normed(values):
    centre = values - jnp.mean(values, axis=-1, keepdims=True)
    inverse = lax.rsqrt(jnp.mean(centre * centre, axis=-1, keepdims=True) + EPS_NORM)
    return centre * inverse, inverse


def norm_back(grad_out, norm, inverse, gain):
    grad_normed = grad_out * gain
    return inverse * (
        grad_normed
        - jnp.mean(grad_normed, axis=-1, keepdims=True)
        - norm * jnp.mean(grad_normed * norm, axis=-1, keepdims=True)
    )


def eight_rows(values):
    rows, width = values.shape
    return jnp.sum(values.reshape(rows // 8, 8, width), axis=0)


def phase_qkv(sz, gb_ref, xr, act_cuts, w_qkv, qkv):
    gain, bias = gb_ref[0:1, :], gb_ref[1:2, :]

    def step(i, carry):
        norm, _ = normed(xr[rows_at(i), :].astype(F32))
        act = (norm * gain + bias).astype(BF16)
        cuts = BLOCK // CUT
        act_cuts[pl.ds(i * cuts, cuts)] = act.reshape(cuts, CUT, sz.width)
        qkv[rows_at(i), :] = mm(act, w_qkv[...]).astype(BF16)
        return carry

    lax.fori_loop(0, sz.rows // BLOCK, step, 0, unroll=2)


def head_at(head, offset=0):
    return pl.ds(pl.multiple_of(offset + head * HEAD, HEAD), HEAD)


def attend_forward(sz, base, key_count, query_count, exps, qkv, qm, km, ctx, ctx_t, inv_ref, hook=None):
    keep = pl.ds(base, key_count)
    here = pl.ds(base, query_count)
    scale = math.log2(math.e) / math.sqrt(HEAD)

    def per_head(head, carry):
        keys = jnp.concatenate([qkv[keep, head_at(head, sz.width)], km[keep, :]], axis=1)
        values_t = qkv[keep, head_at(head, 2 * sz.width)].T
        queries = jnp.concatenate([qkv[here, head_at(head)], qm[here, :]], axis=1)
        scores = mm_t(keys, queries)
        top = jnp.max(scores, axis=0, keepdims=True)
        shifted = jnp.exp2((scores - top) * scale)
        total = jnp.sum(shifted, axis=0, keepdims=True)
        low = shifted.astype(BF16)
        exps[head] = low
        inverse = 1.0 / total
        mixed = (mm(values_t, low) * inverse).astype(BF16)
        ctx_t[head_at(head), here] = mixed
        ctx[here, head_at(head)] = mixed.T
        inv_ref[head, :, here] = jnp.broadcast_to(inverse, (8, query_count))
        if hook:
            hook(head)
        return carry

    lax.fori_loop(0, sz.heads, per_head, 0)


def pool_at(sz, column, start, size):
    return pl.ds(pl.multiple_of(column * sz.rows + start, 256), size)


def phase_up(sz, gb_ref, xr, ctx, w_out, w_up, act_t, hid, pool, resid_ref):
    gain, bias = gb_ref[2:3, :], gb_ref[3:4, :]

    def step(i, carry):
        here = rows_at(i, TALL)
        resid = xr[here, :].astype(F32) + mm(ctx[here, :], w_out[...])
        resid_ref[here, :] = resid
        norm, _ = normed(resid)
        act = (norm * gain + bias).astype(BF16)
        act_t[:, here] = act.T
        for f in range(sz.ffn // BLOCK):
            part = slice(f * BLOCK, (f + 1) * BLOCK)
            pre = mm(act, w_up[:, part])
            square = pre * pre
            bent = jnp.tanh(pre * (GELU_ONE + GELU_ONE * GELU_THREE * square))
            half = 0.5 + 0.5 * bent
            value = pre * half
            hid[here, part] = value.astype(BF16)
            slope = half + value * (1.0 - half) * (2.0 * GELU_ONE + 6.0 * GELU_ONE * GELU_THREE * square)
            slope = slope.astype(BF16)
            for c in range(BLOCK // HEAD):
                pool[pool_at(sz, f * (BLOCK // HEAD) + c, i * TALL, TALL), :] = slope[:, c * HEAD : (c + 1) * HEAD]
        return carry

    lax.fori_loop(0, sz.rows // TALL, step, 0)


def phase_down(sz, gb_ref, cr, w_up, w_down, hid, pool, resid_ref, out_r, gres_low, sums, hook=None):
    gain = gb_ref[2:3, :]

    def step(i, carry):
        here = rows_at(i, TALL)
        cot = cr[here, :]
        resid = resid_ref[here, :]
        norm, inverse = normed(resid)
        grad_pre = []
        for f in range(sz.ffn // BLOCK):
            part = slice(f * BLOCK, (f + 1) * BLOCK)
            grad_hidden = mm_t(cot, w_down[part, :])
            for c in range(BLOCK // HEAD):
                at = pool_at(sz, f * (BLOCK // HEAD) + c, i * TALL, TALL)
                low = (grad_hidden[:, c * HEAD : (c + 1) * HEAD] * pool[at, :].astype(F32)).astype(BF16)
                pool[at, :] = low
                grad_pre.append(low)
        grad_act = mm_t(jnp.concatenate(grad_pre, axis=1), w_up[...])
        total = resid + mm(hid[here, :], w_down[...])
        cuts = TALL // CUT
        out_r[pl.ds(i * cuts, cuts)] = total.astype(BF16).reshape(cuts, CUT, sz.width)
        sums[2] += eight_rows(grad_act * norm)
        sums[3] += eight_rows(grad_act)
        low = (cot.astype(F32) + norm_back(grad_act, norm, inverse, gain)).astype(BF16)
        gres_low[here, :] = low
        if hook:
            hook(i)
        return carry

    lax.fori_loop(0, sz.rows // TALL, step, 0)


def phase_heads(sz, ctx, inv_ref, w_out, gres_low, dox, hook=None):
    def step(i, carry):
        here = rows_at(i, TALL)
        grad_ctx = mm_t(gres_low[here, :], w_out[...]).astype(BF16).astype(F32)
        lane = lax.broadcasted_iota(jnp.int32, (TALL, HEAD), 1)
        for head in range(sz.heads):
            part = slice(head * HEAD, (head + 1) * HEAD)
            column = inv_ref[head, :, here].T[:, 0:1]
            scaled = (grad_ctx[:, part] * column).astype(BF16)
            delta = jnp.sum(scaled.astype(F32) * ctx[here, part].astype(F32), axis=1, keepdims=True)
            high = delta.astype(BF16).astype(F32)
            rest = delta - high
            dox[head, here, 0:HEAD] = scaled
            dox[head, here, HEAD : 2 * HEAD] = jnp.where(lane == 0, -high, jnp.where(lane == 1, -rest, 0.0)).astype(BF16)
        if hook:
            hook(i)
        return carry

    lax.fori_loop(0, sz.rows // TALL, step, 0, unroll=3)


def weight_grad(layout, m, left_t, right, parts):
    rows, per = layout.flat_rows, BLOCK // HEAD

    def step(i, carry):
        product = mm(left_t[...], right(i)).astype(BF16)
        for k, own in enumerate(layout.pieces):
            for matrix, r, n, f in own:
                if matrix == m:
                    for c in range(per):
                        there = pl.multiple_of(k * rows + f + (i * per + c) * n, 16)
                        parts[pl.ds(there, n), :] = product[r : r + n, c * HEAD : (c + 1) * HEAD]
        return carry

    lax.fori_loop(0, layout.blocks[m] // per, step, 0, unroll=2)


def weight_grad_turned(layout, m, left_t, right, parts):
    rows, unit = layout.flat_rows, layout.unit
    first_k, first = next((k, p) for k, own in enumerate(layout.pieces) for p in own if p[0] == m)
    later = layout.pieces[first_k + 1][-1][2]

    def step(i, carry):
        product = mm(left_t[...], right(i)).astype(BF16).T
        for q in range(BLOCK // unit):
            r = i * BLOCK + q * unit
            head = r < first[2]
            n = jnp.where(head, first[2], later)
            k = jnp.where(head, first_k, first_k + 1 + (r - first[2]) // later)
            base = jnp.where(head, first[3] + r, (r - first[2]) % later)
            for c in range(layout.blocks[m]):
                there = pl.multiple_of(k * rows + base + c * n, 16)
                parts[pl.ds(there, unit), :] = product[q * unit : (q + 1) * unit, c * HEAD : (c + 1) * HEAD]
        return carry

    lax.fori_loop(0, layout.ffn // BLOCK, step, 0, unroll=2)


def attend_backward(sz, base, key_count, query_count, exps, qkv, dox, gqkv, hook=None):
    keep = pl.ds(base, key_count)
    asked = pl.ds(base, query_count)
    scale = 1.0 / math.sqrt(HEAD)
    lane = lax.broadcasted_iota(jnp.int32, (key_count, HEAD), 1)
    ones = jnp.where(lane < 2, 1.0, 0.0).astype(BF16)

    def per_head(head, carry):
        values = jnp.concatenate([qkv[keep, head_at(head, 2 * sz.width)], ones], axis=1)
        keys_t = qkv[keep, head_at(head, sz.width)].T
        gqkv[keep, head_at(head, 2 * sz.width)] = mm(exps[head], dox[head, asked, 0:HEAD]).astype(BF16)
        for j in range(query_count // TALL):
            here = pl.ds(base + j * TALL, TALL)
            columns = pl.ds(j * TALL, TALL)
            grad_probs = mm_t(values, dox[head, here, :])
            grad_scores = (exps[head, :, columns].astype(F32) * grad_probs).astype(BF16)
            exps[head, :, columns] = grad_scores
            gqkv[here, head_at(head)] = (mm(keys_t, grad_scores) * scale).astype(BF16).T
        gqkv[keep, head_at(head, sz.width)] = (mm(exps[head], qkv[asked, head_at(head)]) * scale).astype(BF16)
        if hook:
            hook(head)
        return carry

    lax.fori_loop(0, sz.heads, per_head, 0)


def phase_input(sz, gb_ref, xr, gqkv, w_qkv, gres_low, gin_r, sums, hook=None):
    gain = gb_ref[0:1, :]

    def step(i, carry):
        for j in range(2):
            here = rows_at(2 * i + j)
            grad_act = mm_t(gqkv[here, 0 : 3 * sz.width], w_qkv[...])
            norm, inverse = normed(xr[here, :].astype(F32))
            sums[0] += eight_rows(grad_act * norm)
            sums[1] += eight_rows(grad_act)
            grad = (gres_low[here, :].astype(F32) + norm_back(grad_act, norm, inverse, gain)).astype(BF16)
            cuts = BLOCK // CUT
            gin_r[pl.ds((2 * i + j) * cuts, cuts)] = grad.reshape(cuts, CUT, sz.width)
        if hook:
            hook(i)
        return carry

    lax.fori_loop(0, sz.rows // (2 * BLOCK), step, 0)


def place():
    z, f = lax.axis_index("dp"), lax.axis_index("fsdp")
    core, across, up = f % 2, (f // 2) % 2, f // 4
    return z, f, f + 1 - 2 * core, f + 2 - 4 * across, f + 4 - 8 * up


def shifted_rows(source, off, odd, count, first):
    low = source[pl.ds(off + first, count), :]
    high = source[pl.ds(off + first + 1, count), :]
    lane = lax.broadcasted_iota(jnp.int32, (count, HEAD), 1)
    turned = jnp.where(lane < HEAD // 2, pltpu.roll(low, HEAD // 2, 1), pltpu.roll(high, HEAD // 2, 1))
    return jnp.where(odd, turned, low)


class Link:
    def __init__(self, layout, send_sem, recv_sem):
        self.layout, self.send_sem, self.recv_sem = layout, send_sem, recv_sem
        self.z, self.f, self.mate, self.fx, self.fy = place()
        self.fd = self.fx + self.fy - self.f
        self.ways = [self.f, self.fx, self.fy, self.fd]
        self.k = self.z * PLANE + self.f
        self.sent, self.finished, self.slots = [], 0, 0

    def new_slots(self, count):
        self.slots += count
        return self.slots - count

    def new_send(self, ref, condition=None):
        self.sent.append((ref, condition))
        return len(self.sent) - 1

    def start(self, src, dst, index, slot, target):
        pltpu.make_async_remote_copy(
            src_ref=src, dst_ref=dst, send_sem=self.send_sem.at[index], recv_sem=self.recv_sem.at[slot],
            device_id=target, device_id_type=MESH,
        ).start()

    def copy(self, src, dst, slot, target, like, condition=None):
        index = self.new_send(like, condition)
        self.when(condition, lambda: self.start(src, dst, index, slot, target))

    def wait(self, ref, slot, condition=None):
        self.when(condition, lambda: pltpu.make_async_copy(ref, ref, self.recv_sem.at[slot]).wait())

    @staticmethod
    def when(condition, act):
        if condition is None:
            act()
        else:
            pl.when(condition())(act)

    def finish(self):
        for index in range(self.finished, len(self.sent)):
            ref, condition = self.sent[index]
            self.when(condition, lambda: pltpu.make_async_copy(ref, ref, self.send_sem.at[index]).wait())
        self.finished = len(self.sent)

    def meet(self):
        step = 1 - 2 * ((self.k + 1) % 2)
        edge = jnp.clip(self.k + step, 0, DEVICES - 1)
        has_edge = (self.k > 0) & (self.k < DEVICES - 1)
        barrier = pltpu.get_barrier_semaphore()
        partners = [((self.z + t) % LINE, self.f) for t in (1, 2, 3)]
        partners += [(self.z, self.mate), (self.z, self.fx), (self.z, self.fy)]
        for who in partners:
            pl.semaphore_signal(barrier, inc=1, device_id=who, device_id_type=MESH)

        @pl.when(has_edge)
        def _():
            pl.semaphore_signal(barrier, inc=1, device_id=(edge // PLANE, edge % PLANE), device_id_type=MESH)

        pl.semaphore_wait(barrier, len(partners) + has_edge.astype(jnp.int32))

    def tell(self, sem):
        for who in (self.mate, self.fx, self.fy):
            pl.semaphore_signal(sem, inc=1, device_id=(self.z, who), device_id_type=MESH)

        @pl.when(self.z % 2 == 0)
        def _():
            sender = jnp.where(self.z == 0, 2, 3)
            pl.semaphore_signal(sem, inc=1, device_id=(sender, self.f), device_id_type=MESH)

        @pl.when(self.z == 2)
        def _():
            pl.semaphore_signal(sem, inc=1, device_id=(1, self.f), device_id_type=MESH)

    def told(self, sem):
        pl.semaphore_wait(sem, 3 + (self.z > 0).astype(jnp.int32))


class Gather:
    def __init__(self, link, mats, gains, gain_send, gain_recv):
        self.link, self.layout, self.mats, self.gains = link, link.layout, mats, gains
        self.gain_send, self.gain_recv, self.gain_sent = gain_send, gain_recv, []
        self.first = link.new_slots(5 * PIECES)
        self.later = {s: link.new_slots(9) for s in range(1, LINE)}

    def is_first(self, way, condition):
        first = self.link.ways[way] == 0
        return first if condition is None else first & condition()

    def send_gains(self, way, target, condition=None):
        index = len(self.gain_sent)
        self.gain_sent.append((way, condition))

        @pl.when(self.is_first(way, condition))
        def _():
            pltpu.make_async_remote_copy(
                src_ref=self.gains, dst_ref=self.gains, send_sem=self.gain_send.at[index], recv_sem=self.gain_recv,
                device_id=target, device_id_type=MESH,
            ).start()

    def wait_gains(self, way, condition=None):
        pl.when(self.is_first(way, condition))(lambda: pltpu.make_async_copy(self.gains, self.gains, self.gain_recv).wait())

    def piece(self, f, p):
        n = self.layout.pieces[0][0][2] // PIECES
        return self.mats[0].at[pl.ds(pl.multiple_of(f * (n * PIECES) + p * n, 8), n), :]

    def send_piece(self, of, p, way, target, condition=None):
        ref = self.piece(self.link.ways[of], p)
        self.link.copy(ref, ref, self.first + way * PIECES + p, target, self.piece(0, 0), condition)
        if p == 0:
            self.send_gains(of, target, condition)

    def wait_piece(self, of, p, way, condition=None):
        self.link.wait(self.piece(0, 0), self.first + way * PIECES + p, condition)
        if p == 0:
            self.wait_gains(of, condition)

    def along(self, p):
        link = self.link
        self.wait_piece(0, p, 0, lambda: link.z > 0)
        self.send_piece(0, p, 0, (jnp.minimum(link.z + 1, LINE - 1), link.f), lambda: link.z < LINE - 1)
        self.send_piece(0, p, 1, (link.z, link.fx))
        self.send_piece(0, p, 2, (link.z, link.fy))

    def across(self, p):
        link = self.link
        self.wait_piece(1, p, 1)
        if p < PIECES // 2:
            self.send_piece(1, p, 3, (link.z, link.fy))
        self.wait_piece(2, p, 2)
        if p >= PIECES // 2:
            self.send_piece(2, p, 3, (link.z, link.fx))

    def whole(self, f):
        n = self.layout.pieces[0][0][2]
        return self.mats[0].at[pl.ds(pl.multiple_of(f * n, 16), n), :]

    def first_to_mate(self, way):
        link = self.link
        if way == 3:
            for p in range(PIECES):
                self.wait_piece(3, p, 3)
        ref = self.whole(link.ways[way])
        link.copy(ref, ref, self.first + 4 * PIECES + way, (link.z, link.mate), self.whole(0))
        self.send_gains(way, (link.z, link.mate))

    def first_from_mate(self):
        for way in range(4):
            self.link.wait(self.whole(0), self.first + 4 * PIECES + way)
        pl.when(self.link.f % 2 == 1)(lambda: pltpu.make_async_copy(self.gains, self.gains, self.gain_recv).wait())

    def some(self, s, f, half):
        rows = self.layout.flat_rows // self.layout.blocks[0]
        return self.mats[0].at[pl.ds(0, rows if half is None else rows // 2), :]

    def send_part(self, s, f, slot, target, half=None, condition=None):
        link = self.link
        index = link.new_send(self.some(s, f, half), condition)

        def go(pieces):
            for m, r, n, _ in pieces if half is None else self.layout.halves(pieces)[half]:
                ref = self.mats[m].at[pl.ds(r, n), :]
                link.start(ref, ref, index, self.slot_of(s, slot), target)

        link.when(condition, lambda: self.layout.each_kind(s * PLANE + f, go))

    def slot_of(self, s, slot):
        return self.later[1] + (s - 1) * 9 + slot

    def wait_part(self, s, slot, half=None, condition=None):
        self.link.wait(self.some(s, 0, half), self.slot_of(s, slot), condition)

    def over_links(self, s, condition=None):
        link = self.link
        self.send_part(s, link.f, 1, (link.z, link.fx), None, condition)
        self.send_part(s, link.f, 2, (link.z, link.fy), None, condition)
        self.send_part(s, link.f, 5, (link.z, link.mate), None, condition)

    def start_later(self):
        link = self.link
        self.over_links(link.z, lambda: link.z > 0)
        for t in (1, 2, 3):
            target = jnp.maximum(link.z - t, 0)
            self.send_part(link.z, link.f, 0, (target, link.f), None, lambda t=t: link.z >= jnp.maximum(t, 1))

    def start_upward(self):
        link = self.link
        for t in (1, 2):
            target = jnp.minimum(link.z + t, LINE - 1)
            self.send_part(link.z, link.f, 0, (target, link.f), None, lambda t=t: (link.z > 0) & (link.z + t < LINE))

    def line(self, s):

        def elsewhere():
            return self.link.z != s

        self.wait_part(s, 0, None, elsewhere)
        self.over_links(s, elsewhere)

    def corner(self, s):
        link = self.link
        self.wait_part(s, 1)
        self.send_part(s, link.fx, 3, (link.z, link.fy), 0)
        self.send_part(s, link.fx, 6, (link.z, link.mate))
        self.wait_part(s, 2)
        self.send_part(s, link.fy, 4, (link.z, link.fx), 1)
        self.send_part(s, link.fy, 7, (link.z, link.mate))

    def far(self, s):
        link = self.link
        self.wait_part(s, 3, 0)
        self.wait_part(s, 4, 1)
        self.send_part(s, link.fd, 8, (link.z, link.mate))

    def mates(self, s):
        for slot in (5, 6, 7, 8):
            self.wait_part(s, slot)

    def finish(self):
        for index, (way, condition) in enumerate(self.gain_sent):
            pl.when(self.is_first(way, condition))(lambda: pltpu.make_async_copy(self.gains, self.gains, self.gain_send.at[index]).wait())


class Scatter:
    def __init__(self, link, parts, room, line_in, chain_in, small, small_in):
        self.link, self.layout, self.parts, self.room, self.line_in = link, link.layout, parts, room, line_in
        self.chain_in, self.small, self.small_in = chain_in, small, small_in
        self.flip = link.mate - link.f
        self.slot = {s: link.new_slots(8) for s in range(LINE)}
        self.line_slot, self.tail_slot, self.small_slot = link.new_slots(LINE), link.new_slots(6 * PIECES), link.new_slots(3 + LINE)
        self.piece_rows = self.layout.flat_rows // PIECES

    def part(self, s, f):
        rows = self.layout.flat_rows
        return self.parts.at[pl.ds(pl.multiple_of((s * PLANE + f) * rows, rows), rows), :]

    def like(self, size=None):
        return self.parts.at[pl.ds(0, self.layout.flat_rows if size is None else size), :]

    def buffer(self, s, index, lo=0, size=None):
        rows = self.layout.flat_rows
        ref, base = self.room(s)
        return ref.at[pl.ds(base + index * rows + lo, rows if size is None else size), :]

    def line_buffer(self, z, lo=0, size=None):
        rows = self.layout.flat_rows
        ref, base = self.line_in
        return ref.at[pl.ds(pl.multiple_of(base + z * rows + lo, 16), rows if size is None else size), :]

    def chain_buffer(self, index):
        ref, base = self.chain_in
        rows = self.layout.flat_rows
        return ref.at[pl.ds(base + index * rows, rows), :]

    def share(self, s):
        link = self.link
        for way in (3, 2, 1, 0):
            link.copy(self.part(s, link.ways[way] + self.flip), self.buffer(s, way), self.slot[s] + way, (link.z, link.mate), self.like())

    def add(self, into, terms):
        step = 96

        def body(i, carry):
            here = pl.ds(pl.multiple_of(i * step, step), step)
            total = into[here, :].astype(F32)
            for ref in terms:
                total = total + ref[here, :].astype(F32)
            into[here, :] = total.astype(BF16)
            return carry

        lax.fori_loop(0, into.shape[0] // step, body, 0, unroll=2)

    def mated(self, s, way):
        self.link.wait(self.buffer(s, way), self.slot[s] + way)

    def corner(self, s):
        link, half = self.link, self.layout.flat_rows // 2
        self.mated(s, 3)
        own = self.part(s, link.fd)
        for cut, target in ((0, link.fx), (1, link.fy)):
            some = own.at[pl.ds(cut * half, half), :]
            self.add(some, [self.buffer(s, 3, cut * half, half)])
            link.copy(some, self.buffer(s, 4, cut * half, half), self.slot[s] + 4 + cut, (link.z, target), self.like(half))

    def side(self, s):
        link, half = self.link, self.layout.flat_rows // 2
        for way, cut, f, target in ((2, 0, link.fy, link.fy), (1, 1, link.fx, link.fx)):
            self.mated(s, way)
            own = self.part(s, f)
            for now in (1 - cut, cut):
                some = own.at[pl.ds(now * half, half), :]
                terms = [self.buffer(s, way, now * half, half)]
                if now == cut:
                    corner = self.buffer(s, 4, cut * half, half)
                    link.wait(corner, self.slot[s] + 4 + cut)
                    terms.append(corner)
                self.add(some, terms)
            link.copy(own, self.buffer(s, 4 + way), self.slot[s] + 5 + way, (link.z, target), self.like())

    def sided(self, s):
        link = self.link
        self.mated(s, 0)
        for way in (1, 2):
            link.wait(self.buffer(s, 4 + way), self.slot[s] + 5 + way)

    def line(self, s):
        link = self.link
        self.sided(s)
        own = self.part(s, link.f)

        @pl.when(link.z != s)
        def _():
            self.add(own, [self.buffer(s, 0), self.buffer(s, 5), self.buffer(s, 6)])

        link.copy(own, self.line_buffer(link.z), self.line_slot + link.z, (s, link.f), self.like(), lambda: link.z != s)

    def piece_of(self, ref, p):
        return ref.at[pl.ds(p * self.piece_rows, self.piece_rows), :]

    def pass_on(self, own, way, p, into, target, condition=None):
        like, slot = self.like(self.piece_rows), self.tail_slot + way * PIECES + p
        self.link.copy(self.piece_of(own, p), self.piece_of(into, p), slot, target, like, condition)

    def passed(self, way, p):
        self.link.wait(self.like(self.piece_rows), self.tail_slot + way * PIECES + p)

    def add_piece(self, own, p, others):
        self.add(self.piece_of(own, p), [self.piece_of(ref, p) for ref in others])

    def tail_corner(self):
        link, half = self.link, PIECES // 2
        self.mated(0, 3)
        own = self.part(0, link.fd)
        for p in range(PIECES):
            self.add_piece(own, p, [self.buffer(0, 3)])
            self.pass_on(own, 0, p, self.buffer(0, 4), (link.z, link.fx if p < half else link.fy))
        for way, pieces, f in ((2, range(half, PIECES), link.fy), (1, range(half), link.fx)):
            self.mated(0, way)
            own = self.part(0, f)
            for p in pieces:
                self.add_piece(own, p, [self.buffer(0, way)])
                self.pass_on(own, way, p, self.buffer(0, 4 + way), (link.z, f))

    def tail_side(self):
        link, half = self.link, PIECES // 2
        for j in range(half):
            for way, p, f in ((2, j, link.fy), (1, half + j, link.fx)):
                own = self.part(0, f)
                self.passed(0, p)
                self.add_piece(own, p, [self.buffer(0, way), self.buffer(0, 4)])
                self.pass_on(own, way, p, self.buffer(0, 4 + way), (link.z, f))

    def tail_sum(self, p, others=()):
        self.passed(1, p)
        self.passed(2, p)
        own = self.part(0, self.link.f)
        self.add_piece(own, p, [self.buffer(0, 0), self.buffer(0, 5), self.buffer(0, 6), *others])


    ORDER = tuple(p for j in range(PIECES // 2) for p in (j, j + PIECES // 2))

    def leaf(self):
        link = self.link
        self.mated(0, 0)
        for p in self.ORDER:
            pl.when(link.z % 2 == 1)(lambda: self.tail_sum(p))
            own, target = self.part(0, link.f), (2, link.f)
            self.pass_on(own, 3, p, self.chain_buffer(0), target, lambda: link.z == 1)
            self.pass_on(own, 4, p, self.chain_buffer(1), target, lambda: link.z == 3)

    def middle(self):
        link = self.link
        for p in self.ORDER:

            @pl.when(link.z == 2)
            def _():
                self.passed(3, p)
                self.passed(4, p)
                self.tail_sum(p, (self.chain_buffer(0), self.chain_buffer(1)))

            self.pass_on(self.part(0, link.f), 5, p, self.chain_buffer(0), (0, link.f), lambda: link.z == 2)

    def total(self, out):
        link, rows, step = self.link, self.layout.flat_rows, 96

        def sum_of(refs):
            def body(i, carry):
                here = pl.ds(pl.multiple_of(i * step, step), step)
                total = refs[0][here, :].astype(F32)
                for ref in refs[1:]:
                    total = total + ref[here, :].astype(F32)
                out[here, :] = total
                return carry

            lax.fori_loop(0, rows // step, body, 0, unroll=2)

        for s in range(LINE):
            refs = [self.part(s, link.f), self.buffer(s, 0), self.buffer(s, 5), self.buffer(s, 6)]
            if s == 0:
                refs.append(self.chain_buffer(0))
            else:
                refs += [self.line_buffer(z) for z in range(LINE) if z != s]

            @pl.when(link.z == s)
            def _():
                for z in range(LINE):
                    if s and z != s:
                        link.wait(self.line_buffer(z), self.line_slot + z)
                if s == 0:
                    for p in self.ORDER:
                        for way in (1, 2, 5):
                            self.passed(way, p)
                sum_of(refs)

    def small_send(self, stage):
        link = self.link
        if stage < 3:
            target = (link.z, (link.mate, link.fx, link.fy)[stage])
            link.copy(self.small.at[stage], self.small_in.at[stage], self.small_slot + stage, target, self.small.at[0])
        else:
            for t in (1, 2, 3):
                target = ((link.z + t) % LINE, link.f)
                link.copy(self.small.at[3], self.small_in.at[3 + link.z], self.small_slot + 3 + link.z, target, self.small.at[0])

    def small_add(self, stage):
        link = self.link
        if stage < 3:
            link.wait(self.small_in.at[stage], self.small_slot + stage)
            self.small[stage + 1] = self.small[stage] + self.small_in[stage]
        else:
            for t in (1, 2, 3):
                z = (link.z + t) % LINE
                link.wait(self.small_in.at[3 + z], self.small_slot + 3 + z)
            self.small_in[pl.ds(3 + link.z, 1)] = self.small[pl.ds(3, 1)]
            self.small[4] = (self.small_in[3] + self.small_in[4]) + (self.small_in[5] + self.small_in[6])


def edge_copy(layout, k, shard, edge, edge_sems):
    before = jnp.maximum(k - 1, 0)
    return pltpu.make_async_remote_copy(
        src_ref=shard.at[pl.ds(0, HALO), :], dst_ref=edge, send_sem=edge_sems.at[0], recv_sem=edge_sems.at[1],
        device_id=(before // PLANE, before % PLANE), device_id_type=MESH,
    )


def own_part(layout, k, chunk, edge, flat, mats, send):
    rows, half = layout.flat_rows, HEAD // 2
    pl.when(k < DEVICES - 1)(lambda: send.wait_recv())
    lane = lax.broadcasted_iota(jnp.int32, (HALO, HEAD), 1)
    row = lax.broadcasted_iota(jnp.int32, (HALO, HEAD), 0)
    turned = pltpu.roll(edge[...], half, 1)
    last = jnp.broadcast_to(chunk[pl.ds(rows, 1), :], (HALO, HEAD))
    down = jnp.where(row == 0, last, pltpu.roll(turned, 1, 0))
    chunk[pl.ds(rows, HALO), :] = jnp.where(lane < half, down, turned)
    off, odd = (DEVICES - k) // 2, (DEVICES - k) % 2 == 1
    step = 96
    for i in range(0, rows, step):
        flat[pl.ds(i, step), :] = shifted_rows(chunk, off, odd, step, i)

    def put(pieces):
        for m, r, n, f in pieces:
            blocks = layout.blocks[m]
            for c in range(blocks):
                mats[m][pl.ds(r, n), c * HEAD : (c + 1) * HEAD] = flat[pl.ds(f + c, n, stride=blocks), :].astype(BF16)

    layout.each_kind(k, put)
    pl.when(k > 0)(lambda: send.wait_send())


def own_rows(layout, k, total, small, flat, edge, edge_sems):
    rows, out = layout.flat_rows, total

    def put(pieces):
        for m, _, n, f in pieces:
            blocks = layout.blocks[m]
            for c in range(blocks):
                flat[pl.ds(HALO + f + c, n, stride=blocks), :] = total[pl.ds(f + c * n, n), :]

    layout.each_kind(k, put)
    after = jnp.minimum(k + 1, DEVICES - 1)
    send = pltpu.make_async_remote_copy(
        src_ref=flat.at[pl.ds(rows, HALO), :], dst_ref=edge, send_sem=edge_sems.at[0], recv_sem=edge_sems.at[1],
        device_id=(after // PLANE, after % PLANE), device_id_type=MESH,
    )
    pl.when(k < DEVICES - 1)(lambda: send.start())

    @pl.when(k == 0)
    def _():
        across = layout.width // HEAD
        for t in range(4):
            for c in range(across):
                flat[t * across + c : t * across + c + 1, :] = small[t : t + 1, c * HEAD : (c + 1) * HEAD]

    @pl.when(k > 0)
    def _():
        send.wait_recv()
        flat[pl.ds(0, HALO), :] = edge[...]

    step = 8 * 97
    for i in range(0, rows + 8, step):
        out[pl.ds(i, step), :] = shifted_rows(flat, k // 2, k % 2 == 1, step, i)
    pl.when(k < DEVICES - 1)(lambda: send.wait_send())


class Steps:
    heads_hook = down_hook = forward_hook = small_forward_hook = backward_hook = small_backward_hook = input_hook = None

    def nothing(self, *args):
        pass

    enter = first_weights = up_weights = down_weights = pool_free = nothing
    up_done = qkv_done = before_output = between_outputs = close = nothing


def layer_body(sz, layout, steps, len_ref, sup_ref, x_hbm, cot_hbm, out_hbm, gin_hbm, gb_ref, work, io_sem):
    (xr, cr, act2_t, cot_t, qkv, exps_big, exps_small, ctx, ctx_t, hid, pool, gres_low, dox, parts,
     resid, qm, km, inv_ref, sums, w_qkv, w_out, w_up, w_down, x_cuts, c_cuts) = work
    width = sz.width
    load_x = pltpu.make_async_copy(x_hbm, x_cuts, io_sem.at[0])
    load_c = pltpu.make_async_copy(cot_hbm, c_cuts, io_sem.at[1])
    load_x.start()
    load_c.start()
    shift, begins, sups = table_facts(sz, len_ref, sup_ref)

    def masks():
        mask_features(sz, begins, sups, qm, km)
        sums[...] = jnp.zeros_like(sums)

    def set_rows(ref):
        def write(rows, values):
            ref[rows, :] = values

        return write

    def before_weights():
        masks()
        load_x.wait()
        roll_rows(sz, shift, x_cuts, set_rows(xr))

    steps.enter(before_weights)

    def take_cotangent():
        load_c.wait()
        roll_rows(sz, shift, c_cuts, set_rows(cr))
        for i in range(sz.rows // TALL):
            cot_t[:, i * TALL : (i + 1) * TALL] = cr[i * TALL : (i + 1) * TALL, :].T

    steps.first_weights(take_cotangent)
    phase_qkv(sz, gb_ref, xr, x_cuts, w_qkv, qkv)
    attend_forward(sz, 0, sz.big_keys, sz.big, exps_big, qkv, qm, km, ctx, ctx_t, inv_ref, steps.forward_hook)
    attend_forward(sz, sz.big, sz.small, sz.small, exps_small, qkv, qm, km, ctx, ctx_t, inv_ref, steps.small_forward_hook)
    steps.up_weights()
    phase_up(sz, gb_ref, xr, ctx, w_out, w_up, act2_t, hid, pool, resid)
    weight_grad_turned(layout, 3, cot_t, lambda i: hid[:, rows_at(i)], parts)
    steps.down_weights()
    out_r, gin_r, gqkv, act1_t = c_cuts, x_cuts, hid, cot_t
    phase_down(sz, gb_ref, cr, w_up, w_down, hid, pool, resid, out_r, gres_low, sums, steps.down_hook)
    per = BLOCK // HEAD
    weight_grad(
        layout, 2, act2_t,
        lambda i: jnp.concatenate([pool[pool_at(sz, i * per + c, 0, sz.rows), :] for c in range(per)], axis=1), parts,
    )
    steps.pool_free()
    weight_grad(layout, 1, ctx_t, lambda i: gres_low[:, rows_at(i)], parts)
    for i in range(sz.rows // CUT):
        act1_t[:, i * CUT : (i + 1) * CUT] = x_cuts[i].T
    steps.up_done()
    phase_heads(sz, ctx, inv_ref, w_out, gres_low, dox, steps.heads_hook)
    gqkv[sz.big_keys : sz.big, width : 3 * width] = jnp.zeros((sz.big - sz.big_keys, 2 * width), BF16)
    attend_backward(sz, 0, sz.big_keys, sz.big, exps_big, qkv, dox, gqkv, steps.backward_hook)
    attend_backward(sz, sz.big, sz.small, sz.small, exps_small, qkv, dox, gqkv, steps.small_backward_hook)
    weight_grad(layout, 0, act1_t, lambda i: gqkv[:, rows_at(i)], parts)
    steps.qkv_done()
    phase_input(sz, gb_ref, xr, gqkv, w_qkv, gres_low, gin_r, sums, steps.input_hook)
    steps.before_output()
    back = lax.rem(sz.rows - shift, sz.rows)
    roll_rows(sz, back, out_r, set_rows(ctx))
    store_out = pltpu.make_async_copy(ctx, out_hbm, io_sem.at[0])
    store_out.start()
    steps.between_outputs()
    roll_rows(sz, back, gin_r, set_rows(xr))
    store_gin = pltpu.make_async_copy(xr, gin_hbm, io_sem.at[1])
    store_gin.start()
    steps.close()
    store_out.wait()
    store_gin.wait()


def small_terms(sums, out):
    for t in range(4):
        out[t : t + 1, :] = jnp.sum(sums[t], axis=0, keepdims=True)


def work_shapes(sz, layout):
    rows, width, ffn = sz.rows, sz.width, sz.ffn

    def low(*shape):
        return pltpu.VMEM(shape, BF16)

    return [
        low(rows, width), low(rows, width), low(width, rows), low(width, rows), low(rows, 3 * width),
        low(sz.heads, sz.big_keys, sz.big), low(sz.heads, sz.small, sz.small), low(rows, width), low(width, rows),
        low(rows, ffn), low(rows * ffn // HEAD, HEAD), low(rows, width), low(sz.heads, rows, 2 * HEAD),
        low(layout.flat_rows * DEVICES, HEAD), pltpu.VMEM((rows, width), F32), low(rows, HEAD), low(rows, HEAD),
        pltpu.VMEM((sz.heads, 8, rows), F32), pltpu.VMEM((4, 8, width), F32),
        low(width, 3 * width), low(width, width), low(width, ffn), low(ffn, width),
        low(rows // CUT, CUT, width), low(rows // CUT, CUT, width),
    ]


WORK = 25
VMEM_LIMIT = 63 * 2**20 + 3 * 2**18


def plain_kernel(sz, layout, len_ref, sup_ref, x_hbm, cot_hbm, gb_ref, *rest):
    weights, (out_hbm, gin_hbm, parts_hbm, small_ref), rest = rest[:4], rest[4:8], rest[8:]
    work, (load_sem, io_sem) = rest[:WORK], rest[WORK:]
    parts, sums, mats = work[13], work[18], work[19:23]
    steps = Steps()
    loads = [pltpu.make_async_copy(src, dst, load_sem.at[i]) for i, (src, dst) in enumerate(zip(weights, mats))]
    store = pltpu.make_async_copy(parts, parts_hbm, load_sem.at[4])

    def enter(fill):
        for copy in loads:
            copy.start()
        fill()

    def first_weights(fill):
        fill()
        loads[0].wait()

    def up_weights():
        for copy in loads[1:]:
            copy.wait()

    def close():
        small_terms(sums, small_ref)
        store.wait()

    steps.enter, steps.first_weights, steps.up_weights = enter, first_weights, up_weights
    steps.qkv_done, steps.close = store.start, close
    layer_body(sz, layout, steps, len_ref, sup_ref, x_hbm, cot_hbm, out_hbm, gin_hbm, gb_ref, work, io_sem)


def cuts_of(values):
    return values.reshape(values.shape[0] // CUT, CUT, values.shape[1])


def layer(x_in, cotangent, lengths, support, gains, w_qkv, w_out, w_up, w_down):
    rows, width = x_in.shape
    ffn = w_up.shape[1]
    sz, layout = Shapes(rows, width, ffn), Layout(width, ffn)
    anywhere = pl.BlockSpec(memory_space=pl.ANY)
    vmem = pl.BlockSpec(memory_space=pltpu.VMEM)
    smem = pl.BlockSpec(memory_space=pltpu.SMEM)
    return pl.pallas_call(
        functools.partial(plain_kernel, sz, layout),
        out_shape=(
            jax.ShapeDtypeStruct((rows, width), BF16),
            jax.ShapeDtypeStruct((rows, width), BF16),
            jax.ShapeDtypeStruct((layout.flat_rows * DEVICES, HEAD), BF16),
            jax.ShapeDtypeStruct((4, width), F32),
        ),
        in_specs=[smem, smem, anywhere, anywhere, vmem, anywhere, anywhere, anywhere, anywhere],
        out_specs=[anywhere] * 3 + [vmem],
        scratch_shapes=work_shapes(sz, layout) + [pltpu.SemaphoreType.DMA((5,)), pltpu.SemaphoreType.DMA((2,))],
        compiler_params=pltpu.CompilerParams(vmem_limit_bytes=VMEM_LIMIT),
    )(lengths, support, cuts_of(x_in), cuts_of(cotangent), gains, w_qkv, w_out, w_up, w_down)


SENDS = 288
SLOTS = 208
ROOM = 7


HEADS_PLAN = {1: [("corner", 2)], 2: [("corner", 1)]}
BACKWARD_PLAN = {1: [("side", 2)], 2: [("side", 1)]}
SMALL_PLAN = {3: [("line", 2)]}


def planned(scatter, plan):
    return {step: [(getattr(scatter, way), s) for way, s in acts] for step, acts in plan.items()}


def whole_kernel(sz, layout, len_ref, sup_ref, x_hbm, cot_hbm, shard, out_hbm, gin_hbm, own_out, small_out, *rest):
    work, rest = rest[:WORK], rest[WORK:]
    (gb_ref, chunk, flat, edge, gains, extra, small, small_in,
     send_sem, recv_sem, gain_send, gain_recv, edge_sems, out_edge_sems, load_sem, io_sem, ready_sem) = rest
    pool, parts, sums, mats = work[10], work[13], work[18], work[19:23]
    rows = layout.flat_rows
    link = Link(layout, send_sem, recv_sem)
    gather = Gather(link, mats, gains, gain_send, gain_recv)
    scatter = Scatter(
        link, parts, lambda s: (extra, 0) if s == LINE - 1 else (pool, s * ROOM * rows), (extra, ROOM * rows),
        (pool, (LINE - 1) * ROOM * rows), small, small_in,
    )
    steps = Steps()

    def at(index, table):
        for number, acts in table.items():

            @pl.when(index == number)
            def _():
                for act, s in acts:
                    act(s)

    def enter(fill):
        rows_of(shard, chunk)
        link.meet()
        send = edge_copy(layout, link.k, chunk, edge, edge_sems)
        pl.when(link.k > 0)(lambda: send.start())

        @pl.when(link.k == 0)
        def _():
            gains[...] = chunk[pl.ds(0, HALO), :].astype(BF16).astype(F32)

        fill()
        own_part(layout, link.k, chunk, edge, flat, mats, send)
        gather.start_later()

    def first_weights(fill):
        pl.when(link.z >= LINE // 2)(fill)
        for p in range(PIECES):
            gather.along(p)
        gather.first_to_mate(0)
        gather.start_upward()
        for p in range(PIECES):
            gather.across(p)
        gather.first_to_mate(1)
        gather.first_to_mate(2)
        gather.first_to_mate(3)
        for s in range(1, LINE):
            gather.line(s)
        gather.first_from_mate()
        pl.when(link.z < LINE // 2)(fill)
        across = layout.width // HEAD
        for t in range(4):
            for c in range(across):
                gb_ref[t : t + 1, c * HEAD : (c + 1) * HEAD] = gains[pl.ds(t * across + c, 1), :]

    def forward_hook(head):
        at(head, {1: [(gather.corner, 1)], 3: [(gather.corner, 2)]})

    def small_forward_hook(head):
        at(head, {1: [(gather.far, 1)], 2: [(gather.corner, 3)], 3: [(gather.far, 2)]})

    def up_weights():
        gather.mates(1)
        gather.mates(2)

    def down_weights():
        scatter.share(3)
        gather.far(3)
        gather.mates(3)

    def down_hook(i):
        at(i, {0: [(scatter.corner, 3)], 1: [(scatter.side, 3)], 2: [(scatter.line, 3)]})

    def pool_free():
        link.tell(ready_sem)

    def up_done():
        link.told(ready_sem)
        scatter.share(2)
        scatter.share(1)

    def heads_hook(i):
        at(i, planned(scatter, HEADS_PLAN))

    def backward_hook(head):
        at(head, planned(scatter, BACKWARD_PLAN))

    def small_backward_hook(head):
        at(head, planned(scatter, SMALL_PLAN))

    def qkv_done():
        scatter.share(0)
        scatter.line(1)

    def input_hook(i):
        at(i, {0: [(lambda s: scatter.tail_corner(), 0)], 2: [(lambda s: scatter.tail_side(), 0)]})

    def before_output():
        small_terms(sums, small.at[0])
        scatter.small_send(0)
        scatter.leaf()
        scatter.small_add(0)
        scatter.small_send(1)

    def between_outputs():
        scatter.small_add(1)
        scatter.small_send(2)
        scatter.middle()
        scatter.small_add(2)
        scatter.small_send(3)

    def close():
        gather.finish()
        link.finish()
        scatter.total(chunk)
        scatter.small_add(3)
        small_out[...] = small[4, 3:4, :]
        own_rows(layout, link.k, chunk, small.at[4], flat, edge, out_edge_sems)
        store = pltpu.make_async_copy(chunk.at[pl.ds(0, rows + 8), :], own_out, load_sem)
        store.start()
        store.wait()

    steps.enter, steps.first_weights, steps.pool_free = enter, first_weights, pool_free
    steps.forward_hook, steps.small_forward_hook, steps.up_weights = forward_hook, small_forward_hook, up_weights
    steps.down_weights, steps.down_hook, steps.up_done = down_weights, down_hook, up_done
    steps.heads_hook = heads_hook
    steps.backward_hook, steps.small_backward_hook, steps.qkv_done = backward_hook, small_backward_hook, qkv_done
    steps.input_hook, steps.before_output, steps.between_outputs, steps.close = input_hook, before_output, between_outputs, close
    layer_body(sz, layout, steps, len_ref, sup_ref, x_hbm, cot_hbm, out_hbm, gin_hbm, gb_ref, work, io_sem)


def rows_of(values, out):
    size, tile = values.shape[0], 8 * HEAD
    for i in range(size // tile):
        out[i * 8 : (i + 1) * 8, :] = values[pl.ds(i * tile, tile)].reshape(8, HEAD)
    done = size // tile * tile
    while done < size:
        count = min(HEAD, size - done)
        out[done // HEAD : done // HEAD + 1, 0:count] = values[pl.ds(done, count)].reshape(1, count)
        done += count


def whole_layer(layout, x_in, cotangent, lengths, support, master):
    rows, width = x_in.shape
    sz = Shapes(rows, width, layout.ffn)
    anywhere = pl.BlockSpec(memory_space=pl.ANY)
    vmem = pl.BlockSpec(memory_space=pltpu.VMEM)
    smem = pl.BlockSpec(memory_space=pltpu.SMEM)
    dma = pltpu.SemaphoreType.DMA
    part = layout.flat_rows
    return pl.pallas_call(
        functools.partial(whole_kernel, sz, layout),
        out_shape=(
            jax.ShapeDtypeStruct((rows, width), BF16),
            jax.ShapeDtypeStruct((rows, width), BF16),
            jax.ShapeDtypeStruct((part + 8, HEAD), F32),
            jax.ShapeDtypeStruct((1, width), F32),
        ),
        in_specs=[smem, smem, anywhere, anywhere, vmem],
        out_specs=[anywhere] * 3 + [vmem],
        scratch_shapes=work_shapes(sz, layout) + [
            pltpu.VMEM((4, width), F32), pltpu.VMEM((part + 3 * HALO, HEAD), F32), pltpu.VMEM((part + 2 * HALO, HEAD), F32),
            pltpu.VMEM((HALO, HEAD), F32), pltpu.VMEM((HALO, HEAD), F32), pltpu.VMEM(((ROOM + LINE) * part, HEAD), BF16),
            pltpu.VMEM((5, 4, width), F32), pltpu.VMEM((3 + LINE, 4, width), F32),
            dma((SENDS,)), dma((SLOTS,)), dma((64,)), dma, dma((2,)), dma((2,)), dma, dma((2,)),
            pltpu.SemaphoreType.REGULAR,
        ],
        compiler_params=pltpu.CompilerParams(collective_id=0, has_side_effects=True, vmem_limit_bytes=VMEM_LIMIT),
    )(lengths, support, cuts_of(x_in), cuts_of(cotangent), master)


CARRIERS = 4


def hand_over_kernel(count, *refs):
    sources, targets, (held, semaphores) = refs[:count], refs[count : 2 * count], (refs[2 * count : 3 * count], refs[3 * count :])
    pairs = []
    for src, dst, mid in zip(sources, targets, held):
        step = max(src.shape[0] // CARRIERS, 1)
        for i in range(0, src.shape[0], step):
            some, index = pl.ds(i, step), len(pairs)
            pairs.append((
                pltpu.make_async_copy(src.at[some, :], mid.at[some, :], semaphores[0].at[index]),
                pltpu.make_async_copy(mid.at[some, :], dst.at[some, :], semaphores[1].at[index]),
            ))
    for load, _ in pairs:
        load.start()
    for load, store in pairs:
        load.wait()
        store.start()
    for _, store in pairs:
        store.wait()


def hand_over(*arrays):
    anywhere = pl.BlockSpec(memory_space=pl.ANY)
    dma = pltpu.SemaphoreType.DMA((CARRIERS * len(arrays),))
    return pl.pallas_call(
        functools.partial(hand_over_kernel, len(arrays)),
        out_shape=tuple(jax.ShapeDtypeStruct(v.shape, v.dtype) for v in arrays),
        in_specs=[anywhere] * len(arrays),
        out_specs=[anywhere] * len(arrays),
        scratch_shapes=[pltpu.VMEM(v.shape, v.dtype) for v in arrays] + [dma, dma],
    )(*arrays)


def adam(grads, first_moment, second_moment, master, step_count):
    step_float = step_count[0].astype(F32)
    new_first = BETA_ONE * first_moment + (1.0 - BETA_ONE) * grads
    new_second = BETA_TWO * second_moment + (1.0 - BETA_TWO) * grads * grads
    first_hat = new_first / (1.0 - jnp.power(F32(BETA_ONE), step_float))
    second_hat = new_second / (1.0 - jnp.power(F32(BETA_TWO), step_float))
    adam_step = first_hat / (jnp.sqrt(second_hat) + ADAM_EPS) + DECAY_RATE * master
    return new_first, new_second, adam_step


def flat_of_parts(layout, parts):
    by_part, flat = parts.reshape(DEVICES, layout.flat_rows, HEAD), []
    for k, own in enumerate(layout.pieces):
        for m, _, n, f in own:
            blocks = layout.blocks[m]
            piece = by_part[k, f : f + n * blocks].reshape(blocks, n, HEAD)
            flat.append(piece.transpose(1, 0, 2).reshape(-1))
    return jnp.concatenate(flat)


def plain_gather(layout, master):
    width, ffn = layout.width, layout.ffn
    flat = lax.all_gather(master.astype(BF16), ("dp", "fsdp"), axis=0, tiled=True)
    shapes = [(4, width), (width, 3 * width), (width, width), (width, ffn), (ffn, width)]
    arrays, start = [], 0
    for shape in shapes:
        arrays.append(flat[start : start + math.prod(shape)].reshape(shape))
        start += math.prod(shape)
    return (*arrays[1:], arrays[0].astype(F32))


def plain_scatter(layout, parts, small):
    axes = ("dp", "fsdp")
    local = jnp.concatenate([small.reshape(-1), flat_of_parts(layout, parts).astype(F32)])
    return lax.psum_scatter(local, axes, scatter_dimension=0, tiled=True), lax.psum(small[3], axes)


def per_device(sizes, x_in, cotangent, table_lengths, support_counts, master, first_moment, second_moment, step_count):
    width, shard = x_in.shape[1], master.shape[0]
    param_count = shard * sizes[0] * sizes[1]
    ffn = (param_count - 4 * width - 4 * width * width) // (2 * width)
    layout = Layout(width, ffn)
    if layout.fits(param_count, sizes):
        output, grad_input, rows, total = whole_layer(layout, x_in, cotangent, table_lengths, support_counts, master)
        output, grad_input, total = hand_over(output, grad_input, total)
        grads, bias_two_grad = rows.reshape(-1)[:shard], total[0]
    else:
        *weights, gains = plain_gather(layout, master)
        output, grad_input, parts, small = layer(x_in, cotangent, table_lengths, support_counts, gains, *weights)
        grads, bias_two_grad = plain_scatter(layout, parts, small)
    new_first, new_second, adam_step = adam(grads, first_moment, second_moment, master, step_count)
    return output, grad_input, grads, new_first, new_second, adam_step, bias_two_grad


def solution(mesh):
    rows, flat = P(("dp", "fsdp"), None), P(("dp", "fsdp"))
    return jax.shard_map(
        functools.partial(per_device, (mesh.shape["dp"], mesh.shape["fsdp"])),
        mesh=mesh,
        in_specs=(rows, rows, rows, rows, flat, flat, flat, P()),
        out_specs=(rows, rows, flat, flat, flat, flat, P()),
        check_vma=False,
    )
```

```python
import functools
import math

import jax
import jax.numpy as jnp
from jax import lax
from jax.experimental import pallas as pl
from jax.experimental.pallas import tpu as pltpu
from jax.sharding import PartitionSpec as P

HEAD = 128
EPS_NORM = 1e-05
BETA_ONE = 0.9
BETA_TWO = 0.999
ADAM_EPS = 1e-08
DECAY_RATE = 0.01
MASKED = -1e30
F32 = jnp.float32
BF16 = jnp.bfloat16
BLOCK = 256
TALL = 512
CUT = 128
GELU_ONE = math.sqrt(2.0 / math.pi)
GELU_THREE = 0.044715


def mm(left, right):
    return jnp.dot(left, right, preferred_element_type=F32)


def mm_t(left, right):
    return lax.dot_general(left, right, (((1,), (1,)), ((), ())), preferred_element_type=F32)


def rows_at(index, size=BLOCK):
    return pl.ds(pl.multiple_of(index * size, size), size)


class Shapes:
    def __init__(self, rows, width, ffn):
        self.rows, self.width, self.ffn = rows, width, ffn
        self.heads = width // HEAD
        self.big = 2 * rows // 3
        self.big_keys = 3 * self.big // 4
        self.small = rows - self.big


MESH = pl.DeviceIdType.MESH
LINE = 4
PLANE = 8
DEVICES = LINE * PLANE
HALO = 16
PIECES = 4


class Layout:
    def __init__(self, width, ffn):
        self.width, self.ffn = width, ffn
        shapes = [(width, 3 * width), (width, width), (width, ffn), (ffn, width)]
        self.blocks = [s[1] // HEAD for s in shapes]
        self.flat_rows = sum(r * c for r, c in shapes) // (HEAD * DEVICES)
        ends, total = [], 0
        for r, c in shapes:
            total += r * c // HEAD
            ends.append(total)
        starts = [0] + ends[:-1]
        self.pieces = []
        for k in range(DEVICES):
            lo, hi, own = k * self.flat_rows, (k + 1) * self.flat_rows, []
            for m in range(4):
                a, b = max(lo, starts[m]), min(hi, ends[m])
                if a < b:
                    own.append((m, (a - starts[m]) // self.blocks[m], (b - a) // self.blocks[m], a - lo))
            self.pieces.append(own)
        self.unit = math.gcd(*(n for own in self.pieces for m, _, n, _ in own if m == 3))
        self.kinds = []
        for k, own in enumerate(self.pieces):
            last = self.kinds[-1] if self.kinds else None
            if last and len(own) == 1 and self.same(self.pieces[last[0]], own):
                last[1] = k + 1
            else:
                self.kinds.append([k, k + 1])

    @staticmethod
    def same(left, right):
        return len(left) == len(right) and all(a[0] == b[0] and a[2:] == b[2:] for a, b in zip(left, right))

    def fits(self, param_count, devices):
        whole = self.flat_rows * HEAD * DEVICES + 4 * self.width
        first = all(len(own) == 1 and own[0][0] == 0 and own[0][2] % (8 * PIECES) == 0 for own in self.pieces[:PLANE])
        exact = all(
            sum(p[2] * self.blocks[p[0]] for p in own) == self.flat_rows and all(p[1] % 8 == 0 and p[2] % 8 == 0 for p in own)
            for own in self.pieces
        )
        return devices == (LINE, PLANE) and exact and first and whole == param_count and 4 * self.width == HALO * HEAD

    def each_kind(self, k, act):
        for lo, hi in self.kinds:
            def run(lo=lo, hi=hi):
                first = self.pieces[lo]
                if hi - lo == 1:
                    act(first)
                else:
                    m, r, n, f = first[0]
                    act([(m, pl.multiple_of(r + (k - lo) * n, 8), n, f)])

            pl.when((k >= lo) & (k < hi))(run)

    def halves(self, pieces):
        goal, done, parts = self.flat_rows // 2, 0, ([], [])
        for m, r, n, f in pieces:
            take = min(n, max(0, (goal - done)) // self.blocks[m])
            if take:
                parts[0].append((m, r, take, f))
            if n - take:
                parts[1].append((m, r + take, n - take, f + take * self.blocks[m]))
            done += take * self.blocks[m]
        return parts


def table_facts(sz, len_ref, sup_ref):
    lengths = [len_ref[0, t] for t in range(4)]
    support = [sup_ref[0, t] for t in range(4)]
    starts = [jnp.int32(0), lengths[0], lengths[0] + lengths[1], lengths[0] + lengths[1] + lengths[2]]
    is_big = [lengths[t] == sz.big for t in range(4)]

    def pick(values):
        total = jnp.int32(0)
        for t in range(4):
            total = total + jnp.where(is_big[t], values[t], 0)
        return total

    shift = pick(starts)
    lens = [pick([lengths[(t + j) % 4] for t in range(4)]) for j in range(4)]
    sups = [pick([support[(t + j) % 4] for t in range(4)]) for j in range(4)]
    begins = [jnp.int32(0), lens[0], lens[0] + lens[1], lens[0] + lens[1] + lens[2]]
    return shift, begins, sups


def mask_features(sz, begins, sups, qm_ref, km_ref):
    def step(i, carry):
        shape = (BLOCK, HEAD)
        row = lax.broadcasted_iota(jnp.int32, shape, 0) + i * BLOCK
        lane = lax.broadcasted_iota(jnp.int32, shape, 1)
        table = jnp.zeros(shape, jnp.int32)
        limit = jnp.full(shape, begins[0] + sups[0], jnp.int32)
        for t in range(1, 4):
            inside = row >= begins[t]
            table = jnp.where(inside, t, table)
            limit = jnp.where(inside, begins[t] + sups[t], limit)
        own = table == lane
        qm_ref[rows_at(i), :] = jnp.where(own, 1.0, 0.0).astype(BF16)
        bad = jnp.where(own, jnp.where(row < limit, 0.0, MASKED), jnp.where(lane < 4, MASKED, 0.0))
        km_ref[rows_at(i), :] = bad.astype(BF16)
        return carry

    lax.fori_loop(0, sz.rows // BLOCK, step, 0, unroll=2)


def roll_rows(sz, shift, source, write):
    blocks = sz.rows // CUT
    coarse, fine = shift // CUT, shift % CUT
    row = lax.broadcasted_iota(jnp.int32, (CUT, 2 * CUT), 0)
    column = lax.broadcasted_iota(jnp.int32, (CUT, 2 * CUT), 1)
    chosen = jnp.where(row + fine == column, 1.0, 0.0).astype(BF16)

    def step(i, carry):
        here = lax.rem(i + coarse, blocks)
        after = lax.rem(i + coarse + 1, blocks)
        pair = jnp.concatenate([source[here], source[after]], axis=0)
        write(rows_at(i, CUT), mm(chosen, pair).astype(BF16))
        return carry

    lax.fori_loop(0, blocks, step, 0, unroll=4)


def normed(values):
    centre = values - jnp.mean(values, axis=-1, keepdims=True)
    inverse = lax.rsqrt(jnp.mean(centre * centre, axis=-1, keepdims=True) + EPS_NORM)
    return centre * inverse, inverse


def norm_back(grad_out, norm, inverse, gain):
    grad_normed = grad_out * gain
    return inverse * (
        grad_normed
        - jnp.mean(grad_normed, axis=-1, keepdims=True)
        - norm * jnp.mean(grad_normed * norm, axis=-1, keepdims=True)
    )


def eight_rows(values):
    rows, width = values.shape
    return jnp.sum(values.reshape(rows // 8, 8, width), axis=0)


def phase_qkv(sz, gb_ref, xr, act_cuts, w_qkv, qkv):
    gain, bias = gb_ref[0:1, :], gb_ref[1:2, :]

    def step(i, carry):
        norm, _ = normed(xr[rows_at(i), :].astype(F32))
        act = (norm * gain + bias).astype(BF16)
        cuts = BLOCK // CUT
        act_cuts[pl.ds(i * cuts, cuts)] = act.reshape(cuts, CUT, sz.width)
        qkv[rows_at(i), :] = mm(act, w_qkv[...]).astype(BF16)
        return carry

    lax.fori_loop(0, sz.rows // BLOCK, step, 0, unroll=2)


def head_at(head, offset=0):
    return pl.ds(pl.multiple_of(offset + head * HEAD, HEAD), HEAD)


def attend_forward(sz, base, key_count, query_count, exps, qkv, qm, km, ctx, ctx_t, inv_ref, hook=None):
    keep = pl.ds(base, key_count)
    here = pl.ds(base, query_count)
    scale = math.log2(math.e) / math.sqrt(HEAD)

    def per_head(head, carry):
        keys = jnp.concatenate([qkv[keep, head_at(head, sz.width)], km[keep, :]], axis=1)
        values_t = qkv[keep, head_at(head, 2 * sz.width)].T
        queries = jnp.concatenate([qkv[here, head_at(head)], qm[here, :]], axis=1)
        scores = mm_t(keys, queries)
        top = jnp.max(scores, axis=0, keepdims=True)
        shifted = jnp.exp2((scores - top) * scale)
        total = jnp.sum(shifted, axis=0, keepdims=True)
        low = shifted.astype(BF16)
        exps[head] = low
        inverse = 1.0 / total
        mixed = (mm(values_t, low) * inverse).astype(BF16)
        ctx_t[head_at(head), here] = mixed
        ctx[here, head_at(head)] = mixed.T
        inv_ref[head, :, here] = jnp.broadcast_to(inverse, (8, query_count))
        if hook:
            hook(head)
        return carry

    lax.fori_loop(0, sz.heads, per_head, 0)


def pool_at(sz, column, start, size):
    return pl.ds(pl.multiple_of(column * sz.rows + start, 256), size)


def phase_up(sz, gb_ref, xr, ctx, w_out, w_up, act_t, hid, pool, resid_ref):
    gain, bias = gb_ref[2:3, :], gb_ref[3:4, :]

    def step(i, carry):
        here = rows_at(i, TALL)
        resid = xr[here, :].astype(F32) + mm(ctx[here, :], w_out[...])
        resid_ref[here, :] = resid
        norm, _ = normed(resid)
        act = (norm * gain + bias).astype(BF16)
        act_t[:, here] = act.T
        for f in range(sz.ffn // BLOCK):
            part = slice(f * BLOCK, (f + 1) * BLOCK)
            pre = mm(act, w_up[:, part])
            square = pre * pre
            bent = jnp.tanh(pre * (GELU_ONE + GELU_ONE * GELU_THREE * square))
            half = 0.5 + 0.5 * bent
            value = pre * half
            hid[here, part] = value.astype(BF16)
            slope = half + value * (1.0 - half) * (2.0 * GELU_ONE + 6.0 * GELU_ONE * GELU_THREE * square)
            slope = slope.astype(BF16)
            for c in range(BLOCK // HEAD):
                pool[pool_at(sz, f * (BLOCK // HEAD) + c, i * TALL, TALL), :] = slope[:, c * HEAD : (c + 1) * HEAD]
        return carry

    lax.fori_loop(0, sz.rows // TALL, step, 0)


def phase_down(sz, gb_ref, cr, w_up, w_down, hid, pool, resid_ref, out_r, gres_low, sums, hook=None):
    gain = gb_ref[2:3, :]

    def step(i, carry):
        here = rows_at(i, TALL)
        cot = cr[here, :]
        resid = resid_ref[here, :]
        norm, inverse = normed(resid)
        grad_pre = []
        for f in range(sz.ffn // BLOCK):
            part = slice(f * BLOCK, (f + 1) * BLOCK)
            grad_hidden = mm_t(cot, w_down[part, :])
            for c in range(BLOCK // HEAD):
                at = pool_at(sz, f * (BLOCK // HEAD) + c, i * TALL, TALL)
                low = (grad_hidden[:, c * HEAD : (c + 1) * HEAD] * pool[at, :].astype(F32)).astype(BF16)
                pool[at, :] = low
                grad_pre.append(low)
        grad_act = mm_t(jnp.concatenate(grad_pre, axis=1), w_up[...])
        total = resid + mm(hid[here, :], w_down[...])
        cuts = TALL // CUT
        out_r[pl.ds(i * cuts, cuts)] = total.astype(BF16).reshape(cuts, CUT, sz.width)
        sums[2] += eight_rows(grad_act * norm)
        sums[3] += eight_rows(grad_act)
        low = (cot.astype(F32) + norm_back(grad_act, norm, inverse, gain)).astype(BF16)
        gres_low[here, :] = low
        if hook:
            hook(i)
        return carry

    lax.fori_loop(0, sz.rows // TALL, step, 0)


def phase_heads(sz, ctx, inv_ref, w_out, gres_low, dox, hook=None):
    def step(i, carry):
        here = rows_at(i, TALL)
        grad_ctx = mm_t(gres_low[here, :], w_out[...]).astype(BF16).astype(F32)
        lane = lax.broadcasted_iota(jnp.int32, (TALL, HEAD), 1)
        for head in range(sz.heads):
            part = slice(head * HEAD, (head + 1) * HEAD)
            column = inv_ref[head, :, here].T[:, 0:1]
            scaled = (grad_ctx[:, part] * column).astype(BF16)
            delta = jnp.sum(scaled.astype(F32) * ctx[here, part].astype(F32), axis=1, keepdims=True)
            high = delta.astype(BF16).astype(F32)
            rest = delta - high
            dox[head, here, 0:HEAD] = scaled
            dox[head, here, HEAD : 2 * HEAD] = jnp.where(lane == 0, -high, jnp.where(lane == 1, -rest, 0.0)).astype(BF16)
        if hook:
            hook(i)
        return carry

    lax.fori_loop(0, sz.rows // TALL, step, 0, unroll=3)


def weight_grad(layout, m, left_t, right, parts):
    rows, per = layout.flat_rows, BLOCK // HEAD

    def step(i, carry):
        product = mm(left_t[...], right(i)).astype(BF16)
        for k, own in enumerate(layout.pieces):
            for matrix, r, n, f in own:
                if matrix == m:
                    for c in range(per):
                        there = pl.multiple_of(k * rows + f + (i * per + c) * n, 16)
                        parts[pl.ds(there, n), :] = product[r : r + n, c * HEAD : (c + 1) * HEAD]
        return carry

    lax.fori_loop(0, layout.blocks[m] // per, step, 0, unroll=2)


def weight_grad_turned(layout, m, left_t, right, parts):
    rows, unit = layout.flat_rows, layout.unit
    first_k, first = next((k, p) for k, own in enumerate(layout.pieces) for p in own if p[0] == m)
    later = layout.pieces[first_k + 1][-1][2]

    def step(i, carry):
        product = mm(left_t[...], right(i)).astype(BF16).T
        for q in range(BLOCK // unit):
            r = i * BLOCK + q * unit
            head = r < first[2]
            n = jnp.where(head, first[2], later)
            k = jnp.where(head, first_k, first_k + 1 + (r - first[2]) // later)
            base = jnp.where(head, first[3] + r, (r - first[2]) % later)
            for c in range(layout.blocks[m]):
                there = pl.multiple_of(k * rows + base + c * n, 16)
                parts[pl.ds(there, unit), :] = product[q * unit : (q + 1) * unit, c * HEAD : (c + 1) * HEAD]
        return carry

    lax.fori_loop(0, layout.ffn // BLOCK, step, 0, unroll=2)


def attend_backward(sz, base, key_count, query_count, exps, qkv, dox, gqkv, hook=None):
    keep = pl.ds(base, key_count)
    asked = pl.ds(base, query_count)
    scale = 1.0 / math.sqrt(HEAD)
    lane = lax.broadcasted_iota(jnp.int32, (key_count, HEAD), 1)
    ones = jnp.where(lane < 2, 1.0, 0.0).astype(BF16)

    def per_head(head, carry):
        values = jnp.concatenate([qkv[keep, head_at(head, 2 * sz.width)], ones], axis=1)
        keys_t = qkv[keep, head_at(head, sz.width)].T
        gqkv[keep, head_at(head, 2 * sz.width)] = mm(exps[head], dox[head, asked, 0:HEAD]).astype(BF16)
        for j in range(query_count // TALL):
            here = pl.ds(base + j * TALL, TALL)
            columns = pl.ds(j * TALL, TALL)
            grad_probs = mm_t(values, dox[head, here, :])
            grad_scores = (exps[head, :, columns].astype(F32) * grad_probs).astype(BF16)
            exps[head, :, columns] = grad_scores
            gqkv[here, head_at(head)] = (mm(keys_t, grad_scores) * scale).astype(BF16).T
        gqkv[keep, head_at(head, sz.width)] = (mm(exps[head], qkv[asked, head_at(head)]) * scale).astype(BF16)
        if hook:
            hook(head)
        return carry

    lax.fori_loop(0, sz.heads, per_head, 0)


def phase_input(sz, gb_ref, xr, gqkv, w_qkv, gres_low, gin_r, sums, hook=None):
    gain = gb_ref[0:1, :]

    def step(i, carry):
        for j in range(2):
            here = rows_at(2 * i + j)
            grad_act = mm_t(gqkv[here, 0 : 3 * sz.width], w_qkv[...])
            norm, inverse = normed(xr[here, :].astype(F32))
            sums[0] += eight_rows(grad_act * norm)
            sums[1] += eight_rows(grad_act)
            grad = (gres_low[here, :].astype(F32) + norm_back(grad_act, norm, inverse, gain)).astype(BF16)
            cuts = BLOCK // CUT
            gin_r[pl.ds((2 * i + j) * cuts, cuts)] = grad.reshape(cuts, CUT, sz.width)
        if hook:
            hook(i)
        return carry

    lax.fori_loop(0, sz.rows // (2 * BLOCK), step, 0)


def place():
    z, f = lax.axis_index("dp"), lax.axis_index("fsdp")
    core, across, up = f % 2, (f // 2) % 2, f // 4
    return z, f, f + 1 - 2 * core, f + 2 - 4 * across, f + 4 - 8 * up


def shifted_rows(source, off, odd, count, first):
    low = source[pl.ds(off + first, count), :]
    high = source[pl.ds(off + first + 1, count), :]
    lane = lax.broadcasted_iota(jnp.int32, (count, HEAD), 1)
    turned = jnp.where(lane < HEAD // 2, pltpu.roll(low, HEAD // 2, 1), pltpu.roll(high, HEAD // 2, 1))
    return jnp.where(odd, turned, low)


class Link:
    def __init__(self, layout, send_sem, recv_sem):
        self.layout, self.send_sem, self.recv_sem = layout, send_sem, recv_sem
        self.z, self.f, self.mate, self.fx, self.fy = place()
        self.fd = self.fx + self.fy - self.f
        self.ways = [self.f, self.fx, self.fy, self.fd]
        self.k = self.z * PLANE + self.f
        self.sent, self.finished, self.slots = [], 0, 0

    def new_slots(self, count):
        self.slots += count
        return self.slots - count

    def new_send(self, ref, condition=None):
        self.sent.append((ref, condition))
        return len(self.sent) - 1

    def start(self, src, dst, index, slot, target):
        pltpu.make_async_remote_copy(
            src_ref=src, dst_ref=dst, send_sem=self.send_sem.at[index], recv_sem=self.recv_sem.at[slot],
            device_id=target, device_id_type=MESH,
        ).start()

    def copy(self, src, dst, slot, target, like, condition=None):
        index = self.new_send(like, condition)
        self.when(condition, lambda: self.start(src, dst, index, slot, target))

    def wait(self, ref, slot, condition=None):
        self.when(condition, lambda: pltpu.make_async_copy(ref, ref, self.recv_sem.at[slot]).wait())

    @staticmethod
    def when(condition, act):
        if condition is None:
            act()
        else:
            pl.when(condition())(act)

    def finish(self):
        for index in range(self.finished, len(self.sent)):
            ref, condition = self.sent[index]
            self.when(condition, lambda: pltpu.make_async_copy(ref, ref, self.send_sem.at[index]).wait())
        self.finished = len(self.sent)

    def meet(self):
        step = 1 - 2 * ((self.k + 1) % 2)
        edge = jnp.clip(self.k + step, 0, DEVICES - 1)
        has_edge = (self.k > 0) & (self.k < DEVICES - 1)
        barrier = pltpu.get_barrier_semaphore()
        partners = [((self.z + t) % LINE, self.f) for t in (1, 2, 3)]
        partners += [(self.z, self.mate), (self.z, self.fx), (self.z, self.fy)]
        for who in partners:
            pl.semaphore_signal(barrier, inc=1, device_id=who, device_id_type=MESH)

        @pl.when(has_edge)
        def _():
            pl.semaphore_signal(barrier, inc=1, device_id=(edge // PLANE, edge % PLANE), device_id_type=MESH)

        pl.semaphore_wait(barrier, len(partners) + has_edge.astype(jnp.int32))

    def tell(self, sem):
        for who in (self.mate, self.fx, self.fy):
            pl.semaphore_signal(sem, inc=1, device_id=(self.z, who), device_id_type=MESH)

        @pl.when(self.z % 2 == 0)
        def _():
            sender = jnp.where(self.z == 0, 2, 3)
            pl.semaphore_signal(sem, inc=1, device_id=(sender, self.f), device_id_type=MESH)

        @pl.when(self.z == 2)
        def _():
            pl.semaphore_signal(sem, inc=1, device_id=(1, self.f), device_id_type=MESH)

    def told(self, sem):
        pl.semaphore_wait(sem, 3 + (self.z > 0).astype(jnp.int32))


class Gather:
    def __init__(self, link, mats, gains, gain_send, gain_recv):
        self.link, self.layout, self.mats, self.gains = link, link.layout, mats, gains
        self.gain_send, self.gain_recv, self.gain_sent = gain_send, gain_recv, []
        self.first = link.new_slots(5 * PIECES)
        self.later = {s: link.new_slots(9) for s in range(1, LINE)}

    def is_first(self, way, condition):
        first = self.link.ways[way] == 0
        return first if condition is None else first & condition()

    def send_gains(self, way, target, condition=None):
        index = len(self.gain_sent)
        self.gain_sent.append((way, condition))

        @pl.when(self.is_first(way, condition))
        def _():
            pltpu.make_async_remote_copy(
                src_ref=self.gains, dst_ref=self.gains, send_sem=self.gain_send.at[index], recv_sem=self.gain_recv,
                device_id=target, device_id_type=MESH,
            ).start()

    def wait_gains(self, way, condition=None):
        pl.when(self.is_first(way, condition))(lambda: pltpu.make_async_copy(self.gains, self.gains, self.gain_recv).wait())

    def piece(self, f, p):
        n = self.layout.pieces[0][0][2] // PIECES
        return self.mats[0].at[pl.ds(pl.multiple_of(f * (n * PIECES) + p * n, 8), n), :]

    def send_piece(self, of, p, way, target, condition=None):
        ref = self.piece(self.link.ways[of], p)
        self.link.copy(ref, ref, self.first + way * PIECES + p, target, self.piece(0, 0), condition)
        if p == 0:
            self.send_gains(of, target, condition)

    def wait_piece(self, of, p, way, condition=None):
        self.link.wait(self.piece(0, 0), self.first + way * PIECES + p, condition)
        if p == 0:
            self.wait_gains(of, condition)

    def along(self, p):
        link = self.link
        self.wait_piece(0, p, 0, lambda: link.z > 0)
        self.send_piece(0, p, 0, (jnp.minimum(link.z + 1, LINE - 1), link.f), lambda: link.z < LINE - 1)
        self.send_piece(0, p, 1, (link.z, link.fx))
        self.send_piece(0, p, 2, (link.z, link.fy))

    def across(self, p):
        link = self.link
        self.wait_piece(1, p, 1)
        if p < PIECES // 2:
            self.send_piece(1, p, 3, (link.z, link.fy))
        self.wait_piece(2, p, 2)
        if p >= PIECES // 2:
            self.send_piece(2, p, 3, (link.z, link.fx))

    def whole(self, f):
        n = self.layout.pieces[0][0][2]
        return self.mats[0].at[pl.ds(pl.multiple_of(f * n, 16), n), :]

    def first_to_mate(self, way):
        link = self.link
        if way == 3:
            for p in range(PIECES):
                self.wait_piece(3, p, 3)
        ref = self.whole(link.ways[way])
        link.copy(ref, ref, self.first + 4 * PIECES + way, (link.z, link.mate), self.whole(0))
        self.send_gains(way, (link.z, link.mate))

    def first_from_mate(self):
        for way in range(4):
            self.link.wait(self.whole(0), self.first + 4 * PIECES + way)
        pl.when(self.link.f % 2 == 1)(lambda: pltpu.make_async_copy(self.gains, self.gains, self.gain_recv).wait())

    def some(self, s, f, half):
        rows = self.layout.flat_rows // self.layout.blocks[0]
        return self.mats[0].at[pl.ds(0, rows if half is None else rows // 2), :]

    def send_part(self, s, f, slot, target, half=None, condition=None):
        link = self.link
        index = link.new_send(self.some(s, f, half), condition)

        def go(pieces):
            for m, r, n, _ in pieces if half is None else self.layout.halves(pieces)[half]:
                ref = self.mats[m].at[pl.ds(r, n), :]
                link.start(ref, ref, index, self.slot_of(s, slot), target)

        link.when(condition, lambda: self.layout.each_kind(s * PLANE + f, go))

    def slot_of(self, s, slot):
        return self.later[1] + (s - 1) * 9 + slot

    def wait_part(self, s, slot, half=None, condition=None):
        self.link.wait(self.some(s, 0, half), self.slot_of(s, slot), condition)

    def over_links(self, s, condition=None):
        link = self.link
        self.send_part(s, link.f, 1, (link.z, link.fx), None, condition)
        self.send_part(s, link.f, 2, (link.z, link.fy), None, condition)
        self.send_part(s, link.f, 5, (link.z, link.mate), None, condition)

    def start_later(self):
        link = self.link
        self.over_links(link.z, lambda: link.z > 0)
        for t in (1, 2, 3):
            target = jnp.maximum(link.z - t, 0)
            self.send_part(link.z, link.f, 0, (target, link.f), None, lambda t=t: link.z >= jnp.maximum(t, 1))

    def start_upward(self):
        link = self.link
        for t in (1, 2):
            target = jnp.minimum(link.z + t, LINE - 1)
            self.send_part(link.z, link.f, 0, (target, link.f), None, lambda t=t: (link.z > 0) & (link.z + t < LINE))

    def line(self, s):

        def elsewhere():
            return self.link.z != s

        self.wait_part(s, 0, None, elsewhere)
        self.over_links(s, elsewhere)

    def corner(self, s):
        link = self.link
        self.wait_part(s, 1)
        self.send_part(s, link.fx, 3, (link.z, link.fy), 0)
        self.send_part(s, link.fx, 6, (link.z, link.mate))
        self.wait_part(s, 2)
        self.send_part(s, link.fy, 4, (link.z, link.fx), 1)
        self.send_part(s, link.fy, 7, (link.z, link.mate))

    def far(self, s):
        link = self.link
        self.wait_part(s, 3, 0)
        self.wait_part(s, 4, 1)
        self.send_part(s, link.fd, 8, (link.z, link.mate))

    def mates(self, s):
        for slot in (5, 6, 7, 8):
            self.wait_part(s, slot)

    def finish(self):
        for index, (way, condition) in enumerate(self.gain_sent):
            pl.when(self.is_first(way, condition))(lambda: pltpu.make_async_copy(self.gains, self.gains, self.gain_send.at[index]).wait())


class Scatter:
    def __init__(self, link, parts, room, line_in, chain_in, small, small_in):
        self.link, self.layout, self.parts, self.room, self.line_in = link, link.layout, parts, room, line_in
        self.chain_in, self.small, self.small_in = chain_in, small, small_in
        self.flip = link.mate - link.f
        self.slot = {s: link.new_slots(8) for s in range(LINE)}
        self.line_slot, self.tail_slot, self.small_slot = link.new_slots(LINE), link.new_slots(6 * PIECES), link.new_slots(3 + LINE)
        self.piece_rows = self.layout.flat_rows // PIECES

    def part(self, s, f):
        rows = self.layout.flat_rows
        return self.parts.at[pl.ds(pl.multiple_of((s * PLANE + f) * rows, rows), rows), :]

    def like(self, size=None):
        return self.parts.at[pl.ds(0, self.layout.flat_rows if size is None else size), :]

    def buffer(self, s, index, lo=0, size=None):
        rows = self.layout.flat_rows
        ref, base = self.room(s)
        return ref.at[pl.ds(base + index * rows + lo, rows if size is None else size), :]

    def line_buffer(self, z, lo=0, size=None):
        rows = self.layout.flat_rows
        ref, base = self.line_in
        return ref.at[pl.ds(pl.multiple_of(base + z * rows + lo, 16), rows if size is None else size), :]

    def chain_buffer(self, index):
        ref, base = self.chain_in
        rows = self.layout.flat_rows
        return ref.at[pl.ds(base + index * rows, rows), :]

    def share(self, s):
        link = self.link
        for way in (3, 2, 1, 0):
            link.copy(self.part(s, link.ways[way] + self.flip), self.buffer(s, way), self.slot[s] + way, (link.z, link.mate), self.like())

    def add(self, into, terms):
        step = 96

        def body(i, carry):
            here = pl.ds(pl.multiple_of(i * step, step), step)
            total = into[here, :].astype(F32)
            for ref in terms:
                total = total + ref[here, :].astype(F32)
            into[here, :] = total.astype(BF16)
            return carry

        lax.fori_loop(0, into.shape[0] // step, body, 0, unroll=2)

    def mated(self, s, way):
        self.link.wait(self.buffer(s, way), self.slot[s] + way)

    def corner(self, s):
        link, half = self.link, self.layout.flat_rows // 2
        self.mated(s, 3)
        own = self.part(s, link.fd)
        for cut, target in ((0, link.fx), (1, link.fy)):
            some = own.at[pl.ds(cut * half, half), :]
            self.add(some, [self.buffer(s, 3, cut * half, half)])
            link.copy(some, self.buffer(s, 4, cut * half, half), self.slot[s] + 4 + cut, (link.z, target), self.like(half))

    def side(self, s):
        link, half = self.link, self.layout.flat_rows // 2
        for way, cut, f, target in ((2, 0, link.fy, link.fy), (1, 1, link.fx, link.fx)):
            self.mated(s, way)
            own = self.part(s, f)
            for now in (1 - cut, cut):
                some = own.at[pl.ds(now * half, half), :]
                terms = [self.buffer(s, way, now * half, half)]
                if now == cut:
                    corner = self.buffer(s, 4, cut * half, half)
                    link.wait(corner, self.slot[s] + 4 + cut)
                    terms.append(corner)
                self.add(some, terms)
            link.copy(own, self.buffer(s, 4 + way), self.slot[s] + 5 + way, (link.z, target), self.like())

    def sided(self, s):
        link = self.link
        self.mated(s, 0)
        for way in (1, 2):
            link.wait(self.buffer(s, 4 + way), self.slot[s] + 5 + way)

    def line(self, s):
        link = self.link
        self.sided(s)
        own = self.part(s, link.f)

        @pl.when(link.z != s)
        def _():
            self.add(own, [self.buffer(s, 0), self.buffer(s, 5), self.buffer(s, 6)])

        link.copy(own, self.line_buffer(link.z), self.line_slot + link.z, (s, link.f), self.like(), lambda: link.z != s)

    def piece_of(self, ref, p):
        return ref.at[pl.ds(p * self.piece_rows, self.piece_rows), :]

    def pass_on(self, own, way, p, into, target, condition=None):
        like, slot = self.like(self.piece_rows), self.tail_slot + way * PIECES + p
        self.link.copy(self.piece_of(own, p), self.piece_of(into, p), slot, target, like, condition)

    def passed(self, way, p):
        self.link.wait(self.like(self.piece_rows), self.tail_slot + way * PIECES + p)

    def add_piece(self, own, p, others):
        self.add(self.piece_of(own, p), [self.piece_of(ref, p) for ref in others])

    def tail_corner(self):
        link, half = self.link, PIECES // 2
        self.mated(0, 3)
        own = self.part(0, link.fd)
        for p in range(PIECES):
            self.add_piece(own, p, [self.buffer(0, 3)])
            self.pass_on(own, 0, p, self.buffer(0, 4), (link.z, link.fx if p < half else link.fy))
        for way, pieces, f in ((2, range(half, PIECES), link.fy), (1, range(half), link.fx)):
            self.mated(0, way)
            own = self.part(0, f)
            for p in pieces:
                self.add_piece(own, p, [self.buffer(0, way)])
                self.pass_on(own, way, p, self.buffer(0, 4 + way), (link.z, f))

    def tail_side(self):
        link, half = self.link, PIECES // 2
        for j in range(half):
            for way, p, f in ((2, j, link.fy), (1, half + j, link.fx)):
                own = self.part(0, f)
                self.passed(0, p)
                self.add_piece(own, p, [self.buffer(0, way), self.buffer(0, 4)])
                self.pass_on(own, way, p, self.buffer(0, 4 + way), (link.z, f))

    def tail_sum(self, p, others=()):
        self.passed(1, p)
        self.passed(2, p)
        own = self.part(0, self.link.f)
        self.add_piece(own, p, [self.buffer(0, 0), self.buffer(0, 5), self.buffer(0, 6), *others])


    ORDER = tuple(p for j in range(PIECES // 2) for p in (j, j + PIECES // 2))

    def leaf(self):
        link = self.link
        self.mated(0, 0)
        for p in self.ORDER:
            pl.when(link.z % 2 == 1)(lambda: self.tail_sum(p))
            own, target = self.part(0, link.f), (2, link.f)
            self.pass_on(own, 3, p, self.chain_buffer(0), target, lambda: link.z == 1)
            self.pass_on(own, 4, p, self.chain_buffer(1), target, lambda: link.z == 3)

    def middle(self):
        link = self.link
        for p in self.ORDER:

            @pl.when(link.z == 2)
            def _():
                self.passed(3, p)
                self.passed(4, p)
                self.tail_sum(p, (self.chain_buffer(0), self.chain_buffer(1)))

            self.pass_on(self.part(0, link.f), 5, p, self.chain_buffer(0), (0, link.f), lambda: link.z == 2)

    def total(self, out):
        link, rows, step = self.link, self.layout.flat_rows, 96

        def sum_of(refs):
            def body(i, carry):
                here = pl.ds(pl.multiple_of(i * step, step), step)
                total = refs[0][here, :].astype(F32)
                for ref in refs[1:]:
                    total = total + ref[here, :].astype(F32)
                out[here, :] = total
                return carry

            lax.fori_loop(0, rows // step, body, 0, unroll=2)

        for s in range(LINE):
            refs = [self.part(s, link.f), self.buffer(s, 0), self.buffer(s, 5), self.buffer(s, 6)]
            if s == 0:
                refs.append(self.chain_buffer(0))
            else:
                refs += [self.line_buffer(z) for z in range(LINE) if z != s]

            @pl.when(link.z == s)
            def _():
                for z in range(LINE):
                    if s and z != s:
                        link.wait(self.line_buffer(z), self.line_slot + z)
                if s == 0:
                    for p in self.ORDER:
                        for way in (1, 2, 5):
                            self.passed(way, p)
                sum_of(refs)

    def small_send(self, stage):
        link = self.link
        if stage < 3:
            target = (link.z, (link.mate, link.fx, link.fy)[stage])
            link.copy(self.small.at[stage], self.small_in.at[stage], self.small_slot + stage, target, self.small.at[0])
        else:
            for t in (1, 2, 3):
                target = ((link.z + t) % LINE, link.f)
                link.copy(self.small.at[3], self.small_in.at[3 + link.z], self.small_slot + 3 + link.z, target, self.small.at[0])

    def small_add(self, stage):
        link = self.link
        if stage < 3:
            link.wait(self.small_in.at[stage], self.small_slot + stage)
            self.small[stage + 1] = self.small[stage] + self.small_in[stage]
        else:
            for t in (1, 2, 3):
                z = (link.z + t) % LINE
                link.wait(self.small_in.at[3 + z], self.small_slot + 3 + z)
            self.small_in[pl.ds(3 + link.z, 1)] = self.small[pl.ds(3, 1)]
            self.small[4] = (self.small_in[3] + self.small_in[4]) + (self.small_in[5] + self.small_in[6])


def edge_copy(layout, k, shard, edge, edge_sems):
    before = jnp.maximum(k - 1, 0)
    return pltpu.make_async_remote_copy(
        src_ref=shard.at[pl.ds(0, HALO), :], dst_ref=edge, send_sem=edge_sems.at[0], recv_sem=edge_sems.at[1],
        device_id=(before // PLANE, before % PLANE), device_id_type=MESH,
    )


def own_part(layout, k, chunk, edge, flat, mats, send):
    rows, half = layout.flat_rows, HEAD // 2
    pl.when(k < DEVICES - 1)(lambda: send.wait_recv())
    lane = lax.broadcasted_iota(jnp.int32, (HALO, HEAD), 1)
    row = lax.broadcasted_iota(jnp.int32, (HALO, HEAD), 0)
    turned = pltpu.roll(edge[...], half, 1)
    last = jnp.broadcast_to(chunk[pl.ds(rows, 1), :], (HALO, HEAD))
    down = jnp.where(row == 0, last, pltpu.roll(turned, 1, 0))
    chunk[pl.ds(rows, HALO), :] = jnp.where(lane < half, down, turned)
    off, odd = (DEVICES - k) // 2, (DEVICES - k) % 2 == 1
    step = 96
    for i in range(0, rows, step):
        flat[pl.ds(i, step), :] = shifted_rows(chunk, off, odd, step, i)

    def put(pieces):
        for m, r, n, f in pieces:
            blocks = layout.blocks[m]
            for c in range(blocks):
                mats[m][pl.ds(r, n), c * HEAD : (c + 1) * HEAD] = flat[pl.ds(f + c, n, stride=blocks), :].astype(BF16)

    layout.each_kind(k, put)
    pl.when(k > 0)(lambda: send.wait_send())


def own_rows(layout, k, total, small, flat, edge, edge_sems):
    rows, out = layout.flat_rows, total

    def put(pieces):
        for m, _, n, f in pieces:
            blocks = layout.blocks[m]
            for c in range(blocks):
                flat[pl.ds(HALO + f + c, n, stride=blocks), :] = total[pl.ds(f + c * n, n), :]

    layout.each_kind(k, put)
    after = jnp.minimum(k + 1, DEVICES - 1)
    send = pltpu.make_async_remote_copy(
        src_ref=flat.at[pl.ds(rows, HALO), :], dst_ref=edge, send_sem=edge_sems.at[0], recv_sem=edge_sems.at[1],
        device_id=(after // PLANE, after % PLANE), device_id_type=MESH,
    )
    pl.when(k < DEVICES - 1)(lambda: send.start())

    @pl.when(k == 0)
    def _():
        across = layout.width // HEAD
        for t in range(4):
            for c in range(across):
                flat[t * across + c : t * across + c + 1, :] = small[t : t + 1, c * HEAD : (c + 1) * HEAD]

    @pl.when(k > 0)
    def _():
        send.wait_recv()
        flat[pl.ds(0, HALO), :] = edge[...]

    step = 8 * 97
    for i in range(0, rows + 8, step):
        out[pl.ds(i, step), :] = shifted_rows(flat, k // 2, k % 2 == 1, step, i)
    pl.when(k < DEVICES - 1)(lambda: send.wait_send())


class Steps:
    heads_hook = down_hook = forward_hook = small_forward_hook = backward_hook = small_backward_hook = input_hook = None

    def nothing(self, *args):
        pass

    enter = first_weights = up_weights = down_weights = pool_free = nothing
    up_done = qkv_done = before_output = between_outputs = close = nothing


def layer_body(sz, layout, steps, len_ref, sup_ref, x_hbm, cot_hbm, out_hbm, gin_hbm, gb_ref, work, io_sem):
    (xr, cr, act2_t, cot_t, qkv, exps_big, exps_small, ctx, ctx_t, hid, pool, gres_low, dox, parts,
     resid, qm, km, inv_ref, sums, w_qkv, w_out, w_up, w_down, x_cuts, c_cuts) = work
    width = sz.width
    load_x = pltpu.make_async_copy(x_hbm, x_cuts, io_sem.at[0])
    load_c = pltpu.make_async_copy(cot_hbm, c_cuts, io_sem.at[1])
    load_x.start()
    load_c.start()
    shift, begins, sups = table_facts(sz, len_ref, sup_ref)

    def masks():
        mask_features(sz, begins, sups, qm, km)
        sums[...] = jnp.zeros_like(sums)

    def set_rows(ref):
        def write(rows, values):
            ref[rows, :] = values

        return write

    def before_weights():
        masks()
        load_x.wait()
        roll_rows(sz, shift, x_cuts, set_rows(xr))

    steps.enter(before_weights)

    def take_cotangent():
        load_c.wait()
        roll_rows(sz, shift, c_cuts, set_rows(cr))
        for i in range(sz.rows // TALL):
            cot_t[:, i * TALL : (i + 1) * TALL] = cr[i * TALL : (i + 1) * TALL, :].T

    steps.first_weights(take_cotangent)
    phase_qkv(sz, gb_ref, xr, x_cuts, w_qkv, qkv)
    attend_forward(sz, 0, sz.big_keys, sz.big, exps_big, qkv, qm, km, ctx, ctx_t, inv_ref, steps.forward_hook)
    attend_forward(sz, sz.big, sz.small, sz.small, exps_small, qkv, qm, km, ctx, ctx_t, inv_ref, steps.small_forward_hook)
    steps.up_weights()
    phase_up(sz, gb_ref, xr, ctx, w_out, w_up, act2_t, hid, pool, resid)
    weight_grad_turned(layout, 3, cot_t, lambda i: hid[:, rows_at(i)], parts)
    steps.down_weights()
    out_r, gin_r, gqkv, act1_t = c_cuts, x_cuts, hid, cot_t
    phase_down(sz, gb_ref, cr, w_up, w_down, hid, pool, resid, out_r, gres_low, sums, steps.down_hook)
    per = BLOCK // HEAD
    weight_grad(
        layout, 2, act2_t,
        lambda i: jnp.concatenate([pool[pool_at(sz, i * per + c, 0, sz.rows), :] for c in range(per)], axis=1), parts,
    )
    steps.pool_free()
    weight_grad(layout, 1, ctx_t, lambda i: gres_low[:, rows_at(i)], parts)
    for i in range(sz.rows // CUT):
        act1_t[:, i * CUT : (i + 1) * CUT] = x_cuts[i].T
    steps.up_done()
    phase_heads(sz, ctx, inv_ref, w_out, gres_low, dox, steps.heads_hook)
    gqkv[sz.big_keys : sz.big, width : 3 * width] = jnp.zeros((sz.big - sz.big_keys, 2 * width), BF16)
    attend_backward(sz, 0, sz.big_keys, sz.big, exps_big, qkv, dox, gqkv, steps.backward_hook)
    attend_backward(sz, sz.big, sz.small, sz.small, exps_small, qkv, dox, gqkv, steps.small_backward_hook)
    weight_grad(layout, 0, act1_t, lambda i: gqkv[:, rows_at(i)], parts)
    steps.qkv_done()
    phase_input(sz, gb_ref, xr, gqkv, w_qkv, gres_low, gin_r, sums, steps.input_hook)
    steps.before_output()
    back = lax.rem(sz.rows - shift, sz.rows)
    roll_rows(sz, back, out_r, set_rows(ctx))
    store_out = pltpu.make_async_copy(ctx, out_hbm, io_sem.at[0])
    store_out.start()
    steps.between_outputs()
    roll_rows(sz, back, gin_r, set_rows(xr))
    store_gin = pltpu.make_async_copy(xr, gin_hbm, io_sem.at[1])
    store_gin.start()
    steps.close()
    store_out.wait()
    store_gin.wait()


def small_terms(sums, out):
    for t in range(4):
        out[t : t + 1, :] = jnp.sum(sums[t], axis=0, keepdims=True)


def work_shapes(sz, layout):
    rows, width, ffn = sz.rows, sz.width, sz.ffn

    def low(*shape):
        return pltpu.VMEM(shape, BF16)

    return [
        low(rows, width), low(rows, width), low(width, rows), low(width, rows), low(rows, 3 * width),
        low(sz.heads, sz.big_keys, sz.big), low(sz.heads, sz.small, sz.small), low(rows, width), low(width, rows),
        low(rows, ffn), low(rows * ffn // HEAD, HEAD), low(rows, width), low(sz.heads, rows, 2 * HEAD),
        low(layout.flat_rows * DEVICES, HEAD), pltpu.VMEM((rows, width), F32), low(rows, HEAD), low(rows, HEAD),
        pltpu.VMEM((sz.heads, 8, rows), F32), pltpu.VMEM((4, 8, width), F32),
        low(width, 3 * width), low(width, width), low(width, ffn), low(ffn, width),
        low(rows // CUT, CUT, width), low(rows // CUT, CUT, width),
    ]


WORK = 25
VMEM_LIMIT = 63 * 2**20 + 3 * 2**18


def plain_kernel(sz, layout, len_ref, sup_ref, x_hbm, cot_hbm, gb_ref, *rest):
    weights, (out_hbm, gin_hbm, parts_hbm, small_ref), rest = rest[:4], rest[4:8], rest[8:]
    work, (load_sem, io_sem) = rest[:WORK], rest[WORK:]
    parts, sums, mats = work[13], work[18], work[19:23]
    steps = Steps()
    loads = [pltpu.make_async_copy(src, dst, load_sem.at[i]) for i, (src, dst) in enumerate(zip(weights, mats))]
    store = pltpu.make_async_copy(parts, parts_hbm, load_sem.at[4])

    def enter(fill):
        for copy in loads:
            copy.start()
        fill()

    def first_weights(fill):
        fill()
        loads[0].wait()

    def up_weights():
        for copy in loads[1:]:
            copy.wait()

    def close():
        small_terms(sums, small_ref)
        store.wait()

    steps.enter, steps.first_weights, steps.up_weights = enter, first_weights, up_weights
    steps.qkv_done, steps.close = store.start, close
    layer_body(sz, layout, steps, len_ref, sup_ref, x_hbm, cot_hbm, out_hbm, gin_hbm, gb_ref, work, io_sem)


def cuts_of(values):
    return values.reshape(values.shape[0] // CUT, CUT, values.shape[1])


def layer(x_in, cotangent, lengths, support, gains, w_qkv, w_out, w_up, w_down):
    rows, width = x_in.shape
    ffn = w_up.shape[1]
    sz, layout = Shapes(rows, width, ffn), Layout(width, ffn)
    anywhere = pl.BlockSpec(memory_space=pl.ANY)
    vmem = pl.BlockSpec(memory_space=pltpu.VMEM)
    smem = pl.BlockSpec(memory_space=pltpu.SMEM)
    return pl.pallas_call(
        functools.partial(plain_kernel, sz, layout),
        out_shape=(
            jax.ShapeDtypeStruct((rows, width), BF16),
            jax.ShapeDtypeStruct((rows, width), BF16),
            jax.ShapeDtypeStruct((layout.flat_rows * DEVICES, HEAD), BF16),
            jax.ShapeDtypeStruct((4, width), F32),
        ),
        in_specs=[smem, smem, anywhere, anywhere, vmem, anywhere, anywhere, anywhere, anywhere],
        out_specs=[anywhere] * 3 + [vmem],
        scratch_shapes=work_shapes(sz, layout) + [pltpu.SemaphoreType.DMA((5,)), pltpu.SemaphoreType.DMA((2,))],
        compiler_params=pltpu.CompilerParams(vmem_limit_bytes=VMEM_LIMIT),
    )(lengths, support, cuts_of(x_in), cuts_of(cotangent), gains, w_qkv, w_out, w_up, w_down)


SENDS = 288
SLOTS = 208
ROOM = 7


HEADS_PLAN = {1: [("corner", 2)], 2: [("corner", 1)]}
BACKWARD_PLAN = {1: [("side", 2)], 2: [("side", 1)]}
SMALL_PLAN = {3: [("line", 2)]}


def planned(scatter, plan):
    return {step: [(getattr(scatter, way), s) for way, s in acts] for step, acts in plan.items()}


def whole_kernel(sz, layout, len_ref, sup_ref, x_hbm, cot_hbm, shard, out_hbm, gin_hbm, own_out, small_out, *rest):
    work, rest = rest[:WORK], rest[WORK:]
    (gb_ref, chunk, flat, edge, gains, extra, small, small_in,
     send_sem, recv_sem, gain_send, gain_recv, edge_sems, out_edge_sems, load_sem, io_sem, ready_sem) = rest
    pool, parts, sums, mats = work[10], work[13], work[18], work[19:23]
    rows = layout.flat_rows
    link = Link(layout, send_sem, recv_sem)
    gather = Gather(link, mats, gains, gain_send, gain_recv)
    scatter = Scatter(
        link, parts, lambda s: (extra, 0) if s == LINE - 1 else (pool, s * ROOM * rows), (extra, ROOM * rows),
        (pool, (LINE - 1) * ROOM * rows), small, small_in,
    )
    steps = Steps()

    def at(index, table):
        for number, acts in table.items():

            @pl.when(index == number)
            def _():
                for act, s in acts:
                    act(s)

    def enter(fill):
        rows_of(shard, chunk)
        link.meet()
        send = edge_copy(layout, link.k, chunk, edge, edge_sems)
        pl.when(link.k > 0)(lambda: send.start())

        @pl.when(link.k == 0)
        def _():
            gains[...] = chunk[pl.ds(0, HALO), :].astype(BF16).astype(F32)

        fill()
        own_part(layout, link.k, chunk, edge, flat, mats, send)
        gather.start_later()

    def first_weights(fill):
        pl.when(link.z >= LINE // 2)(fill)
        for p in range(PIECES):
            gather.along(p)
        gather.first_to_mate(0)
        gather.start_upward()
        for p in range(PIECES):
            gather.across(p)
        gather.first_to_mate(1)
        gather.first_to_mate(2)
        gather.first_to_mate(3)
        for s in range(1, LINE):
            gather.line(s)
        gather.first_from_mate()
        pl.when(link.z < LINE // 2)(fill)
        across = layout.width // HEAD
        for t in range(4):
            for c in range(across):
                gb_ref[t : t + 1, c * HEAD : (c + 1) * HEAD] = gains[pl.ds(t * across + c, 1), :]

    def forward_hook(head):
        at(head, {0: [(gather.corner, 1)], 2: [(gather.corner, 2)], 3: [(gather.far, 1)]})

    def small_forward_hook(head):
        at(head, {0: [(gather.corner, 3)], 2: [(gather.far, 2)]})

    def up_weights():
        gather.mates(1)
        gather.mates(2)

    def down_weights():
        scatter.share(3)
        gather.far(3)
        gather.mates(3)

    def down_hook(i):
        at(i, {0: [(scatter.corner, 3)], 1: [(scatter.side, 3)], 2: [(scatter.line, 3)]})

    def pool_free():
        link.tell(ready_sem)

    def up_done():
        link.told(ready_sem)
        scatter.share(2)
        scatter.share(1)

    def heads_hook(i):
        at(i, planned(scatter, HEADS_PLAN))

    def backward_hook(head):
        at(head, planned(scatter, BACKWARD_PLAN))

    def small_backward_hook(head):
        at(head, planned(scatter, SMALL_PLAN))

    def qkv_done():
        scatter.share(0)
        scatter.line(1)

    def input_hook(i):
        at(i, {0: [(lambda s: scatter.tail_corner(), 0)], 2: [(lambda s: scatter.tail_side(), 0)]})

    def before_output():
        small_terms(sums, small.at[0])
        scatter.small_send(0)
        scatter.leaf()
        scatter.small_add(0)
        scatter.small_send(1)

    def between_outputs():
        scatter.small_add(1)
        scatter.small_send(2)
        scatter.middle()
        scatter.small_add(2)
        scatter.small_send(3)

    def close():
        gather.finish()
        link.finish()
        scatter.total(chunk)
        scatter.small_add(3)
        small_out[...] = small[4, 3:4, :]
        own_rows(layout, link.k, chunk, small.at[4], flat, edge, out_edge_sems)
        store = pltpu.make_async_copy(chunk.at[pl.ds(0, rows + 8), :], own_out, load_sem)
        store.start()
        store.wait()

    steps.enter, steps.first_weights, steps.pool_free = enter, first_weights, pool_free
    steps.forward_hook, steps.small_forward_hook, steps.up_weights = forward_hook, small_forward_hook, up_weights
    steps.down_weights, steps.down_hook, steps.up_done = down_weights, down_hook, up_done
    steps.heads_hook = heads_hook
    steps.backward_hook, steps.small_backward_hook, steps.qkv_done = backward_hook, small_backward_hook, qkv_done
    steps.input_hook, steps.before_output, steps.between_outputs, steps.close = input_hook, before_output, between_outputs, close
    layer_body(sz, layout, steps, len_ref, sup_ref, x_hbm, cot_hbm, out_hbm, gin_hbm, gb_ref, work, io_sem)


def rows_of(values, out):
    size, tile = values.shape[0], 8 * HEAD
    for i in range(size // tile):
        out[i * 8 : (i + 1) * 8, :] = values[pl.ds(i * tile, tile)].reshape(8, HEAD)
    done = size // tile * tile
    while done < size:
        count = min(HEAD, size - done)
        out[done // HEAD : done // HEAD + 1, 0:count] = values[pl.ds(done, count)].reshape(1, count)
        done += count


def whole_layer(layout, x_in, cotangent, lengths, support, master):
    rows, width = x_in.shape
    sz = Shapes(rows, width, layout.ffn)
    anywhere = pl.BlockSpec(memory_space=pl.ANY)
    vmem = pl.BlockSpec(memory_space=pltpu.VMEM)
    smem = pl.BlockSpec(memory_space=pltpu.SMEM)
    dma = pltpu.SemaphoreType.DMA
    part = layout.flat_rows
    return pl.pallas_call(
        functools.partial(whole_kernel, sz, layout),
        out_shape=(
            jax.ShapeDtypeStruct((rows, width), BF16),
            jax.ShapeDtypeStruct((rows, width), BF16),
            jax.ShapeDtypeStruct((part + 8, HEAD), F32),
            jax.ShapeDtypeStruct((1, width), F32),
        ),
        in_specs=[smem, smem, anywhere, anywhere, vmem],
        out_specs=[anywhere] * 3 + [vmem],
        scratch_shapes=work_shapes(sz, layout) + [
            pltpu.VMEM((4, width), F32), pltpu.VMEM((part + 3 * HALO, HEAD), F32), pltpu.VMEM((part + 2 * HALO, HEAD), F32),
            pltpu.VMEM((HALO, HEAD), F32), pltpu.VMEM((HALO, HEAD), F32), pltpu.VMEM(((ROOM + LINE) * part, HEAD), BF16),
            pltpu.VMEM((5, 4, width), F32), pltpu.VMEM((3 + LINE, 4, width), F32),
            dma((SENDS,)), dma((SLOTS,)), dma((64,)), dma, dma((2,)), dma((2,)), dma, dma((2,)),
            pltpu.SemaphoreType.REGULAR,
        ],
        compiler_params=pltpu.CompilerParams(collective_id=0, has_side_effects=True, vmem_limit_bytes=VMEM_LIMIT),
    )(lengths, support, cuts_of(x_in), cuts_of(cotangent), master)


CARRIERS = 4


def hand_over_kernel(count, *refs):
    sources, targets, (held, semaphores) = refs[:count], refs[count : 2 * count], (refs[2 * count : 3 * count], refs[3 * count :])
    pairs = []
    for src, dst, mid in zip(sources, targets, held):
        step = max(src.shape[0] // CARRIERS, 1)
        for i in range(0, src.shape[0], step):
            some, index = pl.ds(i, step), len(pairs)
            pairs.append((
                pltpu.make_async_copy(src.at[some, :], mid.at[some, :], semaphores[0].at[index]),
                pltpu.make_async_copy(mid.at[some, :], dst.at[some, :], semaphores[1].at[index]),
            ))
    for load, _ in pairs:
        load.start()
    for load, store in pairs:
        load.wait()
        store.start()
    for _, store in pairs:
        store.wait()


def hand_over(*arrays):
    anywhere = pl.BlockSpec(memory_space=pl.ANY)
    dma = pltpu.SemaphoreType.DMA((CARRIERS * len(arrays),))
    return pl.pallas_call(
        functools.partial(hand_over_kernel, len(arrays)),
        out_shape=tuple(jax.ShapeDtypeStruct(v.shape, v.dtype) for v in arrays),
        in_specs=[anywhere] * len(arrays),
        out_specs=[anywhere] * len(arrays),
        scratch_shapes=[pltpu.VMEM(v.shape, v.dtype) for v in arrays] + [dma, dma],
    )(*arrays)


def adam(grads, first_moment, second_moment, master, step_count):
    step_float = step_count[0].astype(F32)
    new_first = BETA_ONE * first_moment + (1.0 - BETA_ONE) * grads
    new_second = BETA_TWO * second_moment + (1.0 - BETA_TWO) * grads * grads
    first_hat = new_first / (1.0 - jnp.power(F32(BETA_ONE), step_float))
    second_hat = new_second / (1.0 - jnp.power(F32(BETA_TWO), step_float))
    adam_step = first_hat / (jnp.sqrt(second_hat) + ADAM_EPS) + DECAY_RATE * master
    return new_first, new_second, adam_step


def flat_of_parts(layout, parts):
    by_part, flat = parts.reshape(DEVICES, layout.flat_rows, HEAD), []
    for k, own in enumerate(layout.pieces):
        for m, _, n, f in own:
            blocks = layout.blocks[m]
            piece = by_part[k, f : f + n * blocks].reshape(blocks, n, HEAD)
            flat.append(piece.transpose(1, 0, 2).reshape(-1))
    return jnp.concatenate(flat)


def plain_gather(layout, master):
    width, ffn = layout.width, layout.ffn
    flat = lax.all_gather(master.astype(BF16), ("dp", "fsdp"), axis=0, tiled=True)
    shapes = [(4, width), (width, 3 * width), (width, width), (width, ffn), (ffn, width)]
    arrays, start = [], 0
    for shape in shapes:
        arrays.append(flat[start : start + math.prod(shape)].reshape(shape))
        start += math.prod(shape)
    return (*arrays[1:], arrays[0].astype(F32))


def plain_scatter(layout, parts, small):
    axes = ("dp", "fsdp")
    local = jnp.concatenate([small.reshape(-1), flat_of_parts(layout, parts).astype(F32)])
    return lax.psum_scatter(local, axes, scatter_dimension=0, tiled=True), lax.psum(small[3], axes)


def per_device(sizes, x_in, cotangent, table_lengths, support_counts, master, first_moment, second_moment, step_count):
    width, shard = x_in.shape[1], master.shape[0]
    param_count = shard * sizes[0] * sizes[1]
    ffn = (param_count - 4 * width - 4 * width * width) // (2 * width)
    layout = Layout(width, ffn)
    if layout.fits(param_count, sizes):
        output, grad_input, rows, total = whole_layer(layout, x_in, cotangent, table_lengths, support_counts, master)
        output, grad_input, total = hand_over(output, grad_input, total)
        grads, bias_two_grad = rows.reshape(-1)[:shard], total[0]
    else:
        *weights, gains = plain_gather(layout, master)
        output, grad_input, parts, small = layer(x_in, cotangent, table_lengths, support_counts, gains, *weights)
        grads, bias_two_grad = plain_scatter(layout, parts, small)
    new_first, new_second, adam_step = adam(grads, first_moment, second_moment, master, step_count)
    return output, grad_input, grads, new_first, new_second, adam_step, bias_two_grad


def solution(mesh):
    rows, flat = P(("dp", "fsdp"), None), P(("dp", "fsdp"))
    return jax.shard_map(
        functools.partial(per_device, (mesh.shape["dp"], mesh.shape["fsdp"])),
        mesh=mesh,
        in_specs=(rows, rows, rows, rows, flat, flat, flat, P()),
        out_specs=(rows, rows, flat, flat, flat, flat, P()),
        check_vma=False,
    )
```
